256 devices in a mesh: dom: 64 (over z, x, core), grp: 4 (over y).
Axes of the slice: x: 4, y: 4, z: 8, core: 2. Of those that a mesh axis runs over, the one named last changes fastest.
Arguments:
- features: bfloat16 [131072, 128], P('dom'), may hold values from -6 to 6
- weight_self: bfloat16 [128, 1024], P(None, 'grp'), may hold values from -0.5 to 0.5
- weight_neigh: bfloat16 [128, 1024], P(None, 'grp'), may hold values from -3 to 3
- cotangent: bfloat16 [131072, 1024], P('dom', 'grp'), may hold values from -6 to 6
- inner_rows: int32 [64, 64], P('dom'), may hold values from 0 to 15
- inner_cols: int32 [64, 64], P('dom'), may hold values from 0 to 15
- inner_values: bfloat16 [64, 64, 128, 128], P('dom'), may hold values from 0 to 1, as said below
- send_blocks: int32 [64, 64, 3], P('dom'), may hold values from 0 to 15
- outer_rows: int32 [64, 192], P('dom'), may hold values from 0 to 15
- outer_values: bfloat16 [64, 192, 128, 128], P('dom'), may hold values from 0 to 1, as said below
- live_count: int32 [64, 64], P('dom'), may hold values from 0 to 3
Outputs:
- layer_out: bfloat16 [131072, 1024], P('dom', 'grp')
- feature_grad: float32 [131072, 128], P('dom')
- self_grad: float32 [128, 1024], P(None, 'grp')
- neigh_grad: float32 [128, 1024], P(None, 'grp')
The draws below stay inside these ranges and needn't reach their ends.
Inputs may be any that keep to these rules, and one draw needn't show every extreme that they name: `inner_values`: edge weights are zero or positive; most are zero. `outer_values`: edge weights are zero or positive; most are zero.
All inputs are finite; a program needn't handle non-finite values.
Results may differ from the reference program's by a relative error of at most 0.0055.
Values may be sent and summed in bfloat16 or wider, within the bound.
A program may use at most 128 MiB of HBM per device.

```python
import jax
import jax.numpy as jnp
from jax import lax

F = 128
H = 1024
BLK = 128
NODE_DEV = 2048
NI = 64
SLOTS = 3
LOC_BLK = 16
BSLOTS = 192
NODES = 131072
N_DOM = 64


def sparse_weights(key, shape):
    uniform_a = jax.random.uniform(jax.random.fold_in(key, 11), shape, jnp.float32)
    uniform_b = jax.random.uniform(jax.random.fold_in(key, 12), shape, jnp.float32)
    return jnp.where(uniform_a > 0.97, 0.02 + 0.97 * uniform_b, 0.0)


def draw_inner_values(key, part):
    return sparse_weights(jax.random.fold_in(key, 1), (N_DOM, NI, BLK, BLK)).astype(jnp.bfloat16)


def draw_outer_values(key, part):
    return sparse_weights(jax.random.fold_in(key, 2), (N_DOM, N_DOM * SLOTS, BLK, BLK)).astype(jnp.bfloat16)


def touch_ends(array, key, low, largest):
    longest = array.shape.index(max(array.shape))
    spots = []
    for shift in (0, 1):
        where = [jax.random.randint(jax.random.fold_in(key, axis), (), 0, length) for axis, length in enumerate(array.shape)]
        where[longest] = (where[longest] + shift) % array.shape[longest]
        spots.append(tuple(where))
    return array.at[spots[0]].set(low).at[spots[1]].set(largest)


def block_levels(key, shape, cuts, smallest, largest):
    loudness, own = 1.0, jax.random.fold_in(key, 6)
    for axis_at, parts in cuts:
        heights = jnp.exp(jax.random.uniform(jax.random.fold_in(own, axis_at), (parts,), jnp.float32, smallest / len(cuts), largest / len(cuts)))
        loudness = loudness * jnp.repeat(heights, shape[axis_at] // parts).reshape([-1 if axis == axis_at else 1 for axis in range(len(shape))])
    return loudness


def gaussian(stream_key, extent, width, reach, pieces=(), kind=jnp.bfloat16):
    gain = block_levels(stream_key, extent, pieces, -0.22, 0.18) if pieces else 1.0
    values = jax.random.normal(stream_key, extent, jnp.float32) * width * gain
    return jnp.minimum(jnp.maximum(values, -reach), reach).astype(kind)


def setup_inputs(seed: int = 0) -> dict:
    streams_of = jax.random.split(jax.random.key(seed), 12)
    features = gaussian(streams_of[0], (NODES, F), 1.0, 6.0, ((0, 64),))
    weight_self = gaussian(streams_of[1], (F, H), F ** -0.5, 0.5, ((1, 4),))
    weight_neigh = gaussian(streams_of[2], (F, H), 0.5, 3.0, ((1, 4),))
    cotangent = gaussian(streams_of[3], (NODES, H), 1.0, 6.0, ((0, 64), (1, 4)))
    inner_rows = touch_ends(jax.random.randint(streams_of[4], (N_DOM, NI), 0, LOC_BLK), jax.random.fold_in(streams_of[4], 1), 0, LOC_BLK - 1).astype(jnp.int32)
    inner_cols = touch_ends(jax.random.randint(streams_of[5], (N_DOM, NI), 0, LOC_BLK), jax.random.fold_in(streams_of[5], 1), 0, LOC_BLK - 1).astype(jnp.int32)
    inner_values = draw_inner_values(jax.random.fold_in(streams_of[11], 71), 0)
    send_blocks = touch_ends(jax.random.randint(streams_of[7], (N_DOM, N_DOM, SLOTS), 0, LOC_BLK), jax.random.fold_in(streams_of[7], 1), 0, LOC_BLK - 1).astype(jnp.int32)
    outer_rows = touch_ends(jax.random.randint(streams_of[8], (N_DOM, BSLOTS), 0, LOC_BLK), jax.random.fold_in(streams_of[8], 1), 0, LOC_BLK - 1).astype(jnp.int32)
    outer_values = draw_outer_values(jax.random.fold_in(streams_of[11], 71), 0)
    live_count = touch_ends(jax.random.randint(streams_of[10], (N_DOM, N_DOM), 0, SLOTS + 1), jax.random.fold_in(streams_of[10], 1), 0, SLOTS).astype(jnp.int32)
    return {"features": features, "weight_self": weight_self, "weight_neigh": weight_neigh, "cotangent": cotangent, "inner_rows": inner_rows, "inner_cols": inner_cols, "inner_values": inner_values, "send_blocks": send_blocks, "outer_rows": outer_rows, "outer_values": outer_values, "live_count": live_count}


def reference(features, weight_self, weight_neigh, cotangent, inner_rows, inner_cols, inner_values, send_blocks, outer_rows, outer_values, live_count):
    loc_blocks = NODE_DEV // BLK
    slot_total = N_DOM * SLOTS
    slot_peer = jnp.arange(slot_total, dtype=jnp.int32) // SLOTS
    slot_index = jnp.arange(slot_total, dtype=jnp.int32) % SLOTS
    feat_blocks = features.reshape(N_DOM, loc_blocks, BLK, F)

    def block_sum(values, indices):
        return jax.ops.segment_sum(values, indices, num_segments=loc_blocks)

    def forward_one(device):
        inner_a = inner_values[device].astype(jnp.float32)
        outer_a = outer_values[device].astype(jnp.float32)
        live_mask = (slot_index < live_count[device][slot_peer]).astype(jnp.float32)
        inner_x = feat_blocks[device][inner_cols[device]].astype(jnp.float32)
        outer_x = feat_blocks[slot_peer, send_blocks[slot_peer, device, slot_index]].astype(jnp.float32)
        block_total = block_sum(jnp.einsum('nij,njf->nif', inner_a, inner_x), inner_rows[device])
        block_total = block_total + block_sum(jnp.einsum('nij,njf->nif', outer_a, outer_x) * live_mask[:, None, None], outer_rows[device])
        degree = 1.0 + block_sum(jnp.sum(inner_a, axis=-1), inner_rows[device])
        degree = degree + block_sum(jnp.sum(outer_a, axis=-1) * live_mask[:, None], outer_rows[device])
        aggregate = ((feat_blocks[device].astype(jnp.float32) + block_total) / degree[..., None]).astype(jnp.bfloat16)
        return aggregate, degree

    aggregate, degree = lax.map(forward_one, jnp.arange(N_DOM, dtype=jnp.int32))
    rows_x = features.reshape(N_DOM, NODE_DEV, F)
    rows_a = aggregate.reshape(N_DOM, NODE_DEV, F)
    rows_g = cotangent.reshape(N_DOM, NODE_DEV, H)

    def project(carried, batch_items):
        feature_rows, agg_rows, cot_rows = batch_items
        preact = jnp.dot(feature_rows, weight_self, preferred_element_type=jnp.float32) + jnp.dot(agg_rows, weight_neigh, preferred_element_type=jnp.float32)
        layer_out = jax.nn.silu(preact).astype(jnp.bfloat16)
        sigmoid_v = jax.nn.sigmoid(preact)
        grad_pre = (cot_rows.astype(jnp.float32) * sigmoid_v * (1.0 + preact * (1.0 - sigmoid_v))).astype(jnp.bfloat16)
        grad_self = carried[0] + jnp.dot(feature_rows.T, grad_pre, preferred_element_type=jnp.float32)
        grad_neigh = carried[1] + jnp.dot(agg_rows.T, grad_pre, preferred_element_type=jnp.float32)
        self_back = jnp.dot(grad_pre, weight_self.T, preferred_element_type=jnp.float32)
        neigh_back = jnp.dot(grad_pre, weight_neigh.T, preferred_element_type=jnp.float32)
        return (grad_self, grad_neigh), (layer_out, self_back, neigh_back)

    zero_grad = jnp.zeros((F, H), jnp.float32)
    (grad_self, grad_neigh), (layer_out, self_back, neigh_back) = lax.scan(project, (zero_grad, zero_grad), (rows_x, rows_a, rows_g))
    scaled = (neigh_back.reshape(N_DOM, loc_blocks, BLK, F) / degree[..., None]).astype(jnp.bfloat16)

    def backward_one(accumulated, device):
        inner_a = inner_values[device].astype(jnp.float32)
        outer_a = outer_values[device].astype(jnp.float32)
        live_mask = (slot_index < live_count[device][slot_peer]).astype(jnp.float32)
        inner_s = scaled[device][inner_rows[device]].astype(jnp.float32)
        accumulated = accumulated.at[device, inner_cols[device]].add(jnp.einsum('nij,nif->njf', inner_a, inner_s))
        outer_s = scaled[device][outer_rows[device]].astype(jnp.float32)
        outer_terms = jnp.einsum('nij,nif->njf', outer_a, outer_s) * live_mask[:, None, None]
        accumulated = accumulated.at[slot_peer, send_blocks[slot_peer, device, slot_index]].add(outer_terms)
        return accumulated, None

    accumulated, _ = lax.scan(backward_one, jnp.zeros((N_DOM, loc_blocks, BLK, F), jnp.float32), jnp.arange(N_DOM, dtype=jnp.int32))
    feature_grad = (self_back.reshape(N_DOM, loc_blocks, BLK, F) + scaled.astype(jnp.float32) + accumulated).reshape(NODES, F)
    return layer_out.reshape(NODES, H), feature_grad, grad_self, grad_neigh
```

```python
import functools

import jax
import jax.numpy as jnp
from jax import lax
from jax.experimental import pallas as pl
from jax.experimental.pallas import tpu as pltpu
from jax.sharding import PartitionSpec as P

MESH = pl.DeviceIdType.MESH
ANY = pl.BlockSpec(memory_space=pl.ANY)
VM = pl.BlockSpec(memory_space=pltpu.VMEM)
SM = pl.BlockSpec(memory_space=pltpu.SMEM)
F32 = jnp.float32
BF16 = jnp.bfloat16
TRANS_A = (((0,), (0,)), ((), ()))
TRANS_B = (((1,), (1,)), ((), ()))


def x_extent(parts):
    return 4 if parts == 64 else 1


def plane_peer(i, q, g, x):
    z = q // (2 * x)
    return (((i // x) * 2 + (z + g // 2) % 2) * x + i % x) * 2 + (q + g) % 2


def plane_slot(q, x):
    return (q // (4 * x)) * x + (q // 2) % x


def enter(peers, count):
    barrier = pltpu.get_barrier_semaphore()
    for peer in peers:
        peer(barrier)
    pl.semaphore_wait(barrier, count)


def signal_plane(q, g, x, n_src):
    slot = plane_slot(q, x)

    def go(barrier):
        @pl.when(g != 0)
        def _():
            pl.semaphore_signal(barrier, inc=1, device_id=(plane_peer(slot, q, g, x), g), device_id_type=MESH)

        @pl.loop(1, n_src)
        def _(i):
            peer = plane_peer((slot + i) % n_src, q, g, x)
            pl.semaphore_signal(barrier, inc=1, device_id=(peer, g), device_id_type=MESH)

    return go


def signal_group(q, g, n_grp):
    def go(barrier):
        for r in range(1, n_grp):
            pl.semaphore_signal(barrier, inc=1, device_id=(q, (g + r) % n_grp), device_id_type=MESH)

    return go


def forward_exchange(x, n_src, n_grp, idx, feat, cot, w_self, w_neigh, inc, cot_all, w_all, stage, send, recv, cot_s, cot_r, w_s, w_r, loc):
    q, g = lax.axis_index("dom"), lax.axis_index("grp")
    slots = stage.shape[1]
    quarter = cot_all.shape[1]
    fw = w_self.shape[0]
    slot = plane_slot(q, x)
    barrier = pltpu.get_barrier_semaphore()
    signal_plane(q, g, x, n_src)(barrier)
    signal_group(q, g, n_grp)(barrier)
    own = [
        pltpu.make_async_copy(cot.at[pl.ds(g * quarter, quarter)], cot_all.at[g], loc.at[0]),
        pltpu.make_async_copy(w_self, w_all.at[g, pl.ds(0, fw)], loc.at[1]),
        pltpu.make_async_copy(w_neigh, w_all.at[g, pl.ds(fw, fw)], loc.at[2]),
    ]
    for c in own:
        c.start()

    def fill(d):
        peer = plane_peer(d, q, g, x)
        for s in range(slots):
            stage[d, s] = feat[idx[peer, s]]
        return peer

    def remote(d, peer):
        return pltpu.make_async_remote_copy(
            src_ref=stage.at[d], dst_ref=inc.at[slot], send_sem=send.at[d], recv_sem=recv.at[slot],
            device_id=(peer, g), device_id_type=MESH)

    home = fill(slot)

    @pl.when(g == 0)
    def _():
        pl.semaphore_wait(barrier, n_src - 1 + n_grp - 1)

    @pl.when(g != 0)
    def _():
        pl.semaphore_wait(barrier, n_src + n_grp - 1)

    far = []
    for r in range(1, n_grp):
        y = (g + r) % n_grp
        to = dict(device_id=(q, y), device_id_type=MESH)
        far.append(pltpu.make_async_remote_copy(
            src_ref=cot.at[pl.ds(y * quarter, quarter)], dst_ref=cot_all.at[g],
            send_sem=cot_s.at[r - 1], recv_sem=cot_r.at[r - 1], **to))
        far.append(pltpu.make_async_remote_copy(
            src_ref=w_self, dst_ref=w_all.at[g, pl.ds(0, fw)],
            send_sem=w_s.at[r - 1, 0], recv_sem=w_r.at[r - 1, 0], **to))
        far.append(pltpu.make_async_remote_copy(
            src_ref=w_neigh, dst_ref=w_all.at[g, pl.ds(fw, fw)],
            send_sem=w_s.at[r - 1, 1], recv_sem=w_r.at[r - 1, 1], **to))

    @pl.when(g == 0)
    def _():
        pltpu.make_async_copy(stage.at[slot], inc.at[slot], recv.at[slot]).start()

    @pl.when(g != 0)
    def _():
        remote(slot, home).start()

    @pl.loop(1, n_src)
    def _(i):
        d = (slot + i) % n_src
        remote(d, fill(d)).start()

    for c in far:
        c.start()
    for c in own:
        c.wait()
    for c in far:
        c.wait()

    @pl.when(g != 0)
    def _():
        remote(slot, home).wait_send()

    @pl.loop(1, n_src)
    def _(i):
        d = (slot + i) % n_src
        remote(d, plane_peer(d, q, g, x)).wait_send()

    @pl.loop(0, n_src)
    def _(j):
        pltpu.make_async_copy(stage.at[j], inc.at[j], recv.at[j]).wait()


def aggregate_kernel(x, n_src, n_grp, in_rows, in_cols, out_rows, live, feat, inc, inner, outer, part, deg, acc, deg_acc, a_in, a_out, x_in, sem_in, sem_out, sem_x):
    q, g = lax.axis_index("dom"), lax.axis_index("grp")
    slots = inc.shape[1]
    n_in = inner.shape[0] // n_grp
    load_in = pltpu.make_async_copy(inner.at[pl.ds(g * n_in, n_in)], a_in, sem_in)
    load_in.start()
    load_x = pltpu.make_async_copy(inc, x_in, sem_x)
    load_x.start()

    def load(i):
        peer = plane_peer(i, q, g, x)
        return pltpu.make_async_copy(outer.at[pl.ds(peer * slots, slots)], a_out.at[i], sem_out)

    @pl.loop(0, n_src)
    def _(i):
        load(i).start()

    acc[...] = jnp.zeros_like(acc)
    deg_acc[...] = jnp.zeros_like(deg_acc)
    ones = jnp.ones((8, acc.shape[1]), BF16)

    def add(row, a, b):
        acc[row] += jnp.dot(a, b, preferred_element_type=F32)
        deg_acc[row] += lax.dot_general(ones, a, TRANS_B, preferred_element_type=F32)

    load_in.wait()

    @pl.loop(0, n_in)
    def _(n):
        add(in_rows[g * n_in + n], a_in[n], feat[in_cols[g * n_in + n]])

    load_x.wait()
    pltpu.make_async_copy(a_out, a_out, sem_out).wait()

    @pl.loop(0, n_src)
    def _(i):
        peer = plane_peer(i, q, g, x)
        for s in range(slots):
            @pl.when(s < live[peer])
            def _():
                add(out_rows[peer * slots + s], a_out[i, s], x_in[i, s])

    part[...] = acc[...].astype(BF16)
    deg[...] = deg_acc[...]


def dense_kernel(n_grp, part, deg, feat, cot_all, w_all, out_all, scaled, base, wgrad, got, got_d, sent, s1, r1, s2, r2, s3, r3):
    q, g = lax.axis_index("dom"), lax.axis_index("grp")
    n_blk, blk, fw = part.shape
    own_blk = n_blk // n_grp
    rows = own_blk * blk
    mine = pl.ds(g * own_blk, own_blk)
    barrier = pltpu.get_barrier_semaphore()
    signal_group(q, g, n_grp)(barrier)
    pl.semaphore_wait(barrier, n_grp - 1)
    copies, last = [], []
    for r in range(1, n_grp):
        y = (g + r) % n_grp
        to = dict(device_id=(q, y), device_id_type=MESH)
        theirs = pl.ds(y * own_blk, own_blk)
        copies.append(pltpu.make_async_remote_copy(
            src_ref=part.at[theirs], dst_ref=got.at[r - 1], send_sem=s1.at[r - 1], recv_sem=r1.at[r - 1], **to))
        copies.append(pltpu.make_async_remote_copy(
            src_ref=deg.at[theirs], dst_ref=got_d.at[r - 1], send_sem=s2.at[r - 1], recv_sem=r2.at[r - 1], **to))
        last.append(pltpu.make_async_remote_copy(
            src_ref=sent, dst_ref=scaled.at[mine], send_sem=s3.at[r - 1], recv_sem=r3.at[r - 1], **to))
    for c in copies:
        c.start()
    for c in copies:
        c.wait()
    total = part[mine].astype(F32)
    degree = 1.0 + deg[mine]
    for r in range(n_grp - 1):
        total = total + got[r].astype(F32)
        degree = degree + got_d[r]
    own_feat = feat[mine]
    divisor = jnp.stack([jnp.broadcast_to(degree[b, 0:1, :], (blk, blk)).T for b in range(own_blk)])
    agg = ((own_feat.astype(F32) + total) / divisor).astype(BF16)
    both = jnp.concatenate([own_feat.reshape(rows, fw), agg.reshape(rows, fw)], axis=1)
    back = jnp.zeros((rows, 2 * fw), F32)
    for j in range(n_grp):
        pre = jnp.dot(both, w_all[j], preferred_element_type=F32)
        sig = jax.nn.sigmoid(pre)
        out_all[j] = (pre * sig).astype(BF16)
        grad = (cot_all[j].astype(F32) * sig * (1.0 + pre * (1.0 - sig))).astype(BF16)
        wgrad[j] = lax.dot_general(both, grad, TRANS_A, preferred_element_type=F32)
        back = back + lax.dot_general(grad, w_all[j], TRANS_B, preferred_element_type=F32)
    down = (back[:, fw:].reshape(own_blk, blk, fw) / divisor).astype(BF16)
    sent[...] = down
    scaled[mine] = down
    base[...] = back[:, :fw].reshape(own_blk, blk, fw) + down.astype(F32)
    for c in last:
        c.start()
    for c in last:
        c.wait()


def backward_exchange(x, n_src, n_grp, out_rows, live, scaled, outer, out_all, inc, out, a_out, stage, send, recv, o_s, o_r, a_sem, loc):
    q, g = lax.axis_index("dom"), lax.axis_index("grp")
    slots = stage.shape[1]
    quarter = out_all.shape[1]
    slot = plane_slot(q, x)
    barrier = pltpu.get_barrier_semaphore()
    signal_plane(q, g, x, n_src)(barrier)
    signal_group(q, g, n_grp)(barrier)

    def load(d):
        peer = plane_peer(d, q, g, x)
        return pltpu.make_async_copy(outer.at[pl.ds(peer * slots, slots)], a_out.at[d], a_sem.at[d])

    @pl.loop(0, n_src)
    def _(i):
        load((slot + i) % n_src).start()

    own = pltpu.make_async_copy(out_all.at[g], out.at[pl.ds(g * quarter, quarter)], loc)
    own.start()

    def fill(d):
        peer = plane_peer(d, q, g, x)
        load(d).wait()
        for s in range(slots):
            value = lax.dot_general(a_out[d, s], scaled[out_rows[peer * slots + s]], TRANS_A, preferred_element_type=F32)
            stage[d, s] = jnp.where(s < live[peer], value, 0.0).astype(BF16)
        return peer

    def remote(d, peer):
        return pltpu.make_async_remote_copy(
            src_ref=stage.at[d], dst_ref=inc.at[slot], send_sem=send.at[d], recv_sem=recv.at[slot],
            device_id=(peer, g), device_id_type=MESH)

    home = fill(slot)

    @pl.when(g == 0)
    def _():
        pl.semaphore_wait(barrier, n_src - 1 + n_grp - 1)

    @pl.when(g != 0)
    def _():
        pl.semaphore_wait(barrier, n_src + n_grp - 1)

    @pl.when(g == 0)
    def _():
        pltpu.make_async_copy(stage.at[slot], inc.at[slot], recv.at[slot]).start()

    @pl.when(g != 0)
    def _():
        remote(slot, home).start()

    @pl.loop(1, n_src)
    def _(i):
        d = (slot + i) % n_src
        remote(d, fill(d)).start()

    far = []
    for r in range(1, n_grp):
        y = (g + r) % n_grp
        far.append(pltpu.make_async_remote_copy(
            src_ref=out_all.at[y], dst_ref=out.at[pl.ds(g * quarter, quarter)],
            send_sem=o_s.at[r - 1], recv_sem=o_r.at[r - 1], device_id=(q, y), device_id_type=MESH))
    for c in far:
        c.start()
    own.wait()
    for c in far:
        c.wait()

    @pl.when(g != 0)
    def _():
        remote(slot, home).wait_send()

    @pl.loop(1, n_src)
    def _(i):
        d = (slot + i) % n_src
        remote(d, plane_peer(d, q, g, x)).wait_send()

    @pl.loop(0, n_src)
    def _(j):
        pltpu.make_async_copy(stage.at[j], inc.at[j], recv.at[j]).wait()


def pull_kernel(x, n_src, n_grp, in_rows, in_cols, idx, scaled, inc, inner, part, acc, a_in, x_in, sem_in, sem_x):
    q, g = lax.axis_index("dom"), lax.axis_index("grp")
    slots = inc.shape[1]
    n_in = inner.shape[0] // n_grp
    load_in = pltpu.make_async_copy(inner.at[pl.ds(g * n_in, n_in)], a_in, sem_in)
    load_in.start()
    load_x = pltpu.make_async_copy(inc, x_in, sem_x)
    load_x.start()
    acc[...] = jnp.zeros_like(acc)
    load_in.wait()

    @pl.loop(0, n_in)
    def _(n):
        acc[in_cols[g * n_in + n]] += lax.dot_general(
            a_in[n], scaled[in_rows[g * n_in + n]], TRANS_A, preferred_element_type=F32)

    load_x.wait()

    @pl.loop(0, n_src)
    def _(i):
        peer = plane_peer(i, q, g, x)
        for s in range(slots):
            acc[idx[peer, s]] += x_in[i, s].astype(F32)

    part[...] = acc[...].astype(BF16)


def finish_kernel(n_grp, part, base, out, got, whole, s1, r1, s2, r2):
    q, g = lax.axis_index("dom"), lax.axis_index("grp")
    own_blk = base.shape[0]
    mine = pl.ds(g * own_blk, own_blk)
    barrier = pltpu.get_barrier_semaphore()
    signal_group(q, g, n_grp)(barrier)
    pl.semaphore_wait(barrier, n_grp - 1)
    first, last = [], []
    for r in range(1, n_grp):
        y = (g + r) % n_grp
        to = dict(device_id=(q, y), device_id_type=MESH)
        first.append(pltpu.make_async_remote_copy(
            src_ref=part.at[pl.ds(y * own_blk, own_blk)], dst_ref=got.at[r - 1],
            send_sem=s1.at[r - 1], recv_sem=r1.at[r - 1], **to))
        last.append(pltpu.make_async_remote_copy(
            src_ref=whole.at[mine], dst_ref=whole.at[mine], send_sem=s2.at[r - 1], recv_sem=r2.at[r - 1], **to))
    for c in first:
        c.start()
    for c in first:
        c.wait()
    total = base[...] + part[mine].astype(F32)
    for r in range(n_grp - 1):
        total = total + got[r].astype(F32)
    whole[mine] = total.astype(BF16)
    for c in last:
        c.start()
    for c in last:
        c.wait()
    out[...] = whole[...].astype(F32)


def params(collective=None, vmem=48):
    if collective is None:
        return pltpu.CompilerParams(vmem_limit_bytes=vmem << 20)
    return pltpu.CompilerParams(vmem_limit_bytes=vmem << 20, collective_id=collective, has_side_effects=True)


def shards(features, w_self, w_neigh, cotangent, inner_rows, inner_cols, inner_values, send_blocks, outer_rows, outer_values, live_count):
    blk = inner_values.shape[-1]
    nodes, fw = features.shape
    n_blk = nodes // blk
    parts, n_grp = lax.axis_size("dom"), lax.axis_size("grp")
    x = x_extent(parts)
    n_src = parts // n_grp
    slots = send_blocks.shape[-1]
    hid = w_self.shape[1]
    own_blk = n_blk // n_grp
    rows = own_blk * blk
    n_in = inner_values.shape[1] // n_grp
    inner, outer = inner_values[0], outer_values[0]
    rows_in, cols_in, rows_out, live, idx = inner_rows[0], inner_cols[0], outer_rows[0], live_count[0], send_blocks[0]
    feat = features.reshape(n_blk, blk, fw)
    dma, sds = pltpu.SemaphoreType.DMA, jax.ShapeDtypeStruct
    block = (n_src, slots, blk, fw)

    inc, cot_all, w_all = pl.pallas_call(
        functools.partial(forward_exchange, x, n_src, n_grp),
        out_shape=(sds(block, BF16), sds((n_grp, rows, hid), BF16), sds((n_grp, 2 * fw, hid), BF16)),
        in_specs=[SM, VM, ANY, ANY, ANY],
        out_specs=(ANY, ANY, ANY),
        scratch_shapes=[pltpu.VMEM(block, BF16), dma((n_src,)), dma((n_src,)), dma((n_grp - 1,)), dma((n_grp - 1,)),
                        dma((n_grp - 1, 2)), dma((n_grp - 1, 2)), dma((3,))],
        compiler_params=params(0), name="forward_exchange",
    )(idx, feat, cotangent, w_self, w_neigh)

    part, deg = pl.pallas_call(
        functools.partial(aggregate_kernel, x, n_src, n_grp),
        out_shape=(sds((n_blk, blk, fw), BF16), sds((n_blk, 8, blk), F32)),
        in_specs=[SM, SM, SM, SM, VM, ANY, ANY, ANY],
        out_specs=(VM, VM),
        scratch_shapes=[pltpu.VMEM((n_blk, blk, fw), F32), pltpu.VMEM((n_blk, 8, blk), F32),
                        pltpu.VMEM((n_in, blk, blk), BF16), pltpu.VMEM((n_src, slots, blk, blk), BF16),
                        pltpu.VMEM(block, BF16), dma, dma, dma],
        compiler_params=params(), name="aggregate",
    )(rows_in, cols_in, rows_out, live, feat, inc, inner, outer)

    y_sems = [dma((n_grp - 1,))] * 6
    out_all, scaled, base, wgrad = pl.pallas_call(
        functools.partial(dense_kernel, n_grp),
        out_shape=(sds((n_grp, rows, hid), BF16), sds((n_blk, blk, fw), BF16), sds((own_blk, blk, fw), F32), sds((n_grp, 2 * fw, hid), F32)),
        in_specs=[VM] * 5,
        out_specs=(VM,) * 4,
        scratch_shapes=[pltpu.VMEM((n_grp - 1, own_blk, blk, fw), BF16), pltpu.VMEM((n_grp - 1, own_blk, 8, blk), F32),
                        pltpu.VMEM((own_blk, blk, fw), BF16)] + y_sems,
        compiler_params=params(1), name="dense",
    )(part, deg, feat, cot_all, w_all)

    grads = lax.psum(lax.psum_scatter(wgrad, "grp", scatter_dimension=0, tiled=False), "dom")

    inc_back, layer_out = pl.pallas_call(
        functools.partial(backward_exchange, x, n_src, n_grp),
        out_shape=(sds(block, BF16), sds((nodes, hid), BF16)),
        in_specs=[SM, SM, VM, ANY, ANY],
        out_specs=(ANY, ANY),
        scratch_shapes=[pltpu.VMEM((n_src, slots, blk, blk), BF16), pltpu.VMEM(block, BF16), dma((n_src,)), dma((n_src,)),
                        dma((n_grp - 1,)), dma((n_grp - 1,)), dma((n_src,)), dma],
        compiler_params=params(2), name="backward_exchange",
    )(rows_out, live, scaled, outer, out_all)

    pulled = pl.pallas_call(
        functools.partial(pull_kernel, x, n_src, n_grp),
        out_shape=sds((n_blk, blk, fw), BF16),
        in_specs=[SM, SM, SM, VM, ANY, ANY],
        out_specs=VM,
        scratch_shapes=[pltpu.VMEM((n_blk, blk, fw), F32), pltpu.VMEM((n_in, blk, blk), BF16), pltpu.VMEM(block, BF16), dma, dma],
        compiler_params=params(), name="pull",
    )(rows_in, cols_in, idx, scaled, inc_back, inner)

    feature_grad = pl.pallas_call(
        functools.partial(finish_kernel, n_grp),
        out_shape=sds((n_blk, blk, fw), F32),
        in_specs=[VM, VM],
        out_specs=VM,
        scratch_shapes=[pltpu.VMEM((n_grp - 1, own_blk, blk, fw), BF16), pltpu.VMEM((n_blk, blk, fw), BF16)] + [dma((n_grp - 1,))] * 4,
        compiler_params=params(3), name="finish",
    )(pulled, base)

    return layer_out, feature_grad.reshape(nodes, fw), grads[:fw], grads[fw:]


def solution(mesh):
    placed = (
        P("dom", None),
        P(None, "grp"),
        P(None, "grp"),
        P("dom", "grp"),
        P("dom", None),
        P("dom", None),
        P("dom", None, None, None),
        P("dom", None, None),
        P("dom", None),
        P("dom", None, None, None),
        P("dom", None),
    )
    return jax.shard_map(
        shards,
        mesh=mesh,
        in_specs=placed,
        out_specs=(P("dom", "grp"), P("dom", None), P(None, "grp"), P(None, "grp")),
        check_vma=False,
    )
```

```python
import functools

import jax
import jax.numpy as jnp
from jax import lax
from jax.experimental import pallas as pl
from jax.experimental.pallas import tpu as pltpu
from jax.sharding import PartitionSpec as P

MESH = pl.DeviceIdType.MESH
ANY = pl.BlockSpec(memory_space=pl.ANY)
VM = pl.BlockSpec(memory_space=pltpu.VMEM)
SM = pl.BlockSpec(memory_space=pltpu.SMEM)
HB = pl.BlockSpec(memory_space=pltpu.HBM)
F32 = jnp.float32
BF16 = jnp.bfloat16
TRANS_A = (((0,), (0,)), ((), ()))
TRANS_B = (((1,), (1,)), ((), ()))


def x_extent(parts):
    return 4 if parts == 64 else 1


def plane_peer(i, q, g, x):
    z = q // (2 * x)
    return (((i // x) * 2 + (z + g // 2) % 2) * x + i % x) * 2 + (q + g) % 2


def plane_slot(q, x):
    return (q // (4 * x)) * x + (q // 2) % x


def enter(peers, count):
    barrier = pltpu.get_barrier_semaphore()
    for peer in peers:
        peer(barrier)
    pl.semaphore_wait(barrier, count)


def signal_plane(q, g, x, n_src):
    slot = plane_slot(q, x)

    def go(barrier):
        @pl.when(g != 0)
        def _():
            pl.semaphore_signal(barrier, inc=1, device_id=(plane_peer(slot, q, g, x), g), device_id_type=MESH)

        @pl.loop(1, n_src)
        def _(i):
            peer = plane_peer((slot + i) % n_src, q, g, x)
            pl.semaphore_signal(barrier, inc=1, device_id=(peer, g), device_id_type=MESH)

    return go


def signal_group(q, g, n_grp):
    def go(barrier):
        for r in range(1, n_grp):
            pl.semaphore_signal(barrier, inc=1, device_id=(q, (g + r) % n_grp), device_id_type=MESH)

    return go


def forward_exchange(x, n_src, n_grp, table, features, cot, w_self, w_neigh, inc, cot_all, w_all, feat, stage, send, recv, cot_s, cot_r, w_s, w_r, loc):
    q, g = lax.axis_index("dom"), lax.axis_index("grp")
    slots = stage.shape[1]
    quarter = cot_all.shape[1]
    fw = w_self.shape[0]
    slot = plane_slot(q, x)
    barrier = pltpu.get_barrier_semaphore()
    load_feat = pltpu.make_async_copy(features, feat, loc.at[3])
    load_feat.start()
    signal_plane(q, g, x, n_src)(barrier)
    signal_group(q, g, n_grp)(barrier)
    own = [
        pltpu.make_async_copy(cot.at[pl.ds(g * quarter, quarter)], cot_all.at[g], loc.at[0]),
        pltpu.make_async_copy(w_self, w_all.at[g, pl.ds(0, fw)], loc.at[1]),
        pltpu.make_async_copy(w_neigh, w_all.at[g, pl.ds(fw, fw)], loc.at[2]),
    ]
    for c in own:
        c.start()

    def fill(d):
        peer = plane_peer(d, q, g, x)
        for s in range(slots):
            stage[d, s] = feat[table[peer * slots + s]]
        return peer

    def remote(d, peer):
        return pltpu.make_async_remote_copy(
            src_ref=stage.at[d], dst_ref=inc.at[slot], send_sem=send.at[d], recv_sem=recv.at[slot],
            device_id=(peer, g), device_id_type=MESH)

    load_feat.wait()
    home = fill(slot)

    @pl.when(g == 0)
    def _():
        pl.semaphore_wait(barrier, n_src - 1 + n_grp - 1)

    @pl.when(g != 0)
    def _():
        pl.semaphore_wait(barrier, n_src + n_grp - 1)

    far = []
    for r in range(1, n_grp):
        y = (g + r) % n_grp
        to = dict(device_id=(q, y), device_id_type=MESH)
        far.append(pltpu.make_async_remote_copy(
            src_ref=cot.at[pl.ds(y * quarter, quarter)], dst_ref=cot_all.at[g],
            send_sem=cot_s.at[r - 1], recv_sem=cot_r.at[r - 1], **to))
        far.append(pltpu.make_async_remote_copy(
            src_ref=w_self, dst_ref=w_all.at[g, pl.ds(0, fw)],
            send_sem=w_s.at[r - 1, 0], recv_sem=w_r.at[r - 1, 0], **to))
        far.append(pltpu.make_async_remote_copy(
            src_ref=w_neigh, dst_ref=w_all.at[g, pl.ds(fw, fw)],
            send_sem=w_s.at[r - 1, 1], recv_sem=w_r.at[r - 1, 1], **to))

    @pl.when(g == 0)
    def _():
        pltpu.make_async_copy(stage.at[slot], inc.at[slot], recv.at[slot]).start()

    @pl.when(g != 0)
    def _():
        remote(slot, home).start()

    @pl.loop(1, n_src)
    def _(i):
        d = (slot + i) % n_src
        remote(d, fill(d)).start()

    for c in far:
        c.start()
    for c in own:
        c.wait()
    for c in far:
        c.wait()

    @pl.when(g != 0)
    def _():
        remote(slot, home).wait_send()

    @pl.loop(1, n_src)
    def _(i):
        d = (slot + i) % n_src
        remote(d, plane_peer(d, q, g, x)).wait_send()

    @pl.loop(0, n_src)
    def _(j):
        pltpu.make_async_copy(stage.at[j], inc.at[j], recv.at[j]).wait()


def tables(parts, slots, n_inner):
    out_rows = parts * slots
    live = 2 * parts * slots
    return out_rows, live, live + parts, live + parts + n_inner


def aggregate_kernel(x, n_src, n_grp, table, features, inc, inner, outer, part, deg, feat, acc, deg_acc, a_in, a_out, x_in, sem_f, sem_in, sem_out, sem_x):
    q, g = lax.axis_index("dom"), lax.axis_index("grp")
    slots = inc.shape[1]
    n_in = inner.shape[0] // n_grp
    out_rows, live, in_rows, in_cols = tables(n_grp * n_src, slots, inner.shape[0])
    load_f = pltpu.make_async_copy(features, feat, sem_f)
    load_f.start()
    load_in = pltpu.make_async_copy(inner.at[pl.ds(g * n_in, n_in)], a_in, sem_in)
    load_in.start()
    load_x = pltpu.make_async_copy(inc, x_in, sem_x)
    load_x.start()

    def load(i):
        peer = plane_peer(i, q, g, x)
        return pltpu.make_async_copy(outer.at[pl.ds(peer * slots, slots)], a_out.at[i], sem_out)

    @pl.loop(0, n_src)
    def _(i):
        load(i).start()

    acc[...] = jnp.zeros_like(acc)
    deg_acc[...] = jnp.zeros_like(deg_acc)
    ones = jnp.ones((8, acc.shape[1]), BF16)

    def add(row, a, b):
        acc[row] += jnp.dot(a, b, preferred_element_type=F32)
        deg_acc[row] += lax.dot_general(ones, a, TRANS_B, preferred_element_type=F32)

    load_f.wait()
    load_in.wait()

    @pl.loop(0, n_in)
    def _(n):
        add(table[in_rows + g * n_in + n], a_in[n], feat[table[in_cols + g * n_in + n]])

    load_x.wait()
    pltpu.make_async_copy(a_out, a_out, sem_out).wait()

    @pl.loop(0, n_src)
    def _(i):
        peer = plane_peer(i, q, g, x)
        for s in range(slots):
            @pl.when(s < table[live + peer])
            def _():
                add(table[out_rows + peer * slots + s], a_out[i, s], x_in[i, s])

    part[...] = acc[...].astype(BF16)
    deg[...] = deg_acc[...]


def dense_kernel(n_grp, part, deg, features, cots, ws, out_all, scaled, base, wgrad, feat, cot_all, w_all, got, got_d, sent, s1, r1, s2, r2, s3, r3, loc):
    q, g = lax.axis_index("dom"), lax.axis_index("grp")
    n_blk, blk, fw = part.shape
    own_blk = n_blk // n_grp
    rows, hid = own_blk * blk, ws.shape[2]
    mine = pl.ds(g * own_blk, own_blk)
    barrier = pltpu.get_barrier_semaphore()
    signal_group(q, g, n_grp)(barrier)
    loads = [
        pltpu.make_async_copy(features.at[mine], feat, loc.at[0]),
        pltpu.make_async_copy(ws, w_all, loc.at[1]),
        pltpu.make_async_copy(cots, cot_all, loc.at[2]),
    ]
    for c in loads:
        c.start()
    pl.semaphore_wait(barrier, n_grp - 1)
    copies, last = [], []
    for r in range(1, n_grp):
        y = (g + r) % n_grp
        to = dict(device_id=(q, y), device_id_type=MESH)
        theirs = pl.ds(y * own_blk, own_blk)
        copies.append(pltpu.make_async_remote_copy(
            src_ref=part.at[theirs], dst_ref=got.at[r - 1], send_sem=s1.at[r - 1], recv_sem=r1.at[r - 1], **to))
        copies.append(pltpu.make_async_remote_copy(
            src_ref=deg.at[theirs], dst_ref=got_d.at[r - 1], send_sem=s2.at[r - 1], recv_sem=r2.at[r - 1], **to))
        last.append(pltpu.make_async_remote_copy(
            src_ref=sent, dst_ref=scaled.at[mine], send_sem=s3.at[r - 1], recv_sem=r3.at[r - 1], **to))
    for c in copies:
        c.start()
    for c in loads:
        c.wait()
    for c in copies:
        c.wait()
    total = part[mine].astype(F32)
    degree = 1.0 + deg[mine]
    for r in range(n_grp - 1):
        total = total + got[r].astype(F32)
        degree = degree + got_d[r]
    own_feat = feat[...]
    divisor = jnp.stack([jnp.broadcast_to(degree[b, 0:1, :], (blk, blk)).T for b in range(own_blk)])
    agg = ((own_feat.astype(F32) + total) / divisor).astype(BF16)
    both = jnp.concatenate([own_feat.reshape(rows, fw), agg.reshape(rows, fw)], axis=1)
    back = jnp.zeros((rows, 2 * fw), F32)
    for j in range(n_grp):
        pre = jnp.dot(both, w_all[j], preferred_element_type=F32)
        sig = jax.nn.sigmoid(pre)
        out_all[j] = (pre * sig).astype(BF16)
        grad = (cot_all[j].astype(F32) * sig * (1.0 + pre * (1.0 - sig))).astype(BF16)
        gw = lax.dot_general(both, grad, TRANS_A, preferred_element_type=F32).astype(BF16)
        for h in range(hid // 128):
            wgrad[j, h] = gw[:, 128 * h:128 * (h + 1)]
        back = back + lax.dot_general(grad, w_all[j], TRANS_B, preferred_element_type=F32)
    down = (back[:, fw:].reshape(own_blk, blk, fw) / divisor).astype(BF16)
    sent[...] = down
    scaled[mine] = down
    base[...] = back[:, :fw].reshape(own_blk, blk, fw) + down.astype(F32)
    for c in last:
        c.start()
    for c in last:
        c.wait()


def backward_exchange(x, n_src, n_grp, table, scaled, outer, out_all, wgrad, inc, out, wsum, a_out, stage, w_got, send, recv, o_s, o_r, w_s, w_r, a_sem, loc):
    q, g = lax.axis_index("dom"), lax.axis_index("grp")
    slots = stage.shape[1]
    quarter = out_all.shape[1]
    slot = plane_slot(q, x)
    out_rows, live, _, _ = tables(n_grp * n_src, slots, 0)
    barrier = pltpu.get_barrier_semaphore()
    signal_plane(q, g, x, n_src)(barrier)
    signal_group(q, g, n_grp)(barrier)

    def load(d):
        peer = plane_peer(d, q, g, x)
        return pltpu.make_async_copy(outer.at[pl.ds(peer * slots, slots)], a_out.at[d], a_sem.at[d])

    @pl.loop(0, n_src)
    def _(i):
        load((slot + i) % n_src).start()

    own = pltpu.make_async_copy(out_all.at[g], out.at[g], loc)
    own.start()

    def fill(d):
        peer = plane_peer(d, q, g, x)
        load(d).wait()
        for s in range(slots):
            value = lax.dot_general(a_out[d, s], scaled[table[out_rows + peer * slots + s]], TRANS_A, preferred_element_type=F32)
            stage[d, s] = jnp.where(s < table[live + peer], value, 0.0).astype(BF16)
        return peer

    def remote(d, peer):
        return pltpu.make_async_remote_copy(
            src_ref=stage.at[d], dst_ref=inc.at[slot], send_sem=send.at[d], recv_sem=recv.at[slot],
            device_id=(peer, g), device_id_type=MESH)

    home = fill(slot)

    @pl.when(g == 0)
    def _():
        pl.semaphore_wait(barrier, n_src - 1 + n_grp - 1)

    @pl.when(g != 0)
    def _():
        pl.semaphore_wait(barrier, n_src + n_grp - 1)

    far, grad_far = [], []
    for r in range(1, n_grp):
        y = (g + r) % n_grp
        far.append(pltpu.make_async_remote_copy(
            src_ref=out_all.at[y], dst_ref=out.at[g],
            send_sem=o_s.at[r - 1], recv_sem=o_r.at[r - 1], device_id=(q, y), device_id_type=MESH))
        grad_far.append(pltpu.make_async_remote_copy(
            src_ref=wgrad.at[y], dst_ref=w_got.at[r - 1],
            send_sem=w_s.at[r - 1], recv_sem=w_r.at[r - 1], device_id=(q, y), device_id_type=MESH))
    for c in grad_far:
        c.start()

    @pl.when(g == 0)
    def _():
        pltpu.make_async_copy(stage.at[slot], inc.at[slot], recv.at[slot]).start()

    @pl.when(g != 0)
    def _():
        remote(slot, home).start()

    @pl.loop(1, n_src)
    def _(i):
        d = (slot + i) % n_src
        remote(d, fill(d)).start()

    for c in far:
        c.start()
    own.wait()
    for c in grad_far:
        c.wait()
    for h in range(wsum.shape[0]):
        total = wgrad[g, h].astype(F32)
        for r in range(n_grp - 1):
            total = total + w_got[r, h].astype(F32)
        wsum[h] = total
    for c in far:
        c.wait()

    @pl.when(g != 0)
    def _():
        remote(slot, home).wait_send()

    @pl.loop(1, n_src)
    def _(i):
        d = (slot + i) % n_src
        remote(d, plane_peer(d, q, g, x)).wait_send()

    @pl.loop(0, n_src)
    def _(j):
        pltpu.make_async_copy(stage.at[j], inc.at[j], recv.at[j]).wait()


def pull_kernel(x, n_src, n_grp, table, scaled, inc, inner, out_parts, part, out, acc, a_in, x_in, sem_in, sem_x, sem_o):
    q, g = lax.axis_index("dom"), lax.axis_index("grp")
    slots = inc.shape[1]
    n_in = inner.shape[0] // n_grp
    load_in = pltpu.make_async_copy(inner.at[pl.ds(g * n_in, n_in)], a_in, sem_in)
    load_in.start()
    load_x = pltpu.make_async_copy(inc, x_in, sem_x)
    load_x.start()
    keep = pltpu.make_async_copy(out_parts, out, sem_o)
    keep.start()
    _, _, in_rows, in_cols = tables(n_grp * n_src, slots, inner.shape[0])
    acc[...] = jnp.zeros_like(acc)
    load_in.wait()

    @pl.loop(0, n_in)
    def _(n):
        acc[table[in_cols + g * n_in + n]] += lax.dot_general(
            a_in[n], scaled[table[in_rows + g * n_in + n]], TRANS_A, preferred_element_type=F32)

    load_x.wait()

    @pl.loop(0, n_src)
    def _(i):
        peer = plane_peer(i, q, g, x)
        for s in range(slots):
            acc[table[peer * slots + s]] += x_in[i, s].astype(F32)

    part[...] = acc[...].astype(BF16)
    keep.wait()


def finish_kernel(x, n_grp, part, base, pieces, whole, grads, got, near_got, far_sent, far_got, s1, r1, s2, r2, a_s, a_r, b_s, b_r, c_s, c_r, d_s, d_r):
    q, g = lax.axis_index("dom"), lax.axis_index("grp")
    own_blk = base.shape[0]
    near, layers = near_got.shape[0], near_got.shape[1]
    mine = pl.ds(g * own_blk, own_blk)
    z, k = q // near, q % near
    barrier = pltpu.get_barrier_semaphore()
    signal_group(q, g, n_grp)(barrier)

    @pl.loop(1, near)
    def _(r):
        pl.semaphore_signal(barrier, inc=1, device_id=(z * near + (k + r) % near, g), device_id_type=MESH)

    @pl.loop(1, layers)
    def _(r):
        pl.semaphore_signal(barrier, inc=1, device_id=((z + r) % layers * near + k, g), device_id_type=MESH)

    first, last = [], []
    for r in range(1, n_grp):
        y = (g + r) % n_grp
        to = dict(device_id=(q, y), device_id_type=MESH)
        first.append(pltpu.make_async_remote_copy(
            src_ref=part.at[pl.ds(y * own_blk, own_blk)], dst_ref=got.at[r - 1],
            send_sem=s1.at[r - 1], recv_sem=r1.at[r - 1], **to))
        last.append(pltpu.make_async_remote_copy(
            src_ref=whole.at[mine], dst_ref=whole.at[mine], send_sem=s2.at[r - 1], recv_sem=r2.at[r - 1], **to))

    def near_peer(r):
        return (k + r) % near

    def far_peer(r):
        return (z + r) % layers

    def near_reduce(r):
        return pltpu.make_async_remote_copy(
            src_ref=pieces.at[pl.ds(near_peer(r) * layers, layers)], dst_ref=near_got.at[r],
            send_sem=a_s.at[r], recv_sem=a_r.at[r], device_id=(z * near + near_peer(r), g), device_id_type=MESH)

    def far_reduce(r):
        return pltpu.make_async_remote_copy(
            src_ref=far_sent.at[far_peer(r)], dst_ref=far_got.at[r],
            send_sem=b_s.at[r], recv_sem=b_r.at[r], device_id=(far_peer(r) * near + k, g), device_id_type=MESH)

    def far_gather(r):
        return pltpu.make_async_remote_copy(
            src_ref=grads.at[k * layers + z], dst_ref=grads.at[k * layers + z],
            send_sem=c_s.at[r], recv_sem=c_r.at[r], device_id=(far_peer(r) * near + k, g), device_id_type=MESH)

    def near_gather(r):
        return pltpu.make_async_remote_copy(
            src_ref=grads.at[pl.ds(k * layers, layers)], dst_ref=grads.at[pl.ds(k * layers, layers)],
            send_sem=d_s.at[r], recv_sem=d_r.at[r], device_id=(z * near + near_peer(r), g), device_id_type=MESH)

    def each(count, make, act):
        @pl.loop(1, count)
        def _(r):
            act(make(r))

    pl.semaphore_wait(barrier, n_grp - 1 + near - 1 + layers - 1)
    for c in first:
        c.start()
    each(near, near_reduce, lambda c: c.start())
    each(near, near_reduce, lambda c: c.wait())
    total = pieces[pl.ds(k * layers, layers)]
    for r in range(1, near):
        total = total + near_got[r]
    far_sent[...] = total
    each(layers, far_reduce, lambda c: c.start())
    for c in first:
        c.wait()
    total = base[...] + part[mine].astype(F32)
    for r in range(n_grp - 1):
        total = total + got[r].astype(F32)
    whole[mine] = total.astype(BF16)
    for c in last:
        c.start()
    each(layers, far_reduce, lambda c: c.wait())
    total = far_sent[z]
    for r in range(1, layers):
        total = total + far_got[r]
    grads[k * layers + z] = total
    each(layers, far_gather, lambda c: c.start())
    each(layers, far_gather, lambda c: c.wait())
    each(near, near_gather, lambda c: c.start())
    each(near, near_gather, lambda c: c.wait())
    for c in last:
        c.wait()


def params(collective=None, vmem=48):
    if collective is None:
        return pltpu.CompilerParams(vmem_limit_bytes=vmem << 20)
    return pltpu.CompilerParams(vmem_limit_bytes=vmem << 20, collective_id=collective, has_side_effects=True)


def shards(features, w_self, w_neigh, cotangent, inner_rows, inner_cols, inner_values, send_blocks, outer_rows, outer_values, live_count):
    blk = inner_values.shape[-1]
    nodes, fw = features.shape
    n_blk = nodes // blk
    parts, n_grp = lax.axis_size("dom"), lax.axis_size("grp")
    x = x_extent(parts)
    n_src = parts // n_grp
    slots = send_blocks.shape[-1]
    hid = w_self.shape[1]
    own_blk = n_blk // n_grp
    rows = own_blk * blk
    n_in = inner_values.shape[1] // n_grp
    inner, outer = inner_values[0], outer_values[0]
    table = jnp.concatenate([send_blocks.reshape(-1), outer_rows[0], live_count[0], inner_rows[0], inner_cols[0]])
    feat = features.reshape(n_blk, blk, fw)
    dma, sds = pltpu.SemaphoreType.DMA, jax.ShapeDtypeStruct
    block = (n_src, slots, blk, fw)

    inc, cot_all, w_all = pl.pallas_call(
        functools.partial(forward_exchange, x, n_src, n_grp),
        out_shape=(sds(block, BF16), sds((n_grp, rows, hid), BF16), sds((n_grp, 2 * fw, hid), BF16)),
        in_specs=[SM, HB, HB, HB, HB],
        out_specs=(ANY, ANY, ANY),
        scratch_shapes=[pltpu.VMEM((n_blk, blk, fw), BF16), pltpu.VMEM(block, BF16), dma((n_src,)), dma((n_src,)), dma((n_grp - 1,)), dma((n_grp - 1,)),
                        dma((n_grp - 1, 2)), dma((n_grp - 1, 2)), dma((4,))],
        compiler_params=params(0), name="forward_exchange",
    )(table, feat, cotangent, w_self, w_neigh)

    part, deg = pl.pallas_call(
        functools.partial(aggregate_kernel, x, n_src, n_grp),
        out_shape=(sds((n_blk, blk, fw), BF16), sds((n_blk, 8, blk), F32)),
        in_specs=[SM, HB, ANY, HB, HB],
        out_specs=(VM, VM),
        scratch_shapes=[pltpu.VMEM((n_blk, blk, fw), BF16), pltpu.VMEM((n_blk, blk, fw), F32), pltpu.VMEM((n_blk, 8, blk), F32),
                        pltpu.VMEM((n_in, blk, blk), BF16), pltpu.VMEM((n_src, slots, blk, blk), BF16),
                        pltpu.VMEM(block, BF16), dma, dma, dma, dma],
        compiler_params=params(), name="aggregate",
    )(table, feat, inc, inner, outer)

    y_sems = [dma((n_grp - 1,))] * 6
    out_all, scaled, base, wgrad = pl.pallas_call(
        functools.partial(dense_kernel, n_grp),
        out_shape=(sds((n_grp, rows, hid), BF16), sds((n_blk, blk, fw), BF16), sds((own_blk, blk, fw), F32), sds((n_grp, hid // 128, 2 * fw, 128), BF16)),
        in_specs=[VM, VM, HB, ANY, ANY],
        out_specs=(VM,) * 4,
        scratch_shapes=[pltpu.VMEM((own_blk, blk, fw), BF16), pltpu.VMEM((n_grp, rows, hid), BF16), pltpu.VMEM((n_grp, 2 * fw, hid), BF16),
                        pltpu.VMEM((n_grp - 1, own_blk, blk, fw), BF16), pltpu.VMEM((n_grp - 1, own_blk, 8, blk), F32),
                        pltpu.VMEM((own_blk, blk, fw), BF16)] + y_sems + [dma((3,))],
        compiler_params=params(1), name="dense",
    )(part, deg, feat, cot_all, w_all)

    halves = hid // 128
    inc_back, out_parts, wsum = pl.pallas_call(
        functools.partial(backward_exchange, x, n_src, n_grp),
        out_shape=(sds(block, BF16), sds((n_grp, rows, hid), BF16), sds((halves, 2 * fw, 128), F32)),
        in_specs=[SM, VM, HB, ANY, VM],
        out_specs=(ANY, ANY, VM),
        scratch_shapes=[pltpu.VMEM((n_src, slots, blk, blk), BF16), pltpu.VMEM(block, BF16), pltpu.VMEM((n_grp - 1, halves, 2 * fw, 128), BF16),
                        dma((n_src,)), dma((n_src,)), dma((n_grp - 1,)), dma((n_grp - 1,)), dma((n_grp - 1,)), dma((n_grp - 1,)),
                        dma((n_src,)), dma],
        compiler_params=params(2), name="backward_exchange",
    )(table, scaled, outer, out_all, wgrad)

    pulled, layer_out = pl.pallas_call(
        functools.partial(pull_kernel, x, n_src, n_grp),
        out_shape=(sds((n_blk, blk, fw), BF16), sds((n_grp, rows, hid), BF16)),
        in_specs=[SM, VM, ANY, HB, ANY],
        out_specs=(VM, ANY),
        scratch_shapes=[pltpu.VMEM((n_blk, blk, fw), F32), pltpu.VMEM((n_in, blk, blk), BF16), pltpu.VMEM(block, BF16), dma, dma, dma],
        compiler_params=params(), name="pull",
    )(table, scaled, inc_back, inner, out_parts)

    near = 2 * x
    layers = parts // near
    pieces = wsum.reshape(parts, -1, 128)
    depth = pieces.shape[1]
    whole, grads = pl.pallas_call(
        functools.partial(finish_kernel, x, n_grp),
        out_shape=(sds((n_blk, blk, fw), BF16), sds(pieces.shape, F32)),
        in_specs=[VM, VM, VM],
        out_specs=(VM, VM),
        scratch_shapes=[pltpu.VMEM((n_grp - 1, own_blk, blk, fw), BF16), pltpu.VMEM((near, layers, depth, 128), F32), pltpu.VMEM((layers, depth, 128), F32),
                        pltpu.VMEM((layers, depth, 128), F32)]
        + [dma((n_grp - 1,))] * 4 + [dma((near,))] * 2 + [dma((layers,))] * 2 + [dma((layers,))] * 2 + [dma((near,))] * 2,
        compiler_params=params(3), name="finish",
    )(pulled, base, pieces)
    grads = jnp.concatenate([grads.reshape(halves, 2 * fw, 128)[h] for h in range(halves)], axis=1)
    feature_grad = whole.astype(F32)
    layer_out = layer_out.reshape(nodes, hid)

    return layer_out, feature_grad.reshape(nodes, fw), grads[:fw], grads[fw:]


def solution(mesh):
    placed = (
        P("dom", None),
        P(None, "grp"),
        P(None, "grp"),
        P("dom", "grp"),
        P("dom", None),
        P("dom", None),
        P("dom", None, None, None),
        P("dom", None, None),
        P("dom", None),
        P("dom", None, None, None),
        P("dom", None),
    )
    return jax.shard_map(
        shards,
        mesh=mesh,
        in_specs=placed,
        out_specs=(P("dom", "grp"), P("dom", None), P(None, "grp"), P(None, "grp")),
        check_vma=False,
    )
```

```python
import functools

import jax
import jax.numpy as jnp
from jax import lax
from jax.experimental import pallas as pl
from jax.experimental.pallas import tpu as pltpu
from jax.sharding import PartitionSpec as P

MESH = pl.DeviceIdType.MESH
ANY = pl.BlockSpec(memory_space=pl.ANY)
VM = pl.BlockSpec(memory_space=pltpu.VMEM)
SM = pl.BlockSpec(memory_space=pltpu.SMEM)
HB = pl.BlockSpec(memory_space=pltpu.HBM)
F32 = jnp.float32
BF16 = jnp.bfloat16
TRANS_A = (((0,), (0,)), ((), ()))
TRANS_B = (((1,), (1,)), ((), ()))


def x_extent(parts):
    return 4 if parts == 64 else 1


def plane_peer(i, q, g, x):
    z = q // (2 * x)
    return (((i // x) * 2 + (z + g // 2) % 2) * x + i % x) * 2 + (q + g) % 2


def plane_slot(q, x):
    return (q // (4 * x)) * x + (q // 2) % x


def enter(peers, count):
    barrier = pltpu.get_barrier_semaphore()
    for peer in peers:
        peer(barrier)
    pl.semaphore_wait(barrier, count)


def signal_plane(q, g, x, n_src):
    slot = plane_slot(q, x)

    def go(barrier):
        @pl.when(g != 0)
        def _():
            pl.semaphore_signal(barrier, inc=1, device_id=(plane_peer(slot, q, g, x), g), device_id_type=MESH)

        @pl.loop(1, n_src)
        def _(i):
            peer = plane_peer((slot + i) % n_src, q, g, x)
            pl.semaphore_signal(barrier, inc=1, device_id=(peer, g), device_id_type=MESH)

    return go


def signal_group(q, g, n_grp):
    def go(barrier):
        for r in range(1, n_grp):
            pl.semaphore_signal(barrier, inc=1, device_id=(q, (g + r) % n_grp), device_id_type=MESH)

    return go


def tables(parts, slots, n_inner):
    out_rows = parts * slots
    live = 2 * parts * slots
    return out_rows, live, live + parts, live + parts + n_inner


def signal_ring(q, g, near, layers):
    z, k = q // near, q % near

    def go(barrier):
        @pl.loop(1, near)
        def _(r):
            pl.semaphore_signal(barrier, inc=1, device_id=(z * near + (k + r) % near, g), device_id_type=MESH)

        @pl.loop(1, layers)
        def _(r):
            pl.semaphore_signal(barrier, inc=1, device_id=((z + r) % layers * near + k, g), device_id_type=MESH)

    return go


def each(first, count, make, act):
    @pl.loop(first, count)
    def _(r):
        act(make(r))


def start(c):
    c.start()


def wait(c):
    c.wait()


def forward_exchange(x, n_src, n_grp, table, keys, places, features, cot, w_self, w_neigh, inner, outer,
                     inc, cot_all, w_all, place_all, cols, divisor,
                     feat, stage, blocks, row_sums, send, recv, cot_s, cot_r, w_s, w_r, p_s, p_r, loc):
    q, g = lax.axis_index("dom"), lax.axis_index("grp")
    slots = stage.shape[1]
    own = cot_all.shape[2]
    fw = w_self.shape[0]
    n_blk, blk, _ = feat.shape
    near = 2 * x
    layers = places.shape[0]
    z, k = q // near, q % near
    slot = plane_slot(q, x)
    n_out, n_in = outer.shape[0], inner.shape[0]
    barrier = pltpu.get_barrier_semaphore()
    load_feat = pltpu.make_async_copy(features, feat, loc.at[3])
    load_feat.start()
    signal_plane(q, g, x, n_src)(barrier)
    signal_group(q, g, n_grp)(barrier)

    @pl.loop(1, layers)
    def _(r):
        pl.semaphore_signal(barrier, inc=1, device_id=((z + r) % layers * near + k, g), device_id_type=MESH)

    mine = pl.ds(pl.multiple_of(g * own, own), own)
    local = [
        pltpu.make_async_copy(cot.at[:, mine], cot_all.at[g], loc.at[0]),
        pltpu.make_async_copy(w_self, w_all.at[g, pl.ds(0, fw)], loc.at[1]),
        pltpu.make_async_copy(w_neigh, w_all.at[g, pl.ds(fw, fw)], loc.at[2]),
        pltpu.make_async_copy(places.at[z], place_all.at[z], loc.at[6]),
    ]
    loads = [
        pltpu.make_async_copy(outer, blocks.at[pl.ds(0, n_out)], loc.at[4]),
        pltpu.make_async_copy(inner, blocks.at[pl.ds(n_out, n_in)], loc.at[5]),
    ]

    def fill(d):
        peer = plane_peer(d, q, g, x)
        for s in range(slots):
            stage[d, s] = feat[table[peer * slots + s]]
        return peer

    def remote(d, peer):
        return pltpu.make_async_remote_copy(
            src_ref=stage.at[d], dst_ref=inc.at[slot], send_sem=send.at[d], recv_sem=recv.at[slot],
            device_id=(peer, g), device_id_type=MESH)

    def place(r):
        to = (z + r) % layers
        return pltpu.make_async_remote_copy(
            src_ref=places.at[to], dst_ref=place_all.at[z], send_sem=p_s.at[r], recv_sem=p_r.at[r],
            device_id=(to * near + k, g), device_id_type=MESH)

    load_feat.wait()
    home = fill(slot)
    others = n_grp - 1 + layers - 1

    @pl.when(g == 0)
    def _():
        pl.semaphore_wait(barrier, n_src - 1 + others)

    @pl.when(g != 0)
    def _():
        pl.semaphore_wait(barrier, n_src + others)

    far = []
    for r in range(1, n_grp):
        y = (g + r) % n_grp
        to = dict(device_id=(q, y), device_id_type=MESH)
        theirs = pl.ds(pl.multiple_of(y * own, own), own)
        far.append(pltpu.make_async_remote_copy(
            src_ref=cot.at[:, theirs], dst_ref=cot_all.at[g],
            send_sem=cot_s.at[r - 1], recv_sem=cot_r.at[r - 1], **to))
        far.append(pltpu.make_async_remote_copy(
            src_ref=w_self, dst_ref=w_all.at[g, pl.ds(0, fw)],
            send_sem=w_s.at[r - 1, 0], recv_sem=w_r.at[r - 1, 0], **to))
        far.append(pltpu.make_async_remote_copy(
            src_ref=w_neigh, dst_ref=w_all.at[g, pl.ds(fw, fw)],
            send_sem=w_s.at[r - 1, 1], recv_sem=w_r.at[r - 1, 1], **to))

    @pl.when(g == 0)
    def _():
        pltpu.make_async_copy(stage.at[slot], inc.at[slot], recv.at[slot]).start()

    @pl.when(g != 0)
    def _():
        remote(slot, home).start()

    @pl.loop(1, n_src)
    def _(i):
        d = (slot + i) % n_src
        remote(d, fill(d)).start()

    for c in far + local + loads:
        c.start()
    each(1, layers, place, start)

    row = lax.broadcasted_iota(jnp.int32, (own + 16, blk), 0)
    lane = lax.broadcasted_iota(jnp.int32, (own + 16, blk), 1)
    pick = jnp.where((row == own) | (lane == row + g * own) & (row < own), 1.0, 0.0).astype(BF16)
    for c in loads:
        c.wait()

    @pl.loop(0, (n_out + n_in) // 4)
    def _(m):
        for u in range(4):
            n = m * 4 + u
            got = lax.dot_general(pick, blocks[n], TRANS_B, preferred_element_type=F32)
            cols[n] = got[:own].astype(BF16)
            row_sums[pl.ds(n, 1), :] = got[own:own + 1]

    hits = jnp.where(lax.broadcasted_iota(jnp.int32, (n_blk, n_out + n_in), 0) == keys[...], 1.0, 0.0)
    degree = 1.0 + jnp.dot(hits, row_sums[...], precision=lax.Precision.HIGHEST, preferred_element_type=F32)
    sel = (lax.broadcasted_iota(jnp.int32, (own, blk), 1) == lax.broadcasted_iota(jnp.int32, (own, blk), 0) + g * own)
    for b in range(n_blk):
        column = jnp.sum(jnp.where(sel, degree[b:b + 1], 0.0), axis=1, keepdims=True)
        divisor[b] = jnp.broadcast_to(column, (own, fw))

    for c in local:
        c.wait()
    for c in far:
        c.wait()
    each(1, layers, place, wait)

    @pl.when(g != 0)
    def _():
        remote(slot, home).wait_send()

    @pl.loop(1, n_src)
    def _(i):
        d = (slot + i) % n_src
        remote(d, plane_peer(d, q, g, x)).wait_send()

    @pl.loop(0, n_src)
    def _(j):
        pltpu.make_async_copy(stage.at[j], inc.at[j], recv.at[j]).wait()


def aggregate_kernel(x, n_src, n_grp, table, features, inc, inner, outer, part, feat, acc, a_in, a_out, x_in, sem_f, sem_in, sem_out, sem_x):
    q, g = lax.axis_index("dom"), lax.axis_index("grp")
    slots = inc.shape[1]
    n_in = inner.shape[0] // n_grp
    out_rows, live, in_rows, in_cols = tables(n_grp * n_src, slots, inner.shape[0])
    load_f = pltpu.make_async_copy(features, feat, sem_f)
    load_f.start()
    load_in = pltpu.make_async_copy(inner.at[pl.ds(g * n_in, n_in)], a_in, sem_in)
    load_in.start()
    load_x = pltpu.make_async_copy(inc, x_in, sem_x)
    load_x.start()

    def load(i):
        peer = plane_peer(i, q, g, x)
        return pltpu.make_async_copy(outer.at[pl.ds(peer * slots, slots)], a_out.at[i], sem_out)

    @pl.loop(0, n_src)
    def _(i):
        load(i).start()

    acc[...] = jnp.zeros_like(acc)
    load_f.wait()
    load_in.wait()

    @pl.loop(0, n_in)
    def _(n):
        acc[table[in_rows + g * n_in + n]] += jnp.dot(
            a_in[n], feat[table[in_cols + g * n_in + n]], preferred_element_type=F32)

    load_x.wait()
    pltpu.make_async_copy(a_out, a_out, sem_out).wait()

    @pl.loop(0, n_src)
    def _(i):
        peer = plane_peer(i, q, g, x)
        for s in range(slots):
            @pl.when(s < table[live + peer])
            def _():
                acc[table[out_rows + peer * slots + s]] += jnp.dot(a_out[i, s], x_in[i, s], preferred_element_type=F32)

    part[...] = acc[...].astype(BF16)


def dense_kernel(n_grp, part, features, divisor, cots, ws, out_all, scaled, base, wgrad, feat, cot_all, w_all, got, sent, s1, r1, s3, r3, loc):
    q, g = lax.axis_index("dom"), lax.axis_index("grp")
    n_blk, blk, fw = part.shape
    own = base.shape[1]
    rows, hid = n_blk * own, ws.shape[2]
    mine = pl.ds(pl.multiple_of(g * own, own), own)
    barrier = pltpu.get_barrier_semaphore()
    signal_group(q, g, n_grp)(barrier)
    loads = [
        pltpu.make_async_copy(features.at[:, mine], feat, loc.at[0]),
        pltpu.make_async_copy(ws, w_all, loc.at[1]),
        pltpu.make_async_copy(cots, cot_all, loc.at[2]),
    ]
    for c in loads:
        c.start()
    pl.semaphore_wait(barrier, n_grp - 1)
    copies, last = [], []
    for r in range(1, n_grp):
        y = (g + r) % n_grp
        to = dict(device_id=(q, y), device_id_type=MESH)
        theirs = pl.ds(pl.multiple_of(y * own, own), own)
        copies.append(pltpu.make_async_remote_copy(
            src_ref=part.at[:, theirs], dst_ref=got.at[r - 1], send_sem=s1.at[r - 1], recv_sem=r1.at[r - 1], **to))
        last.append(pltpu.make_async_remote_copy(
            src_ref=sent, dst_ref=scaled.at[:, mine], send_sem=s3.at[r - 1], recv_sem=r3.at[r - 1], **to))
    for c in copies:
        c.start()
    for c in loads:
        c.wait()
    for c in copies:
        c.wait()
    own_feat = feat[...]
    total = own_feat.astype(F32) + part[:, mine].astype(F32)
    for r in range(n_grp - 1):
        total = total + got[r].astype(F32)
    agg = (total / divisor[...]).astype(BF16)
    both = jnp.concatenate([own_feat.reshape(rows, fw), agg.reshape(rows, fw)], axis=1)
    back = jnp.zeros((rows, 2 * fw), F32)
    grads = []
    for j in range(n_grp):
        pre = jnp.dot(both, w_all[j], preferred_element_type=F32)
        sig = jax.nn.sigmoid(pre)
        out_all[j] = (pre * sig).astype(BF16).reshape(n_blk, own, hid)
        cot = cot_all[j].reshape(rows, hid).astype(F32)
        grad = (cot * sig * (1.0 + pre * (1.0 - sig))).astype(BF16)
        grads.append(grad)
        back = back + lax.dot_general(grad, w_all[j], TRANS_B, preferred_element_type=F32)
    down = (back[:, fw:].reshape(n_blk, own, fw) / divisor[...]).astype(BF16)
    sent[...] = down
    for c in last:
        c.start()
    scaled[:, mine] = down
    base[...] = back[:, :fw].reshape(n_blk, own, fw) + down.astype(F32)
    for j in range(n_grp):
        gw = lax.dot_general(both, grads[j], TRANS_A, preferred_element_type=F32).astype(BF16)
        for h in range(hid // 128):
            wgrad[j, h] = gw[:, 128 * h:128 * (h + 1)]
    for c in last:
        c.wait()


def backward_exchange(x, n_grp, table, scaled, cols, out_all, wgrad, places, pulled, out, grads,
                      stage, inbox, right_out, right_in, left_out, left_in, w_got, pieces, near_got, far_sent, far_got,
                      send, recv, rs, rr, ls, lr, o_s, o_r, w_s, w_r, a_s, a_r, b_s, b_r, c_s, c_r, d_s, d_r, loc):
    q, g = lax.axis_index("dom"), lax.axis_index("grp")
    layers, near, slots, own, fw = stage.shape
    n_blk = pulled.shape[0]
    cut = n_blk // 2
    half = layers // 2
    z, k = q // near, q % near
    out_rows, live, _, _ = tables(layers * near, slots, 0)
    barrier = pltpu.get_barrier_semaphore()
    signal_group(q, g, n_grp)(barrier)
    signal_ring(q, g, near, layers)(barrier)
    mine = pl.ds(pl.multiple_of(g * own, own), own)
    keep = pltpu.make_async_copy(out_all.at[g], out.at[:, mine], loc)
    keep.start()
    far, grad_far = [], []
    for r in range(1, n_grp):
        y = (g + r) % n_grp
        to = dict(device_id=(q, y), device_id_type=MESH)
        far.append(pltpu.make_async_remote_copy(
            src_ref=out_all.at[y], dst_ref=out.at[:, mine], send_sem=o_s.at[r - 1], recv_sem=o_r.at[r - 1], **to))
        grad_far.append(pltpu.make_async_remote_copy(
            src_ref=wgrad.at[y], dst_ref=w_got.at[r - 1], send_sem=w_s.at[r - 1], recv_sem=w_r.at[r - 1], **to))

    def to_near(d, r):
        to = (k + r) % near
        return pltpu.make_async_remote_copy(
            src_ref=stage.at[d, to], dst_ref=inbox.at[d, k], send_sem=send.at[d, r], recv_sem=recv.at[d, r],
            device_id=(z * near + to, g), device_id_type=MESH)

    def own_term(d):
        return pltpu.make_async_copy(stage.at[d, k], inbox.at[d, k], recv.at[d, 0])

    def products(d):
        base = (z + d) % layers * near

        @pl.loop(0, near)
        def _(r):
            to = (k + r) % near
            for s in range(slots):
                n = (base + to) * slots + s
                value = jnp.dot(cols[n], scaled[table[out_rows + n]], preferred_element_type=F32)
                stage[d, to, s] = jnp.where(s < table[live + base + to], value, 0.0).astype(BF16)

    def ship(d):
        own_term(d).start()
        each(1, near, functools.partial(to_near, d), start)

    def reduce(d):
        own_term(d).wait()
        each(1, near, functools.partial(to_near, d), wait)
        n = near * slots * own
        spot = places[(z + d) % layers]
        row = lax.broadcasted_iota(jnp.int32, (n_blk * own, 128), 0)
        hot = [jnp.where(row == spot[c:c + 1], 1.0, 0.0).astype(BF16) for c in range(pl.cdiv(n, 128))]
        hot = jnp.concatenate(hot, axis=1)[:, :n] if len(hot) > 1 else hot[0][:, :n]
        terms = inbox[d].reshape(n, fw)
        return jnp.dot(hot, terms, preferred_element_type=F32).reshape(n_blk, own, fw)

    def ring(i, to_right):
        count = cut if i == 0 else n_blk
        held, lands, s_sem, r_sem, step = (right_out, right_in, rs, rr, 1) if to_right else (left_out, left_in, ls, lr, layers - 1)
        return pltpu.make_async_remote_copy(
            src_ref=held.at[i, pl.ds(0, count)], dst_ref=lands.at[i, pl.ds(0, count)], send_sem=s_sem.at[i], recv_sem=r_sem.at[i],
            device_id=((z + step) % layers * near + k, g), device_id_type=MESH)

    def with_right(i, value):
        ring(i, True).wait()
        if i == 0:
            return jnp.concatenate([value[:cut] + right_in[0, :cut].astype(F32), value[cut:]], axis=0)
        return value + right_in[i].astype(F32)

    def with_left(i, value):
        ring(i, False).wait()
        if i == 0:
            return jnp.concatenate([value[:cut], value[cut:] + left_in[0, :cut].astype(F32)], axis=0)
        return value + left_in[i].astype(F32)

    def near_reduce(r):
        to = (k + r) % near
        return pltpu.make_async_remote_copy(
            src_ref=pieces.at[pl.ds(to * layers, layers)], dst_ref=near_got.at[r],
            send_sem=a_s.at[r], recv_sem=a_r.at[r], device_id=(z * near + to, g), device_id_type=MESH)

    def far_reduce(r):
        to = (z + r) % layers
        return pltpu.make_async_remote_copy(
            src_ref=far_sent.at[to], dst_ref=far_got.at[r],
            send_sem=b_s.at[r], recv_sem=b_r.at[r], device_id=(to * near + k, g), device_id_type=MESH)

    def far_gather(r):
        to = (z + r) % layers
        return pltpu.make_async_remote_copy(
            src_ref=grads.at[k * layers + z], dst_ref=grads.at[k * layers + z],
            send_sem=c_s.at[r], recv_sem=c_r.at[r], device_id=(to * near + k, g), device_id_type=MESH)

    def near_gather(r):
        to = (k + r) % near
        return pltpu.make_async_remote_copy(
            src_ref=grads.at[pl.ds(k * layers, layers)], dst_ref=grads.at[pl.ds(k * layers, layers)],
            send_sem=d_s.at[r], recv_sem=d_r.at[r], device_id=(z * near + to, g), device_id_type=MESH)

    def sum_grp():
        for c in grad_far:
            c.wait()
        halves = wgrad.shape[1]
        per = pieces.shape[0] // halves
        for h in range(halves):
            total = wgrad[g, h].astype(F32)
            for r in range(n_grp - 1):
                total = total + w_got[r, h].astype(F32)
            pieces[h * per:(h + 1) * per] = total.reshape(per, pieces.shape[1], 128)
        each(1, near, near_reduce, start)

    def sum_near():
        each(1, near, near_reduce, wait)
        total = pieces[pl.ds(k * layers, layers)]
        for r in range(1, near):
            total = total + near_got[r]
        far_sent[...] = total
        each(1, layers, far_reduce, start)

    def sum_far():
        each(1, layers, far_reduce, wait)
        total = far_sent[z]
        for r in range(1, layers):
            total = total + far_got[r]
        grads[k * layers + z] = total
        each(1, layers, far_gather, start)

    def spread():
        each(1, layers, far_gather, wait)
        each(1, near, near_gather, start)

    chain = [sum_grp, sum_near, sum_far, spread]
    products(half)
    pl.semaphore_wait(barrier, n_grp - 1 + near - 1 + layers - 1)
    for c in grad_far:
        c.start()
    ship(half)
    for c in far:
        c.start()
    for i in range(half):
        d = half - i
        if d > 1:
            for e in (d - 1, layers - d + 1):
                products(e)
                ship(e)
        else:
            products(0)
            ship(0)
        if i == 0:
            value = reduce(half)
            right_out[0, :cut] = value[:cut].astype(BF16)
            left_out[0, :cut] = value[cut:].astype(BF16)
        else:
            right_out[i] = with_right(i - 1, reduce(d)).astype(BF16)
            left_out[i] = with_left(i - 1, reduce(layers - d)).astype(BF16)
        ring(i, True).start()
        ring(i, False).start()
        if chain:
            chain.pop(0)()
    value = reduce(0)
    value = with_right(half - 1, value)
    pulled[...] = with_left(half - 1, value)
    while chain:
        chain.pop(0)()
    each(1, near, near_gather, wait)
    keep.wait()
    for c in far:
        c.wait()


def pull_kernel(table, scaled, cols, outer_sum, base, out_parts, part, out, acc, sem_o, *, n_out, where):
    keep = pltpu.make_async_copy(out_parts, out, sem_o)
    keep.start()
    in_rows, in_cols = where
    acc[...] = outer_sum[...] + base[...]

    @pl.loop(0, cols.shape[0] - n_out)
    def _(n):
        acc[table[in_cols + n]] += jnp.dot(cols[n_out + n], scaled[table[in_rows + n]], preferred_element_type=F32)

    part[...] = acc[...].astype(BF16)
    keep.wait()


def finish_kernel(n_grp, part, whole, s2, r2):
    q, g = lax.axis_index("dom"), lax.axis_index("grp")
    own = part.shape[1]
    mine = pl.ds(pl.multiple_of(g * own, own), own)
    barrier = pltpu.get_barrier_semaphore()
    signal_group(q, g, n_grp)(barrier)
    pl.semaphore_wait(barrier, n_grp - 1)
    last = []
    for r in range(1, n_grp):
        last.append(pltpu.make_async_remote_copy(
            src_ref=part, dst_ref=whole.at[:, mine], send_sem=s2.at[r - 1], recv_sem=r2.at[r - 1],
            device_id=(q, (g + r) % n_grp), device_id_type=MESH))
    for c in last:
        c.start()
    whole[:, mine] = part[...]
    for c in last:
        c.wait()


def params(collective=None, vmem=48):
    if collective is None:
        return pltpu.CompilerParams(vmem_limit_bytes=vmem << 20)
    return pltpu.CompilerParams(vmem_limit_bytes=vmem << 20, collective_id=collective, has_side_effects=True)


def shards(features, w_self, w_neigh, cotangent, inner_rows, inner_cols, inner_values, send_blocks, outer_rows, outer_values, live_count):
    blk = inner_values.shape[-1]
    nodes, fw = features.shape
    n_blk = nodes // blk
    parts, n_grp = lax.axis_size("dom"), lax.axis_size("grp")
    x = x_extent(parts)
    near = 2 * x
    layers = parts // near
    n_src = parts // n_grp
    slots = send_blocks.shape[-1]
    hid = w_self.shape[1]
    own = blk // n_grp
    n_in, n_out = inner_values.shape[1], outer_values.shape[1]
    n_all = n_in + n_out
    inner, outer = inner_values[0], outer_values[0]
    table = jnp.concatenate([send_blocks.reshape(-1), outer_rows[0], live_count[0], inner_rows[0], inner_cols[0]])
    dead = jnp.tile(jnp.arange(slots, dtype=jnp.int32), parts) >= jnp.repeat(live_count[0], slots)
    keys = jnp.concatenate([jnp.where(dead, n_blk, outer_rows[0]), inner_rows[0]])[None]
    places = (send_blocks.reshape(layers, near * slots, 1) * own + jnp.arange(own, dtype=jnp.int32)).reshape(layers, -1)
    places = jnp.pad(places, ((0, 0), (0, 8 * 128 - places.shape[1]))).reshape(layers, 8, 128)
    feat = features.reshape(n_blk, blk, fw)
    dma, sds = pltpu.SemaphoreType.DMA, jax.ShapeDtypeStruct
    vm = pltpu.VMEM
    block = (n_src, slots, blk, fw)
    mine = (n_blk, own, fw)
    y_sem = dma((n_grp - 1,))

    inc, cot_all, w_all, place_all, cols, divisor = pl.pallas_call(
        functools.partial(forward_exchange, x, n_src, n_grp),
        out_shape=(sds(block, BF16), sds((n_grp, n_blk, own, hid), BF16), sds((n_grp, 2 * fw, hid), BF16), sds((layers, 8, 128), jnp.int32),
                   sds((n_all, own, blk), BF16), sds(mine, F32)),
        in_specs=[SM, VM, HB, HB, HB, HB, HB, HB, HB],
        out_specs=(ANY, ANY, ANY, ANY, VM, VM),
        scratch_shapes=[vm((n_blk, blk, fw), BF16), vm(block, BF16), vm((n_all, blk, blk), BF16), vm((n_all, blk), F32),
                        dma((n_src,)), dma((n_src,)), y_sem, y_sem, dma((n_grp - 1, 2)), dma((n_grp - 1, 2)),
                        dma((layers,)), dma((layers,)), dma((7,))],
        compiler_params=params(0), name="forward_exchange",
    )(table, keys, places, feat, cotangent.reshape(n_blk, blk, hid), w_self, w_neigh, inner, outer)

    part = pl.pallas_call(
        functools.partial(aggregate_kernel, x, n_src, n_grp),
        out_shape=sds((n_blk, blk, fw), BF16),
        in_specs=[SM, HB, ANY, HB, HB],
        out_specs=VM,
        scratch_shapes=[vm((n_blk, blk, fw), BF16), vm((n_blk, blk, fw), F32), vm((n_in // n_grp, blk, blk), BF16),
                        vm((n_src, slots, blk, blk), BF16), vm(block, BF16), dma, dma, dma, dma],
        compiler_params=params(), name="aggregate",
    )(table, feat, inc, inner, outer)

    halves = hid // 128
    out_all, scaled, base, wgrad = pl.pallas_call(
        functools.partial(dense_kernel, n_grp),
        out_shape=(sds((n_grp, n_blk, own, hid), BF16), sds((n_blk, blk, fw), BF16), sds(mine, F32), sds((n_grp, halves, 2 * fw, 128), BF16)),
        in_specs=[VM, HB, VM, ANY, ANY],
        out_specs=(VM,) * 4,
        scratch_shapes=[vm(mine, BF16), vm((n_grp, n_blk, own, hid), BF16), vm((n_grp, 2 * fw, hid), BF16),
                        vm((n_grp - 1,) + mine, BF16), vm(mine, BF16), y_sem, y_sem, y_sem, y_sem, dma((3,))],
        compiler_params=params(1), name="dense",
    )(part, feat, divisor, cot_all, w_all)

    depth = halves * 2 * fw // parts
    half = layers // 2
    near_sem, far_sem = dma((near,)), dma((layers,))
    outer_sum, out_parts, grads = pl.pallas_call(
        functools.partial(backward_exchange, x, n_grp),
        out_shape=(sds(mine, F32), sds((n_blk, blk, hid), BF16), sds((parts, depth, 128), F32)),
        in_specs=[SM, VM, VM, ANY, VM, VM],
        out_specs=(VM, ANY, VM),
        scratch_shapes=[vm((layers, near, slots, own, fw), BF16), vm((layers, near, slots, own, fw), BF16)]
        + [vm((half,) + mine, BF16)] * 4
        + [vm((n_grp - 1, halves, 2 * fw, 128), BF16), vm((parts, depth, 128), F32), vm((near, layers, depth, 128), F32),
           vm((layers, depth, 128), F32), vm((layers, depth, 128), F32)]
        + [dma((layers, near))] * 2 + [dma((half,))] * 4 + [y_sem] * 4
        + [near_sem] * 2 + [far_sem] * 4 + [near_sem] * 2 + [dma],
        compiler_params=params(2), name="backward_exchange",
    )(table, scaled, cols, out_all, wgrad, place_all)

    _, _, in_rows, in_cols = tables(parts, slots, n_in)
    pulled, layer_out = pl.pallas_call(
        functools.partial(pull_kernel, n_out=n_out, where=(in_rows, in_cols)),
        out_shape=(sds(mine, BF16), sds((n_blk, blk, hid), BF16)),
        in_specs=[SM, VM, VM, VM, VM, ANY],
        out_specs=(VM, ANY),
        scratch_shapes=[vm(mine, F32), dma],
        compiler_params=params(), name="pull",
    )(table, scaled, cols, outer_sum, base, out_parts)

    whole = pl.pallas_call(
        functools.partial(finish_kernel, n_grp),
        out_shape=sds((n_blk, blk, fw), BF16),
        in_specs=[VM],
        out_specs=VM,
        scratch_shapes=[y_sem, y_sem],
        compiler_params=params(3), name="finish",
    )(pulled)
    grads = grads.reshape(halves, 2 * fw, 128)
    grads = jnp.concatenate([grads[h] for h in range(halves)], axis=1)
    return layer_out.reshape(nodes, hid), whole.astype(F32).reshape(nodes, fw), grads[:fw], grads[fw:]


def solution(mesh):
    placed = (
        P("dom", None),
        P(None, "grp"),
        P(None, "grp"),
        P("dom", "grp"),
        P("dom", None),
        P("dom", None),
        P("dom", None, None, None),
        P("dom", None, None),
        P("dom", None),
        P("dom", None, None, None),
        P("dom", None),
    )
    return jax.shard_map(
        shards,
        mesh=mesh,
        in_specs=placed,
        out_specs=(P("dom", "grp"), P("dom", None), P(None, "grp"), P(None, "grp")),
        check_vma=False,
    )
```

```python
import functools

import jax
import jax.numpy as jnp
from jax import lax
from jax.experimental import pallas as pl
from jax.experimental.pallas import tpu as pltpu
from jax.sharding import PartitionSpec as P

MESH = pl.DeviceIdType.MESH
ANY = pl.BlockSpec(memory_space=pl.ANY)
VM = pl.BlockSpec(memory_space=pltpu.VMEM)
SM = pl.BlockSpec(memory_space=pltpu.SMEM)
HB = pl.BlockSpec(memory_space=pltpu.HBM)
F32 = jnp.float32
BF16 = jnp.bfloat16
TRANS_A = (((0,), (0,)), ((), ()))
TRANS_B = (((1,), (1,)), ((), ()))


def x_extent(parts):
    return 4 if parts == 64 else 1


def plane_peer(i, q, g, x):
    z = q // (2 * x)
    return (((i // x) * 2 + (z + g // 2) % 2) * x + i % x) * 2 + (q + g) % 2


def plane_slot(q, x):
    return (q // (4 * x)) * x + (q // 2) % x


def enter(peers, count):
    barrier = pltpu.get_barrier_semaphore()
    for peer in peers:
        peer(barrier)
    pl.semaphore_wait(barrier, count)


def signal_plane(q, g, x, n_src):
    slot = plane_slot(q, x)

    def go(barrier):
        @pl.when(g != 0)
        def _():
            pl.semaphore_signal(barrier, inc=1, device_id=(plane_peer(slot, q, g, x), g), device_id_type=MESH)

        @pl.loop(1, n_src)
        def _(i):
            peer = plane_peer((slot + i) % n_src, q, g, x)
            pl.semaphore_signal(barrier, inc=1, device_id=(peer, g), device_id_type=MESH)

    return go


def signal_group(q, g, n_grp):
    def go(barrier):
        for r in range(1, n_grp):
            pl.semaphore_signal(barrier, inc=1, device_id=(q, (g + r) % n_grp), device_id_type=MESH)

    return go


def tables(parts, slots, n_inner):
    out_rows = parts * slots
    live = 2 * parts * slots
    return out_rows, live, live + parts, live + parts + n_inner


def signal_ring(q, g, near, layers):
    z, k = q // near, q % near

    def go(barrier):
        @pl.loop(1, near)
        def _(r):
            pl.semaphore_signal(barrier, inc=1, device_id=(z * near + (k + r) % near, g), device_id_type=MESH)

        @pl.loop(1, layers)
        def _(r):
            pl.semaphore_signal(barrier, inc=1, device_id=((z + r) % layers * near + k, g), device_id_type=MESH)

    return go


def each(first, count, make, act):
    @pl.loop(first, count)
    def _(r):
        act(make(r))


def start(c):
    c.start()


def wait(c):
    c.wait()


def forward_exchange(x, n_src, n_grp, table, rows_out, rows_in, live, features, cot, w_self, w_neigh, inner, outer,
                     inc, cot_all, w_all, place_all, cols_out, divisor_out,
                     feat, stage, blocks, row_sums, places, key_out, key_in, key_live, cols, divisor, send, recv, cot_s, cot_r, w_s, w_r, p_s, p_r, loc):
    q, g = lax.axis_index("dom"), lax.axis_index("grp")
    slots = stage.shape[1]
    own = cot_all.shape[2]
    fw = w_self.shape[0]
    n_blk, blk, _ = feat.shape
    near = 2 * x
    layers = place_all.shape[0]
    z, k = q // near, q % near
    slot = plane_slot(q, x)
    n_out, n_in = outer.shape[0], inner.shape[0]
    barrier = pltpu.get_barrier_semaphore()
    load_feat = pltpu.make_async_copy(features, feat, loc.at[3])
    load_feat.start()
    signal_plane(q, g, x, n_src)(barrier)
    signal_group(q, g, n_grp)(barrier)

    @pl.loop(1, layers)
    def _(r):
        pl.semaphore_signal(barrier, inc=1, device_id=((z + r) % layers * near + k, g), device_id_type=MESH)

    mine = pl.ds(pl.multiple_of(g * own, own), own)
    local = [
        pltpu.make_async_copy(cot.at[:, mine], cot_all.at[g], loc.at[0]),
        pltpu.make_async_copy(w_self, w_all.at[g, pl.ds(0, fw)], loc.at[1]),
        pltpu.make_async_copy(w_neigh, w_all.at[g, pl.ds(fw, fw)], loc.at[2]),
        pltpu.make_async_copy(places.at[z], place_all.at[z], loc.at[6]),
    ]
    small = [
        pltpu.make_async_copy(rows_out, key_out, loc.at[7]),
        pltpu.make_async_copy(rows_in, key_in, loc.at[8]),
        pltpu.make_async_copy(live, key_live, loc.at[9]),
    ]
    loads = [
        pltpu.make_async_copy(outer, blocks.at[pl.ds(0, n_out)], loc.at[4]),
        pltpu.make_async_copy(inner, blocks.at[pl.ds(n_out, n_in)], loc.at[5]),
    ]

    def fill(d):
        peer = plane_peer(d, q, g, x)
        for s in range(slots):
            stage[d, s] = feat[table[peer * slots + s]]
        return peer

    def remote(d, peer):
        return pltpu.make_async_remote_copy(
            src_ref=stage.at[d], dst_ref=inc.at[slot], send_sem=send.at[d], recv_sem=recv.at[slot],
            device_id=(peer, g), device_id_type=MESH)

    def place(r):
        to = (z + r) % layers
        return pltpu.make_async_remote_copy(
            src_ref=places.at[to], dst_ref=place_all.at[z], send_sem=p_s.at[r], recv_sem=p_r.at[r],
            device_id=(to * near + k, g), device_id_type=MESH)

    load_feat.wait()
    home = fill(slot)
    others = n_grp - 1 + layers - 1

    @pl.when(g == 0)
    def _():
        pl.semaphore_wait(barrier, n_src - 1 + others)

    @pl.when(g != 0)
    def _():
        pl.semaphore_wait(barrier, n_src + others)

    far = []
    for r in range(1, n_grp):
        y = (g + r) % n_grp
        to = dict(device_id=(q, y), device_id_type=MESH)
        theirs = pl.ds(pl.multiple_of(y * own, own), own)
        far.append(pltpu.make_async_remote_copy(
            src_ref=cot.at[:, theirs], dst_ref=cot_all.at[g],
            send_sem=cot_s.at[r - 1], recv_sem=cot_r.at[r - 1], **to))
        far.append(pltpu.make_async_remote_copy(
            src_ref=w_self, dst_ref=w_all.at[g, pl.ds(0, fw)],
            send_sem=w_s.at[r - 1, 0], recv_sem=w_r.at[r - 1, 0], **to))
        far.append(pltpu.make_async_remote_copy(
            src_ref=w_neigh, dst_ref=w_all.at[g, pl.ds(fw, fw)],
            send_sem=w_s.at[r - 1, 1], recv_sem=w_r.at[r - 1, 1], **to))

    @pl.when(g == 0)
    def _():
        pltpu.make_async_copy(stage.at[slot], inc.at[slot], recv.at[slot]).start()

    @pl.when(g != 0)
    def _():
        remote(slot, home).start()

    @pl.loop(1, n_src)
    def _(i):
        d = (slot + i) % n_src
        remote(d, fill(d)).start()

    for c in far + local[:3] + loads + small:
        c.start()

    per = 128 // own
    lane = lax.broadcasted_iota(jnp.int32, (1, 128), 1)

    @pl.loop(0, layers)
    def _(t):
        for c in range(pl.cdiv(near * slots, per)):
            spot = lane
            for u in range(per):
                if c * per + u < near * slots:
                    target = table[t * (near * slots) + c * per + u]
                    spot = jnp.where(lane // own == u, lane + (target - u) * own, spot)
            places[t, c:c + 1, :] = spot

    local[3].start()
    each(1, layers, place, start)

    row = lax.broadcasted_iota(jnp.int32, (own + 16, blk), 0)
    lane = lax.broadcasted_iota(jnp.int32, (own + 16, blk), 1)
    pick = jnp.where((row == own) | (lane == row + g * own) & (row < own), 1.0, 0.0).astype(BF16)
    for c in loads:
        c.wait()

    @pl.loop(0, (n_out + n_in) // 8)
    def _(m):
        got = [lax.dot_general(pick, blocks[m * 8 + u], TRANS_B, preferred_element_type=F32) for u in range(8)]
        for u in range(8):
            cols[m * 8 + u] = got[u][:own].astype(BF16)
        row_sums[pl.ds(pl.multiple_of(m * 8, 8), 8), :] = jnp.concatenate([v[own:own + 1] for v in got], axis=0)

    keep = pltpu.make_async_copy(cols, cols_out, loc.at[10])
    keep.start()
    for c in small:
        c.wait()
    n_part = key_live.shape[1]
    first = slots * lax.broadcasted_iota(jnp.int32, (n_part, n_out), 0)
    at = lax.broadcasted_iota(jnp.int32, (n_part, n_out), 1) - first
    spread = jnp.where((at >= 0) & (at < slots), 1.0, 0.0)
    limit = jnp.dot(key_live[...].astype(F32), spread, precision=lax.Precision.HIGHEST, preferred_element_type=F32)
    index = jnp.sum(jnp.where((at >= 0) & (at < slots), at, 0), axis=0, keepdims=True)
    key = jnp.concatenate([jnp.where(index.astype(F32) < limit, key_out[...], n_blk), key_in[...]], axis=1)
    hits = jnp.where(lax.broadcasted_iota(jnp.int32, (n_blk, n_out + n_in), 0) == key, 1.0, 0.0)
    degree = 1.0 + jnp.dot(hits, row_sums[...], precision=lax.Precision.HIGHEST, preferred_element_type=F32)
    sel = (lax.broadcasted_iota(jnp.int32, (own, blk), 1) == lax.broadcasted_iota(jnp.int32, (own, blk), 0) + g * own)
    for b in range(n_blk):
        column = jnp.sum(jnp.where(sel, degree[b:b + 1], 0.0), axis=1, keepdims=True)
        divisor[b] = jnp.broadcast_to(column, (own, fw))

    keep_too = pltpu.make_async_copy(divisor, divisor_out, loc.at[11])
    keep_too.start()
    keep.wait()
    keep_too.wait()
    for c in local:
        c.wait()
    for c in far:
        c.wait()
    each(1, layers, place, wait)

    @pl.when(g != 0)
    def _():
        remote(slot, home).wait_send()

    @pl.loop(1, n_src)
    def _(i):
        d = (slot + i) % n_src
        remote(d, plane_peer(d, q, g, x)).wait_send()

    @pl.loop(0, n_src)
    def _(j):
        pltpu.make_async_copy(stage.at[j], inc.at[j], recv.at[j]).wait()


def aggregate_kernel(x, n_src, n_grp, table, features, inc, inner, outer, part, feat, acc, a_in, a_out, x_in, sem_f, sem_in, sem_out, sem_x):
    q, g = lax.axis_index("dom"), lax.axis_index("grp")
    slots = inc.shape[1]
    n_in = inner.shape[0] // n_grp
    out_rows, live, in_rows, in_cols = tables(n_grp * n_src, slots, inner.shape[0])
    load_f = pltpu.make_async_copy(features, feat, sem_f)
    load_f.start()
    load_in = pltpu.make_async_copy(inner.at[pl.ds(g * n_in, n_in)], a_in, sem_in)
    load_in.start()
    load_x = pltpu.make_async_copy(inc, x_in, sem_x)
    load_x.start()

    def load(i):
        peer = plane_peer(i, q, g, x)
        return pltpu.make_async_copy(outer.at[pl.ds(peer * slots, slots)], a_out.at[i], sem_out)

    @pl.loop(0, n_src)
    def _(i):
        load(i).start()

    acc[...] = jnp.zeros_like(acc)
    load_f.wait()
    load_in.wait()

    @pl.loop(0, n_in // 2)
    def _(m):
        value = [jnp.dot(a_in[m * 2 + u], feat[table[in_cols + g * n_in + m * 2 + u]], preferred_element_type=F32) for u in range(2)]
        for u in range(2):
            acc[table[in_rows + g * n_in + m * 2 + u]] += value[u]

    load_x.wait()
    pltpu.make_async_copy(a_out, a_out, sem_out).wait()

    @pl.loop(0, n_src)
    def _(i):
        peer = plane_peer(i, q, g, x)
        value = [jnp.dot(a_out[i, s], x_in[i, s], preferred_element_type=F32) for s in range(slots)]
        for s in range(slots):
            @pl.when(s < table[live + peer])
            def _(s=s):
                acc[table[out_rows + peer * slots + s]] += value[s]

    part[...] = acc[...].astype(BF16)


def dense_kernel(n_grp, part, features, divisor, cots, ws, out_all, scaled, base, wgrad, feat, cot_all, w_all, got, sent, s1, r1, s3, r3, loc):
    q, g = lax.axis_index("dom"), lax.axis_index("grp")
    n_blk, blk, fw = part.shape
    own = base.shape[1]
    rows, hid = n_blk * own, ws.shape[2]
    mine = pl.ds(pl.multiple_of(g * own, own), own)
    barrier = pltpu.get_barrier_semaphore()
    signal_group(q, g, n_grp)(barrier)
    loads = [
        pltpu.make_async_copy(features.at[:, mine], feat, loc.at[0]),
        pltpu.make_async_copy(ws, w_all, loc.at[1]),
        pltpu.make_async_copy(cots, cot_all, loc.at[2]),
    ]
    for c in loads:
        c.start()
    pl.semaphore_wait(barrier, n_grp - 1)
    copies, last = [], []
    for r in range(1, n_grp):
        y = (g + r) % n_grp
        to = dict(device_id=(q, y), device_id_type=MESH)
        theirs = pl.ds(pl.multiple_of(y * own, own), own)
        copies.append(pltpu.make_async_remote_copy(
            src_ref=part.at[:, theirs], dst_ref=got.at[r - 1], send_sem=s1.at[r - 1], recv_sem=r1.at[r - 1], **to))
        last.append(pltpu.make_async_remote_copy(
            src_ref=sent, dst_ref=scaled.at[:, mine], send_sem=s3.at[r - 1], recv_sem=r3.at[r - 1], **to))
    for c in copies:
        c.start()
    for c in loads:
        c.wait()
    for c in copies:
        c.wait()
    own_feat = feat[...]
    total = own_feat.astype(F32) + part[:, mine].astype(F32)
    for r in range(n_grp - 1):
        total = total + got[r].astype(F32)
    agg = (total / divisor[...]).astype(BF16)
    both = jnp.concatenate([own_feat.reshape(rows, fw), agg.reshape(rows, fw)], axis=1)
    back = jnp.zeros((rows, 2 * fw), F32)
    grads = []
    for j in range(n_grp):
        pre = jnp.dot(both, w_all[j], preferred_element_type=F32)
        sig = jax.nn.sigmoid(pre)
        out_all[j] = (pre * sig).astype(BF16).reshape(n_blk, own, hid)
        cot = cot_all[j].reshape(rows, hid).astype(F32)
        grad = (cot * sig * (1.0 + pre * (1.0 - sig))).astype(BF16)
        grads.append(grad)
        back = back + lax.dot_general(grad, w_all[j], TRANS_B, preferred_element_type=F32)
    down = (back[:, fw:].reshape(n_blk, own, fw) / divisor[...]).astype(BF16)
    sent[...] = down
    for c in last:
        c.start()
    scaled[:, mine] = down
    base[...] = back[:, :fw].reshape(n_blk, own, fw) + down.astype(F32)
    for j in range(n_grp):
        gw = lax.dot_general(both, grads[j], TRANS_A, preferred_element_type=F32).astype(BF16)
        for h in range(hid // 128):
            wgrad[j, h] = gw[:, 128 * h:128 * (h + 1)]
    for c in last:
        c.wait()


def backward_exchange(x, n_grp, table, scaled, cols, out_all, wgrad, places, pulled, out, grads,
                      stage, inbox, right_out, right_in, left_out, left_in, w_got, pieces, near_got, far_sent, far_got,
                      send, recv, rs, rr, ls, lr, o_s, o_r, w_s, w_r, a_s, a_r, b_s, b_r, c_s, c_r, d_s, d_r, loc):
    q, g = lax.axis_index("dom"), lax.axis_index("grp")
    layers, near, slots, own, fw = stage.shape
    n_blk = pulled.shape[0]
    cut = n_blk // 2
    half = layers // 2
    z, k = q // near, q % near
    out_rows, live, _, _ = tables(layers * near, slots, 0)
    barrier = pltpu.get_barrier_semaphore()
    signal_group(q, g, n_grp)(barrier)
    signal_ring(q, g, near, layers)(barrier)
    mine = pl.ds(pl.multiple_of(g * own, own), own)
    keep = pltpu.make_async_copy(out_all.at[g], out.at[:, mine], loc)
    keep.start()
    far, grad_far = [], []
    for r in range(1, n_grp):
        y = (g + r) % n_grp
        to = dict(device_id=(q, y), device_id_type=MESH)
        far.append(pltpu.make_async_remote_copy(
            src_ref=out_all.at[y], dst_ref=out.at[:, mine], send_sem=o_s.at[r - 1], recv_sem=o_r.at[r - 1], **to))
        grad_far.append(pltpu.make_async_remote_copy(
            src_ref=wgrad.at[y], dst_ref=w_got.at[r - 1], send_sem=w_s.at[r - 1], recv_sem=w_r.at[r - 1], **to))

    def to_near(d, r):
        to = (k + r) % near
        return pltpu.make_async_remote_copy(
            src_ref=stage.at[d, to], dst_ref=inbox.at[d, k], send_sem=send.at[d, r], recv_sem=recv.at[d, r],
            device_id=(z * near + to, g), device_id_type=MESH)

    def own_term(d):
        return pltpu.make_async_copy(stage.at[d, k], inbox.at[d, k], recv.at[d, 0])

    def products(d):
        base = (z + d) % layers * near

        group = max(1, near // 2)

        @pl.loop(0, near // group)
        def _(r):
            value = []
            for u in range(group):
                for s in range(slots):
                    n = (base + r * group + u) * slots + s
                    value.append(jnp.dot(cols[n], scaled[table[out_rows + n]], preferred_element_type=F32))
            for u in range(group):
                to = r * group + u
                for s in range(slots):
                    stage[d, to, s] = jnp.where(s < table[live + base + to], value[u * slots + s], 0.0).astype(BF16)

    def ship(d):
        own_term(d).start()
        each(1, near, functools.partial(to_near, d), start)

    def reduce(d):
        own_term(d).wait()
        each(1, near, functools.partial(to_near, d), wait)
        n = near * slots * own
        spot = places[(z + d) % layers]
        row = lax.broadcasted_iota(jnp.int32, (n_blk * own, 128), 0)
        hot = [jnp.where(row == spot[c:c + 1], 1.0, 0.0).astype(BF16) for c in range(pl.cdiv(n, 128))]
        hot = jnp.concatenate(hot, axis=1)[:, :n] if len(hot) > 1 else hot[0][:, :n]
        terms = inbox[d].reshape(n, fw)
        return jnp.dot(hot, terms, preferred_element_type=F32).reshape(n_blk, own, fw)

    def ring(i, to_right):
        count = cut if i == 0 else n_blk
        held, lands, s_sem, r_sem, step = (right_out, right_in, rs, rr, 1) if to_right else (left_out, left_in, ls, lr, layers - 1)
        return pltpu.make_async_remote_copy(
            src_ref=held.at[i, pl.ds(0, count)], dst_ref=lands.at[i, pl.ds(0, count)], send_sem=s_sem.at[i], recv_sem=r_sem.at[i],
            device_id=((z + step) % layers * near + k, g), device_id_type=MESH)

    def with_right(i, value):
        ring(i, True).wait()
        if i == 0:
            return jnp.concatenate([value[:cut] + right_in[0, :cut].astype(F32), value[cut:]], axis=0)
        return value + right_in[i].astype(F32)

    def with_left(i, value):
        ring(i, False).wait()
        if i == 0:
            return jnp.concatenate([value[:cut], value[cut:] + left_in[0, :cut].astype(F32)], axis=0)
        return value + left_in[i].astype(F32)

    def near_reduce(r):
        to = (k + r) % near
        return pltpu.make_async_remote_copy(
            src_ref=pieces.at[pl.ds(to * layers, layers)], dst_ref=near_got.at[r],
            send_sem=a_s.at[r], recv_sem=a_r.at[r], device_id=(z * near + to, g), device_id_type=MESH)

    def far_reduce(r):
        to = (z + r) % layers
        return pltpu.make_async_remote_copy(
            src_ref=far_sent.at[to], dst_ref=far_got.at[r],
            send_sem=b_s.at[r], recv_sem=b_r.at[r], device_id=(to * near + k, g), device_id_type=MESH)

    def far_gather(r):
        to = (z + r) % layers
        return pltpu.make_async_remote_copy(
            src_ref=grads.at[k * layers + z], dst_ref=grads.at[k * layers + z],
            send_sem=c_s.at[r], recv_sem=c_r.at[r], device_id=(to * near + k, g), device_id_type=MESH)

    def near_gather(r):
        to = (k + r) % near
        return pltpu.make_async_remote_copy(
            src_ref=grads.at[pl.ds(k * layers, layers)], dst_ref=grads.at[pl.ds(k * layers, layers)],
            send_sem=d_s.at[r], recv_sem=d_r.at[r], device_id=(z * near + to, g), device_id_type=MESH)

    def sum_grp():
        for c in grad_far:
            c.wait()
        halves = wgrad.shape[1]
        per = pieces.shape[0] // halves
        for h in range(halves):
            total = wgrad[g, h].astype(F32)
            for r in range(n_grp - 1):
                total = total + w_got[r, h].astype(F32)
            pieces[h * per:(h + 1) * per] = total.reshape(per, pieces.shape[1], 128)
        each(1, near, near_reduce, start)

    def sum_near():
        each(1, near, near_reduce, wait)
        total = pieces[pl.ds(k * layers, layers)]
        for r in range(1, near):
            total = total + near_got[r]
        far_sent[...] = total
        each(1, layers, far_reduce, start)

    def sum_far():
        each(1, layers, far_reduce, wait)
        total = far_sent[z]
        for r in range(1, layers):
            total = total + far_got[r]
        grads[k * layers + z] = total
        each(1, layers, far_gather, start)

    def spread():
        each(1, layers, far_gather, wait)
        each(1, near, near_gather, start)

    chain = [sum_grp, sum_near, sum_far, spread]
    products(half)
    pl.semaphore_wait(barrier, n_grp - 1 + near - 1 + layers - 1)
    for c in grad_far:
        c.start()
    ship(half)
    for c in far:
        c.start()
    for i in range(half):
        d = half - i
        if d > 1:
            for e in (d - 1, layers - d + 1):
                products(e)
                ship(e)
        else:
            products(0)
            ship(0)
        if i == 0:
            value = reduce(half)
            right_out[0, :cut] = value[:cut].astype(BF16)
            left_out[0, :cut] = value[cut:].astype(BF16)
        else:
            right_out[i] = with_right(i - 1, reduce(d)).astype(BF16)
            left_out[i] = with_left(i - 1, reduce(layers - d)).astype(BF16)
        ring(i, True).start()
        ring(i, False).start()
        if chain:
            chain.pop(0)()
    value = reduce(0)
    value = with_right(half - 1, value)
    pulled[...] = with_left(half - 1, value)
    while chain:
        chain.pop(0)()
    each(1, near, near_gather, wait)
    keep.wait()
    for c in far:
        c.wait()


def pull_kernel(table, scaled, cols, outer_sum, base, out_parts, part, out, acc, sem_o, *, n_out, where):
    keep = pltpu.make_async_copy(out_parts, out, sem_o)
    keep.start()
    in_rows, in_cols = where
    acc[...] = outer_sum[...] + base[...]

    @pl.loop(0, (cols.shape[0] - n_out) // 8)
    def _(m):
        value = [jnp.dot(cols[n_out + m * 8 + u], scaled[table[in_rows + m * 8 + u]], preferred_element_type=F32) for u in range(8)]
        for u in range(8):
            acc[table[in_cols + m * 8 + u]] += value[u]

    part[...] = acc[...].astype(BF16)
    keep.wait()


def finish_kernel(n_grp, part, whole, s2, r2):
    q, g = lax.axis_index("dom"), lax.axis_index("grp")
    own = part.shape[1]
    mine = pl.ds(pl.multiple_of(g * own, own), own)
    barrier = pltpu.get_barrier_semaphore()
    signal_group(q, g, n_grp)(barrier)
    pl.semaphore_wait(barrier, n_grp - 1)
    last = []
    for r in range(1, n_grp):
        last.append(pltpu.make_async_remote_copy(
            src_ref=part, dst_ref=whole.at[:, mine], send_sem=s2.at[r - 1], recv_sem=r2.at[r - 1],
            device_id=(q, (g + r) % n_grp), device_id_type=MESH))
    for c in last:
        c.start()
    whole[:, mine] = part[...]
    for c in last:
        c.wait()


def params(collective=None, vmem=48):
    if collective is None:
        return pltpu.CompilerParams(vmem_limit_bytes=vmem << 20)
    return pltpu.CompilerParams(vmem_limit_bytes=vmem << 20, collective_id=collective, has_side_effects=True)


def shards(features, w_self, w_neigh, cotangent, inner_rows, inner_cols, inner_values, send_blocks, outer_rows, outer_values, live_count):
    blk = inner_values.shape[-1]
    nodes, fw = features.shape
    n_blk = nodes // blk
    parts, n_grp = lax.axis_size("dom"), lax.axis_size("grp")
    x = x_extent(parts)
    near = 2 * x
    layers = parts // near
    n_src = parts // n_grp
    slots = send_blocks.shape[-1]
    hid = w_self.shape[1]
    own = blk // n_grp
    n_in, n_out = inner_values.shape[1], outer_values.shape[1]
    n_all = n_in + n_out
    inner, outer = inner_values[0], outer_values[0]
    table = jnp.concatenate([send_blocks.reshape(-1), outer_rows[0], live_count[0], inner_rows[0], inner_cols[0]])
    feat = features.reshape(n_blk, blk, fw)
    dma, sds = pltpu.SemaphoreType.DMA, jax.ShapeDtypeStruct
    vm = pltpu.VMEM
    block = (n_src, slots, blk, fw)
    mine = (n_blk, own, fw)
    y_sem = dma((n_grp - 1,))

    inc, cot_all, w_all, place_all, cols, divisor = pl.pallas_call(
        functools.partial(forward_exchange, x, n_src, n_grp),
        out_shape=(sds(block, BF16), sds((n_grp, n_blk, own, hid), BF16), sds((n_grp, 2 * fw, hid), BF16), sds((layers, 8, 128), jnp.int32),
                   sds((n_all, own, blk), BF16), sds(mine, F32)),
        in_specs=[SM] + [HB] * 9,
        out_specs=(ANY,) * 6,
        scratch_shapes=[vm((n_blk, blk, fw), BF16), vm(block, BF16), vm((n_all, blk, blk), BF16), vm((n_all, blk), F32),
                        vm((layers, 8, 128), jnp.int32), vm((1, n_out), jnp.int32), vm((1, n_in), jnp.int32), vm((1, parts), jnp.int32), vm((n_all, own, blk), BF16), vm(mine, F32),
                        dma((n_src,)), dma((n_src,)), y_sem, y_sem, dma((n_grp - 1, 2)), dma((n_grp - 1, 2)),
                        dma((layers,)), dma((layers,)), dma((12,))],
        compiler_params=params(0, 62), name="forward_exchange",
    )(table, outer_rows, inner_rows, live_count, feat, cotangent.reshape(n_blk, blk, hid), w_self, w_neigh, inner, outer)

    part = pl.pallas_call(
        functools.partial(aggregate_kernel, x, n_src, n_grp),
        out_shape=sds((n_blk, blk, fw), BF16),
        in_specs=[SM, HB, ANY, HB, HB],
        out_specs=VM,
        scratch_shapes=[vm((n_blk, blk, fw), BF16), vm((n_blk, blk, fw), F32), vm((n_in // n_grp, blk, blk), BF16),
                        vm((n_src, slots, blk, blk), BF16), vm(block, BF16), dma, dma, dma, dma],
        compiler_params=params(None, 62), name="aggregate",
    )(table, feat, inc, inner, outer)

    halves = hid // 128
    out_all, scaled, base, wgrad = pl.pallas_call(
        functools.partial(dense_kernel, n_grp),
        out_shape=(sds((n_grp, n_blk, own, hid), BF16), sds((n_blk, blk, fw), BF16), sds(mine, F32), sds((n_grp, halves, 2 * fw, 128), BF16)),
        in_specs=[VM, HB, VM, ANY, ANY],
        out_specs=(VM,) * 4,
        scratch_shapes=[vm(mine, BF16), vm((n_grp, n_blk, own, hid), BF16), vm((n_grp, 2 * fw, hid), BF16),
                        vm((n_grp - 1,) + mine, BF16), vm(mine, BF16), y_sem, y_sem, y_sem, y_sem, dma((3,))],
        compiler_params=params(1), name="dense",
    )(part, feat, divisor, cot_all, w_all)

    depth = halves * 2 * fw // parts
    half = layers // 2
    near_sem, far_sem = dma((near,)), dma((layers,))
    outer_sum, out_parts, grads = pl.pallas_call(
        functools.partial(backward_exchange, x, n_grp),
        out_shape=(sds(mine, F32), sds((n_blk, blk, hid), BF16), sds((parts, depth, 128), F32)),
        in_specs=[SM, VM, VM, ANY, VM, VM],
        out_specs=(VM, ANY, VM),
        scratch_shapes=[vm((layers, near, slots, own, fw), BF16), vm((layers, near, slots, own, fw), BF16)]
        + [vm((half,) + mine, BF16)] * 4
        + [vm((n_grp - 1, halves, 2 * fw, 128), BF16), vm((parts, depth, 128), F32), vm((near, layers, depth, 128), F32),
           vm((layers, depth, 128), F32), vm((layers, depth, 128), F32)]
        + [dma((layers, near))] * 2 + [dma((half,))] * 4 + [y_sem] * 4
        + [near_sem] * 2 + [far_sem] * 4 + [near_sem] * 2 + [dma],
        compiler_params=params(2), name="backward_exchange",
    )(table, scaled, cols, out_all, wgrad, place_all)

    _, _, in_rows, in_cols = tables(parts, slots, n_in)
    pulled, layer_out = pl.pallas_call(
        functools.partial(pull_kernel, n_out=n_out, where=(in_rows, in_cols)),
        out_shape=(sds(mine, BF16), sds((n_blk, blk, hid), BF16)),
        in_specs=[SM, VM, VM, VM, VM, ANY],
        out_specs=(VM, ANY),
        scratch_shapes=[vm(mine, F32), dma],
        compiler_params=params(), name="pull",
    )(table, scaled, cols, outer_sum, base, out_parts)

    whole = pl.pallas_call(
        functools.partial(finish_kernel, n_grp),
        out_shape=sds((n_blk, blk, fw), BF16),
        in_specs=[VM],
        out_specs=VM,
        scratch_shapes=[y_sem, y_sem],
        compiler_params=params(3), name="finish",
    )(pulled)
    grads = grads.reshape(halves, 2 * fw, 128)
    grads = jnp.concatenate([grads[h] for h in range(halves)], axis=1)
    return layer_out.reshape(nodes, hid), whole.astype(F32).reshape(nodes, fw), grads[:fw], grads[fw:]


def solution(mesh):
    placed = (
        P("dom", None),
        P(None, "grp"),
        P(None, "grp"),
        P("dom", "grp"),
        P("dom", None),
        P("dom", None),
        P("dom", None, None, None),
        P("dom", None, None),
        P("dom", None),
        P("dom", None, None, None),
        P("dom", None),
    )
    return jax.shard_map(
        shards,
        mesh=mesh,
        in_specs=placed,
        out_specs=(P("dom", "grp"), P("dom", None), P(None, "grp"), P(None, "grp")),
        check_vma=False,
    )
```

```python
import functools

import jax
import jax.numpy as jnp
from jax import lax
from jax.experimental import pallas as pl
from jax.experimental.pallas import tpu as pltpu
from jax.sharding import PartitionSpec as P

MESH = pl.DeviceIdType.MESH
ANY = pl.BlockSpec(memory_space=pl.ANY)
VM = pl.BlockSpec(memory_space=pltpu.VMEM)
SM = pl.BlockSpec(memory_space=pltpu.SMEM)
HB = pl.BlockSpec(memory_space=pltpu.HBM)
F32 = jnp.float32
BF16 = jnp.bfloat16
TRANS_A = (((0,), (0,)), ((), ()))
TRANS_B = (((1,), (1,)), ((), ()))


def x_extent(parts):
    return 4 if parts == 64 else 1


def plane_peer(i, q, g, x):
    z = q // (2 * x)
    return (((i // x) * 2 + (z + g // 2) % 2) * x + i % x) * 2 + (q + g) % 2


def plane_slot(q, x):
    return (q // (4 * x)) * x + (q // 2) % x


def enter(peers, count):
    barrier = pltpu.get_barrier_semaphore()
    for peer in peers:
        peer(barrier)
    pl.semaphore_wait(barrier, count)


def signal_plane(q, g, x, n_src):
    slot = plane_slot(q, x)

    def go(barrier):
        @pl.when(g != 0)
        def _():
            pl.semaphore_signal(barrier, inc=1, device_id=(plane_peer(slot, q, g, x), g), device_id_type=MESH)

        @pl.loop(1, n_src)
        def _(i):
            peer = plane_peer((slot + i) % n_src, q, g, x)
            pl.semaphore_signal(barrier, inc=1, device_id=(peer, g), device_id_type=MESH)

    return go


def signal_group(q, g, n_grp):
    def go(barrier):
        for r in range(1, n_grp):
            pl.semaphore_signal(barrier, inc=1, device_id=(q, (g + r) % n_grp), device_id_type=MESH)

    return go


def tables(parts, slots, n_inner):
    out_rows = parts * slots
    live = 2 * parts * slots
    return out_rows, live, live + parts, live + parts + n_inner


def signal_ring(q, g, near, layers):
    z, k = q // near, q % near

    def go(barrier):
        @pl.loop(1, near)
        def _(r):
            pl.semaphore_signal(barrier, inc=1, device_id=(z * near + (k + r) % near, g), device_id_type=MESH)

        @pl.loop(1, layers)
        def _(r):
            pl.semaphore_signal(barrier, inc=1, device_id=((z + r) % layers * near + k, g), device_id_type=MESH)

    return go


def each(first, count, make, act):
    @pl.loop(first, count)
    def _(r):
        act(make(r))


def start(c):
    c.start()


def wait(c):
    c.wait()


def forward_exchange(x, n_src, n_grp, table, rows_out, rows_in, live, features, cot, w_self, w_neigh, inner, outer,
                     inc, cot_all, w_all, place_all, cols_out, divisor_out,
                     feat, stage, blocks, row_sums, places, key_out, key_in, key_live, cols, divisor, send, recv, cot_s, cot_r, w_s, w_r, p_s, p_r, loc):
    q, g = lax.axis_index("dom"), lax.axis_index("grp")
    slots = stage.shape[1]
    own = cot_all.shape[2]
    fw = w_self.shape[0]
    n_blk, blk, _ = feat.shape
    near = 2 * x
    layers = place_all.shape[0]
    z, k = q // near, q % near
    slot = plane_slot(q, x)
    n_out, n_in = outer.shape[0], inner.shape[0]
    barrier = pltpu.get_barrier_semaphore()
    load_feat = pltpu.make_async_copy(features, feat, loc.at[3])
    load_feat.start()
    signal_plane(q, g, x, n_src)(barrier)
    signal_group(q, g, n_grp)(barrier)

    @pl.loop(1, layers)
    def _(r):
        pl.semaphore_signal(barrier, inc=1, device_id=((z + r) % layers * near + k, g), device_id_type=MESH)

    mine = pl.ds(pl.multiple_of(g * own, own), own)
    local = [
        pltpu.make_async_copy(cot.at[:, mine], cot_all.at[g], loc.at[0]),
        pltpu.make_async_copy(w_self, w_all.at[g, pl.ds(0, fw)], loc.at[1]),
        pltpu.make_async_copy(w_neigh, w_all.at[g, pl.ds(fw, fw)], loc.at[2]),
        pltpu.make_async_copy(places.at[z], place_all.at[z], loc.at[6]),
    ]
    small = [
        pltpu.make_async_copy(rows_out, key_out, loc.at[7]),
        pltpu.make_async_copy(rows_in, key_in, loc.at[8]),
        pltpu.make_async_copy(live, key_live, loc.at[9]),
    ]
    loads = [
        pltpu.make_async_copy(outer, blocks.at[pl.ds(0, n_out)], loc.at[4]),
        pltpu.make_async_copy(inner, blocks.at[pl.ds(n_out, n_in)], loc.at[5]),
    ]

    def fill(d):
        peer = plane_peer(d, q, g, x)
        for s in range(slots):
            stage[d, s] = feat[table[peer * slots + s]]
        return peer

    def remote(d, peer):
        return pltpu.make_async_remote_copy(
            src_ref=stage.at[d], dst_ref=inc.at[slot], send_sem=send.at[d], recv_sem=recv.at[slot],
            device_id=(peer, g), device_id_type=MESH)

    def place(r):
        to = (z + r) % layers
        return pltpu.make_async_remote_copy(
            src_ref=places.at[to], dst_ref=place_all.at[z], send_sem=p_s.at[r], recv_sem=p_r.at[r],
            device_id=(to * near + k, g), device_id_type=MESH)

    load_feat.wait()
    home = fill(slot)
    others = n_grp - 1 + layers - 1

    @pl.when(g == 0)
    def _():
        pl.semaphore_wait(barrier, n_src - 1 + others)

    @pl.when(g != 0)
    def _():
        pl.semaphore_wait(barrier, n_src + others)

    far = []
    for r in range(1, n_grp):
        y = (g + r) % n_grp
        to = dict(device_id=(q, y), device_id_type=MESH)
        theirs = pl.ds(pl.multiple_of(y * own, own), own)
        far.append(pltpu.make_async_remote_copy(
            src_ref=cot.at[:, theirs], dst_ref=cot_all.at[g],
            send_sem=cot_s.at[r - 1], recv_sem=cot_r.at[r - 1], **to))
        far.append(pltpu.make_async_remote_copy(
            src_ref=w_self, dst_ref=w_all.at[g, pl.ds(0, fw)],
            send_sem=w_s.at[r - 1, 0], recv_sem=w_r.at[r - 1, 0], **to))
        far.append(pltpu.make_async_remote_copy(
            src_ref=w_neigh, dst_ref=w_all.at[g, pl.ds(fw, fw)],
            send_sem=w_s.at[r - 1, 1], recv_sem=w_r.at[r - 1, 1], **to))

    @pl.when(g == 0)
    def _():
        pltpu.make_async_copy(stage.at[slot], inc.at[slot], recv.at[slot]).start()

    @pl.when(g != 0)
    def _():
        remote(slot, home).start()

    @pl.loop(1, n_src)
    def _(i):
        d = (slot + i) % n_src
        remote(d, fill(d)).start()

    for c in far + local[:3] + loads + small:
        c.start()

    per = 128 // own
    lane = lax.broadcasted_iota(jnp.int32, (1, 128), 1)

    @pl.loop(0, layers)
    def _(t):
        for c in range(pl.cdiv(near * slots, per)):
            spot = lane
            for u in range(per):
                if c * per + u < near * slots:
                    target = table[t * (near * slots) + c * per + u]
                    spot = jnp.where(lane // own == u, lane + (target - u) * own, spot)
            places[t, c:c + 1, :] = spot

    local[3].start()
    each(1, layers, place, start)

    row = lax.broadcasted_iota(jnp.int32, (own + 16, blk), 0)
    lane = lax.broadcasted_iota(jnp.int32, (own + 16, blk), 1)
    pick = jnp.where((row == own) | (lane == row + g * own) & (row < own), 1.0, 0.0).astype(BF16)
    for c in loads:
        c.wait()

    @pl.loop(0, (n_out + n_in) // 8)
    def _(m):
        got = [lax.dot_general(pick, blocks[m * 8 + u], TRANS_B, preferred_element_type=F32) for u in range(8)]
        for u in range(8):
            cols[m * 8 + u] = got[u][:own].astype(BF16)
        row_sums[pl.ds(pl.multiple_of(m * 8, 8), 8), :] = jnp.concatenate([v[own:own + 1] for v in got], axis=0)

    keep = pltpu.make_async_copy(cols, cols_out, loc.at[10])
    keep.start()
    for c in small:
        c.wait()
    n_part = key_live.shape[1]
    first = slots * lax.broadcasted_iota(jnp.int32, (n_part, n_out), 0)
    at = lax.broadcasted_iota(jnp.int32, (n_part, n_out), 1) - first
    spread = jnp.where((at >= 0) & (at < slots), 1.0, 0.0)
    limit = jnp.dot(key_live[...].astype(F32), spread, precision=lax.Precision.HIGHEST, preferred_element_type=F32)
    index = jnp.sum(jnp.where((at >= 0) & (at < slots), at, 0), axis=0, keepdims=True)
    key = jnp.concatenate([jnp.where(index.astype(F32) < limit, key_out[...], n_blk), key_in[...]], axis=1)
    hits = jnp.where(lax.broadcasted_iota(jnp.int32, (n_blk, n_out + n_in), 0) == key, 1.0, 0.0)
    degree = 1.0 + jnp.dot(hits, row_sums[...], precision=lax.Precision.HIGHEST, preferred_element_type=F32)
    sel = (lax.broadcasted_iota(jnp.int32, (own, blk), 1) == lax.broadcasted_iota(jnp.int32, (own, blk), 0) + g * own)
    for b in range(n_blk):
        column = jnp.sum(jnp.where(sel, degree[b:b + 1], 0.0), axis=1, keepdims=True)
        divisor[b] = jnp.broadcast_to(column, (own, fw))

    keep_too = pltpu.make_async_copy(divisor, divisor_out, loc.at[11])
    keep_too.start()
    keep.wait()
    keep_too.wait()
    for c in local:
        c.wait()
    for c in far:
        c.wait()
    each(1, layers, place, wait)

    @pl.when(g != 0)
    def _():
        remote(slot, home).wait_send()

    @pl.loop(1, n_src)
    def _(i):
        d = (slot + i) % n_src
        remote(d, plane_peer(d, q, g, x)).wait_send()

    @pl.loop(0, n_src)
    def _(j):
        pltpu.make_async_copy(stage.at[j], inc.at[j], recv.at[j]).wait()


def aggregate_kernel(x, n_src, n_grp, table, features, inc, inner, outer, part, feat, acc, a_in, a_out, x_in, sem_f, sem_in, sem_out, sem_x):
    q, g = lax.axis_index("dom"), lax.axis_index("grp")
    slots = inc.shape[1]
    n_in = inner.shape[0] // n_grp
    out_rows, live, in_rows, in_cols = tables(n_grp * n_src, slots, inner.shape[0])
    load_f = pltpu.make_async_copy(features, feat, sem_f)
    load_f.start()
    load_in = pltpu.make_async_copy(inner.at[pl.ds(g * n_in, n_in)], a_in, sem_in)
    load_in.start()
    load_x = pltpu.make_async_copy(inc, x_in, sem_x)
    load_x.start()

    def load(i):
        peer = plane_peer(i, q, g, x)
        return pltpu.make_async_copy(outer.at[pl.ds(peer * slots, slots)], a_out.at[i], sem_out)

    @pl.loop(0, n_src)
    def _(i):
        load(i).start()

    acc[...] = jnp.zeros_like(acc)
    load_f.wait()
    load_in.wait()

    @pl.loop(0, n_in // 2)
    def _(m):
        value = [jnp.dot(a_in[m * 2 + u], feat[table[in_cols + g * n_in + m * 2 + u]], preferred_element_type=F32) for u in range(2)]
        for u in range(2):
            acc[table[in_rows + g * n_in + m * 2 + u]] += value[u]

    load_x.wait()
    pltpu.make_async_copy(a_out, a_out, sem_out).wait()

    @pl.loop(0, n_src)
    def _(i):
        peer = plane_peer(i, q, g, x)
        value = [jnp.dot(a_out[i, s], x_in[i, s], preferred_element_type=F32) for s in range(slots)]
        for s in range(slots):
            @pl.when(s < table[live + peer])
            def _(s=s):
                acc[table[out_rows + peer * slots + s]] += value[s]

    part[...] = acc[...].astype(BF16)


def dense_kernel(n_grp, part, features, divisor, cots, ws, out_all, scaled, base, wgrad, feat, cot_all, w_all, got, sent, s1, r1, s3, r3, loc):
    q, g = lax.axis_index("dom"), lax.axis_index("grp")
    n_blk, blk, fw = part.shape
    own = base.shape[1]
    rows, hid = n_blk * own, ws.shape[2]
    mine = pl.ds(pl.multiple_of(g * own, own), own)
    barrier = pltpu.get_barrier_semaphore()
    signal_group(q, g, n_grp)(barrier)
    loads = [
        pltpu.make_async_copy(features.at[:, mine], feat, loc.at[0]),
        pltpu.make_async_copy(ws, w_all, loc.at[1]),
        pltpu.make_async_copy(cots, cot_all, loc.at[2]),
    ]
    for c in loads:
        c.start()
    pl.semaphore_wait(barrier, n_grp - 1)
    copies, last = [], []
    for r in range(1, n_grp):
        y = (g + r) % n_grp
        to = dict(device_id=(q, y), device_id_type=MESH)
        theirs = pl.ds(pl.multiple_of(y * own, own), own)
        copies.append(pltpu.make_async_remote_copy(
            src_ref=part.at[:, theirs], dst_ref=got.at[r - 1], send_sem=s1.at[r - 1], recv_sem=r1.at[r - 1], **to))
        last.append(pltpu.make_async_remote_copy(
            src_ref=sent, dst_ref=scaled.at[:, mine], send_sem=s3.at[r - 1], recv_sem=r3.at[r - 1], **to))
    for c in copies:
        c.start()
    for c in loads:
        c.wait()
    for c in copies:
        c.wait()
    own_feat = feat[...]
    total = own_feat.astype(F32) + part[:, mine].astype(F32)
    for r in range(n_grp - 1):
        total = total + got[r].astype(F32)
    agg = (total / divisor[...]).astype(BF16)
    both = jnp.concatenate([own_feat.reshape(rows, fw), agg.reshape(rows, fw)], axis=1)
    back = jnp.zeros((rows, 2 * fw), F32)
    grads = []
    for j in range(n_grp):
        pre = jnp.dot(both, w_all[j], preferred_element_type=F32)
        sig = jax.nn.sigmoid(pre)
        out_all[j] = (pre * sig).astype(BF16).reshape(n_blk, own, hid)
        cot = cot_all[j].reshape(rows, hid).astype(F32)
        grad = (cot * sig * (1.0 + pre * (1.0 - sig))).astype(BF16)
        grads.append(grad)
        back = back + lax.dot_general(grad, w_all[j], TRANS_B, preferred_element_type=F32)
    down = (back[:, fw:].reshape(n_blk, own, fw) / divisor[...]).astype(BF16)
    sent[...] = down
    for c in last:
        c.start()
    scaled[:, mine] = down
    base[...] = back[:, :fw].reshape(n_blk, own, fw) + down.astype(F32)
    for j in range(n_grp):
        gw = lax.dot_general(both, grads[j], TRANS_A, preferred_element_type=F32).astype(BF16)
        for h in range(hid // 128):
            wgrad[j, h] = gw[:, 128 * h:128 * (h + 1)]
    for c in last:
        c.wait()


def backward_exchange(x, n_grp, n_in, table, scaled, cols, out_all, wgrad, places, base_sum, whole, out, grads,
                      inner_terms, inner_sum, sent, stage, inbox, right_out, right_in, left_out, left_in, w_got, pieces, near_got, far_sent, far_got,
                      send, recv, rs, rr, ls, lr, o_s, o_r, w_s, w_r, a_s, a_r, b_s, b_r, c_s, c_r, d_s, d_r, e_s, e_r, loc):
    q, g = lax.axis_index("dom"), lax.axis_index("grp")
    layers, near, slots, own, fw = stage.shape
    n_blk = whole.shape[0]
    cut = n_blk // 2
    half = layers // 2
    z, k = q // near, q % near
    out_rows, live, in_rows, in_cols = tables(layers * near, slots, n_in)
    n_out = layers * near * slots
    barrier = pltpu.get_barrier_semaphore()
    signal_group(q, g, n_grp)(barrier)
    signal_ring(q, g, near, layers)(barrier)
    mine = pl.ds(pl.multiple_of(g * own, own), own)
    keep = pltpu.make_async_copy(out_all.at[g], out.at[:, mine], loc)
    keep.start()
    far, grad_far, last = [], [], []
    for r in range(1, n_grp):
        y = (g + r) % n_grp
        to = dict(device_id=(q, y), device_id_type=MESH)
        last.append(pltpu.make_async_remote_copy(
            src_ref=sent, dst_ref=whole.at[:, mine], send_sem=e_s.at[r - 1], recv_sem=e_r.at[r - 1], **to))
        far.append(pltpu.make_async_remote_copy(
            src_ref=out_all.at[y], dst_ref=out.at[:, mine], send_sem=o_s.at[r - 1], recv_sem=o_r.at[r - 1], **to))
        grad_far.append(pltpu.make_async_remote_copy(
            src_ref=wgrad.at[y], dst_ref=w_got.at[r - 1], send_sem=w_s.at[r - 1], recv_sem=w_r.at[r - 1], **to))

    def to_near(d, r):
        to = (k + r) % near
        return pltpu.make_async_remote_copy(
            src_ref=stage.at[d, to], dst_ref=inbox.at[d, k], send_sem=send.at[d, r], recv_sem=recv.at[d, r],
            device_id=(z * near + to, g), device_id_type=MESH)

    def own_term(d):
        return pltpu.make_async_copy(stage.at[d, k], inbox.at[d, k], recv.at[d, 0])

    def products(d):
        base = (z + d) % layers * near

        group = max(1, near // 2)

        @pl.loop(0, near // group)
        def _(r):
            value = []
            for u in range(group):
                for s in range(slots):
                    n = (base + r * group + u) * slots + s
                    value.append(jnp.dot(cols[n], scaled[table[out_rows + n]], preferred_element_type=F32))
            for u in range(group):
                to = r * group + u
                for s in range(slots):
                    stage[d, to, s] = jnp.where(s < table[live + base + to], value[u * slots + s], 0.0).astype(BF16)

    def ship(d):
        own_term(d).start()
        each(1, near, functools.partial(to_near, d), start)

    def reduce(d):
        own_term(d).wait()
        each(1, near, functools.partial(to_near, d), wait)
        n = near * slots * own
        spot = places[(z + d) % layers]
        row = lax.broadcasted_iota(jnp.int32, (n_blk * own, 128), 0)
        hot = [jnp.where(row == spot[c:c + 1], 1.0, 0.0).astype(BF16) for c in range(pl.cdiv(n, 128))]
        hot = jnp.concatenate(hot, axis=1)[:, :n] if len(hot) > 1 else hot[0][:, :n]
        terms = inbox[d].reshape(n, fw)
        return jnp.dot(hot, terms, preferred_element_type=F32).reshape(n_blk, own, fw)

    def ring(i, to_right):
        count = cut if i == 0 else n_blk
        held, lands, s_sem, r_sem, step = (right_out, right_in, rs, rr, 1) if to_right else (left_out, left_in, ls, lr, layers - 1)
        return pltpu.make_async_remote_copy(
            src_ref=held.at[i, pl.ds(0, count)], dst_ref=lands.at[i, pl.ds(0, count)], send_sem=s_sem.at[i], recv_sem=r_sem.at[i],
            device_id=((z + step) % layers * near + k, g), device_id_type=MESH)

    def with_right(i, value):
        ring(i, True).wait()
        if i == 0:
            return jnp.concatenate([value[:cut] + right_in[0, :cut].astype(F32), value[cut:]], axis=0)
        return value + right_in[i].astype(F32)

    def with_left(i, value):
        ring(i, False).wait()
        if i == 0:
            return jnp.concatenate([value[:cut], value[cut:] + left_in[0, :cut].astype(F32)], axis=0)
        return value + left_in[i].astype(F32)

    def near_reduce(r):
        to = (k + r) % near
        return pltpu.make_async_remote_copy(
            src_ref=pieces.at[pl.ds(to * layers, layers)], dst_ref=near_got.at[r],
            send_sem=a_s.at[r], recv_sem=a_r.at[r], device_id=(z * near + to, g), device_id_type=MESH)

    def far_reduce(r):
        to = (z + r) % layers
        return pltpu.make_async_remote_copy(
            src_ref=far_sent.at[to], dst_ref=far_got.at[r],
            send_sem=b_s.at[r], recv_sem=b_r.at[r], device_id=(to * near + k, g), device_id_type=MESH)

    def far_gather(r):
        to = (z + r) % layers
        return pltpu.make_async_remote_copy(
            src_ref=grads.at[k * layers + z], dst_ref=grads.at[k * layers + z],
            send_sem=c_s.at[r], recv_sem=c_r.at[r], device_id=(to * near + k, g), device_id_type=MESH)

    def near_gather(r):
        to = (k + r) % near
        return pltpu.make_async_remote_copy(
            src_ref=grads.at[pl.ds(k * layers, layers)], dst_ref=grads.at[pl.ds(k * layers, layers)],
            send_sem=d_s.at[r], recv_sem=d_r.at[r], device_id=(z * near + to, g), device_id_type=MESH)

    def sum_grp():
        for c in grad_far:
            c.wait()
        halves = wgrad.shape[1]
        per = pieces.shape[0] // halves
        for h in range(halves):
            total = wgrad[g, h].astype(F32)
            for r in range(n_grp - 1):
                total = total + w_got[r, h].astype(F32)
            pieces[h * per:(h + 1) * per] = total.reshape(per, pieces.shape[1], 128)
        each(1, near, near_reduce, start)

    def sum_near():
        each(1, near, near_reduce, wait)
        total = pieces[pl.ds(k * layers, layers)]
        for r in range(1, near):
            total = total + near_got[r]
        far_sent[...] = total
        each(1, layers, far_reduce, start)

    def sum_far():
        each(1, layers, far_reduce, wait)
        total = far_sent[z]
        for r in range(1, layers):
            total = total + far_got[r]
        grads[k * layers + z] = total
        each(1, layers, far_gather, start)

    def spread():
        each(1, layers, far_gather, wait)
        each(1, near, near_gather, start)

    def inner():
        per = 128 // own
        step = 4 * per

        @pl.loop(0, n_in // 8)
        def _(m):
            value = [jnp.dot(cols[n_out + m * 8 + u], scaled[table[in_rows + m * 8 + u]], preferred_element_type=F32) for u in range(8)]
            for u in range(8):
                inner_terms[m * 8 + u] = value[u].astype(BF16)

        lane = lax.broadcasted_iota(jnp.int32, (1, 128), 1)
        row = lax.broadcasted_iota(jnp.int32, (n_blk * own, 128), 0)
        inner_sum[...] = base_sum[...]

        def add(m, count):
            hot = []
            for c in range(count):
                spot = lane
                for u in range(per):
                    target = table[in_cols + m * step + c * per + u]
                    spot = jnp.where(lane // own == u, lane + (target - u) * own, spot)
                hot.append(jnp.where(row == spot, 1.0, 0.0).astype(BF16))
            hot = jnp.concatenate(hot, axis=1) if count > 1 else hot[0]
            terms = inner_terms[pl.ds(m * step, count * per)].reshape(count * per * own, fw)
            inner_sum[...] += jnp.dot(hot, terms, preferred_element_type=F32).reshape(n_blk, own, fw)

        if n_in % step:
            for m in range(n_in // step):
                add(m, 4)
            add(n_in // step, n_in % step // per)
        else:
            @pl.loop(0, n_in // step)
            def _(m):
                add(m, 4)

    products(half)
    pl.semaphore_wait(barrier, n_grp - 1 + near - 1 + layers - 1)
    for c in grad_far:
        c.start()
    ship(half)
    for c in far:
        c.start()
    for i in range(half):
        d = half - i
        if d > 1:
            for e in (d - 1, layers - d + 1):
                products(e)
                ship(e)
        else:
            products(0)
            ship(0)
        if i == 0:
            value = reduce(half)
            right_out[0, :cut] = value[:cut].astype(BF16)
            left_out[0, :cut] = value[cut:].astype(BF16)
        else:
            right_out[i] = with_right(i - 1, reduce(d)).astype(BF16)
            left_out[i] = with_left(i - 1, reduce(layers - d)).astype(BF16)
        ring(i, True).start()
        ring(i, False).start()
        if i == 0:
            sum_grp()
            inner()
        if i == min(2, half - 1):
            sum_near()
    value = reduce(0) + inner_sum[...]
    sum_far()
    value = with_left(half - 1, with_right(half - 1, value)).astype(BF16)
    sent[...] = value
    for c in last:
        c.start()
    whole[:, mine] = value
    spread()
    keep.wait()
    for c in far:
        c.wait()
    each(1, near, near_gather, wait)
    for c in last:
        c.wait()


def params(collective=None, vmem=48):
    if collective is None:
        return pltpu.CompilerParams(vmem_limit_bytes=vmem << 20)
    return pltpu.CompilerParams(vmem_limit_bytes=vmem << 20, collective_id=collective, has_side_effects=True)


def shards(features, w_self, w_neigh, cotangent, inner_rows, inner_cols, inner_values, send_blocks, outer_rows, outer_values, live_count):
    blk = inner_values.shape[-1]
    nodes, fw = features.shape
    n_blk = nodes // blk
    parts, n_grp = lax.axis_size("dom"), lax.axis_size("grp")
    x = x_extent(parts)
    near = 2 * x
    layers = parts // near
    n_src = parts // n_grp
    slots = send_blocks.shape[-1]
    hid = w_self.shape[1]
    own = blk // n_grp
    n_in, n_out = inner_values.shape[1], outer_values.shape[1]
    n_all = n_in + n_out
    inner, outer = inner_values[0], outer_values[0]
    table = jnp.concatenate([send_blocks.reshape(-1), outer_rows[0], live_count[0], inner_rows[0], inner_cols[0]])
    feat = features.reshape(n_blk, blk, fw)
    dma, sds = pltpu.SemaphoreType.DMA, jax.ShapeDtypeStruct
    vm = pltpu.VMEM
    block = (n_src, slots, blk, fw)
    mine = (n_blk, own, fw)
    y_sem = dma((n_grp - 1,))

    inc, cot_all, w_all, place_all, cols, divisor = pl.pallas_call(
        functools.partial(forward_exchange, x, n_src, n_grp),
        out_shape=(sds(block, BF16), sds((n_grp, n_blk, own, hid), BF16), sds((n_grp, 2 * fw, hid), BF16), sds((layers, 8, 128), jnp.int32),
                   sds((n_all, own, blk), BF16), sds(mine, F32)),
        in_specs=[SM] + [HB] * 9,
        out_specs=(ANY,) * 6,
        scratch_shapes=[vm((n_blk, blk, fw), BF16), vm(block, BF16), vm((n_all, blk, blk), BF16), vm((n_all, blk), F32),
                        vm((layers, 8, 128), jnp.int32), vm((1, n_out), jnp.int32), vm((1, n_in), jnp.int32), vm((1, parts), jnp.int32), vm((n_all, own, blk), BF16), vm(mine, F32),
                        dma((n_src,)), dma((n_src,)), y_sem, y_sem, dma((n_grp - 1, 2)), dma((n_grp - 1, 2)),
                        dma((layers,)), dma((layers,)), dma((12,))],
        compiler_params=params(0, 62), name="forward_exchange",
    )(table, outer_rows, inner_rows, live_count, feat, cotangent.reshape(n_blk, blk, hid), w_self, w_neigh, inner, outer)

    part = pl.pallas_call(
        functools.partial(aggregate_kernel, x, n_src, n_grp),
        out_shape=sds((n_blk, blk, fw), BF16),
        in_specs=[SM, HB, ANY, HB, HB],
        out_specs=VM,
        scratch_shapes=[vm((n_blk, blk, fw), BF16), vm((n_blk, blk, fw), F32), vm((n_in // n_grp, blk, blk), BF16),
                        vm((n_src, slots, blk, blk), BF16), vm(block, BF16), dma, dma, dma, dma],
        compiler_params=params(None, 62), name="aggregate",
    )(table, feat, inc, inner, outer)

    halves = hid // 128
    out_all, scaled, base, wgrad = pl.pallas_call(
        functools.partial(dense_kernel, n_grp),
        out_shape=(sds((n_grp, n_blk, own, hid), BF16), sds((n_blk, blk, fw), BF16), sds(mine, F32), sds((n_grp, halves, 2 * fw, 128), BF16)),
        in_specs=[VM, HB, VM, ANY, ANY],
        out_specs=(VM,) * 4,
        scratch_shapes=[vm(mine, BF16), vm((n_grp, n_blk, own, hid), BF16), vm((n_grp, 2 * fw, hid), BF16),
                        vm((n_grp - 1,) + mine, BF16), vm(mine, BF16), y_sem, y_sem, y_sem, y_sem, dma((3,))],
        compiler_params=params(1), name="dense",
    )(part, feat, divisor, cot_all, w_all)

    depth = halves * 2 * fw // parts
    half = layers // 2
    near_sem, far_sem = dma((near,)), dma((layers,))
    whole, layer_out, grads = pl.pallas_call(
        functools.partial(backward_exchange, x, n_grp, n_in),
        out_shape=(sds((n_blk, blk, fw), BF16), sds((n_blk, blk, hid), BF16), sds((parts, depth, 128), F32)),
        in_specs=[SM, VM, VM, ANY, VM, VM, VM],
        out_specs=(VM, ANY, VM),
        scratch_shapes=[vm((n_in, own, fw), BF16), vm(mine, F32), vm(mine, BF16), vm((layers, near, slots, own, fw), BF16), vm((layers, near, slots, own, fw), BF16)]
        + [vm((half,) + mine, BF16)] * 4
        + [vm((n_grp - 1, halves, 2 * fw, 128), BF16), vm((parts, depth, 128), F32), vm((near, layers, depth, 128), F32),
           vm((layers, depth, 128), F32), vm((layers, depth, 128), F32)]
        + [dma((layers, near))] * 2 + [dma((half,))] * 4 + [y_sem] * 4
        + [near_sem] * 2 + [far_sem] * 4 + [near_sem] * 2 + [y_sem] * 2 + [dma],
        compiler_params=params(2), name="backward_exchange",
    )(table, scaled, cols, out_all, wgrad, place_all, base)

    grads = grads.reshape(halves, 2 * fw, 128)
    grads = jnp.concatenate([grads[h] for h in range(halves)], axis=1)
    return layer_out.reshape(nodes, hid), whole.astype(F32).reshape(nodes, fw), grads[:fw], grads[fw:]


def solution(mesh):
    placed = (
        P("dom", None),
        P(None, "grp"),
        P(None, "grp"),
        P("dom", "grp"),
        P("dom", None),
        P("dom", None),
        P("dom", None, None, None),
        P("dom", None, None),
        P("dom", None),
        P("dom", None, None, None),
        P("dom", None),
    )
    return jax.shard_map(
        shards,
        mesh=mesh,
        in_specs=placed,
        out_specs=(P("dom", "grp"), P("dom", None), P(None, "grp"), P(None, "grp")),
        check_vma=False,
    )
```

```python
import functools

import jax
import jax.numpy as jnp
from jax import lax
from jax.experimental import pallas as pl
from jax.experimental.pallas import tpu as pltpu
from jax.sharding import PartitionSpec as P

MESH = pl.DeviceIdType.MESH
ANY = pl.BlockSpec(memory_space=pl.ANY)
VM = pl.BlockSpec(memory_space=pltpu.VMEM)
SM = pl.BlockSpec(memory_space=pltpu.SMEM)
HB = pl.BlockSpec(memory_space=pltpu.HBM)
F32 = jnp.float32
BF16 = jnp.bfloat16
TRANS_A = (((0,), (0,)), ((), ()))
TRANS_B = (((1,), (1,)), ((), ()))


def x_extent(parts):
    return 4 if parts == 64 else 1


def plane_peer(i, q, g, x):
    z = q // (2 * x)
    return (((i // x) * 2 + (z + g // 2) % 2) * x + i % x) * 2 + (q + g) % 2


def plane_slot(q, x):
    return (q // (4 * x)) * x + (q // 2) % x


def enter(peers, count):
    barrier = pltpu.get_barrier_semaphore()
    for peer in peers:
        peer(barrier)
    pl.semaphore_wait(barrier, count)


def signal_plane(q, g, x, n_src):
    slot = plane_slot(q, x)

    def go(barrier):
        @pl.when(g != 0)
        def _():
            pl.semaphore_signal(barrier, inc=1, device_id=(plane_peer(slot, q, g, x), g), device_id_type=MESH)

        @pl.loop(1, n_src)
        def _(i):
            peer = plane_peer((slot + i) % n_src, q, g, x)
            pl.semaphore_signal(barrier, inc=1, device_id=(peer, g), device_id_type=MESH)

    return go


def signal_group(q, g, n_grp):
    def go(barrier):
        for r in range(1, n_grp):
            pl.semaphore_signal(barrier, inc=1, device_id=(q, (g + r) % n_grp), device_id_type=MESH)

    return go


def load_indices(arrays, copies, sem):
    loads = [pltpu.make_async_copy(a, b, sem.at[n]) for n, (a, b) in enumerate(zip(arrays, copies))]
    for c in loads:
        c.start()
    return loads


def signal_ring(q, g, near, layers):
    z, k = q // near, q % near

    def go(barrier):
        @pl.loop(1, near)
        def _(r):
            pl.semaphore_signal(barrier, inc=1, device_id=(z * near + (k + r) % near, g), device_id_type=MESH)

        @pl.loop(1, layers)
        def _(r):
            pl.semaphore_signal(barrier, inc=1, device_id=((z + r) % layers * near + k, g), device_id_type=MESH)

    return go


def each(first, count, make, act):
    @pl.loop(first, count)
    def _(r):
        act(make(r))


def start(c):
    c.start()


def wait(c):
    c.wait()


def forward_exchange(x, n_src, n_grp, sends, rows_out, rows_in, live, features, cot, w_self, w_neigh, inner, outer,
                     inc, cot_all, w_all, place_all, cols_out, divisor_out, own_feat,
                     feat, stage, blocks, row_sums, places, key_out, key_in, key_live, cols, divisor, table, send, recv, cot_s, cot_r, w_s, w_r, p_s, p_r, loc):
    q, g = lax.axis_index("dom"), lax.axis_index("grp")
    slots = stage.shape[1]
    own = cot_all.shape[2]
    fw = w_self.shape[0]
    n_blk, blk, _ = feat.shape
    near = 2 * x
    layers = place_all.shape[0]
    z, k = q // near, q % near
    slot = plane_slot(q, x)
    n_out, n_in = outer.shape[0], inner.shape[0]
    barrier = pltpu.get_barrier_semaphore()
    load_feat = pltpu.make_async_copy(features, feat, loc.at[3])
    load_feat.start()
    load_sends = pltpu.make_async_copy(sends, table, loc.at[13])
    load_sends.start()
    signal_plane(q, g, x, n_src)(barrier)
    signal_group(q, g, n_grp)(barrier)

    @pl.loop(1, layers)
    def _(r):
        pl.semaphore_signal(barrier, inc=1, device_id=((z + r) % layers * near + k, g), device_id_type=MESH)

    mine = pl.ds(pl.multiple_of(g * own, own), own)
    local = [
        pltpu.make_async_copy(cot.at[:, mine], cot_all.at[g], loc.at[0]),
        pltpu.make_async_copy(w_self, w_all.at[g, pl.ds(0, fw)], loc.at[1]),
        pltpu.make_async_copy(w_neigh, w_all.at[g, pl.ds(fw, fw)], loc.at[2]),
        pltpu.make_async_copy(places.at[z], place_all.at[z], loc.at[6]),
        pltpu.make_async_copy(feat.at[:, mine], own_feat, loc.at[12]),
    ]
    small = [
        pltpu.make_async_copy(rows_out, key_out, loc.at[7]),
        pltpu.make_async_copy(rows_in, key_in, loc.at[8]),
        pltpu.make_async_copy(live, key_live, loc.at[9]),
    ]
    loads = [
        pltpu.make_async_copy(outer, blocks.at[pl.ds(0, n_out)], loc.at[4]),
        pltpu.make_async_copy(inner, blocks.at[pl.ds(n_out, n_in)], loc.at[5]),
    ]

    def fill(d):
        peer = plane_peer(d, q, g, x)
        for s in range(slots):
            stage[d, s] = feat[table[peer, s]]
        return peer

    def remote(d, peer):
        return pltpu.make_async_remote_copy(
            src_ref=stage.at[d], dst_ref=inc.at[slot], send_sem=send.at[d], recv_sem=recv.at[slot],
            device_id=(peer, g), device_id_type=MESH)

    def place(r):
        to = (z + r) % layers
        return pltpu.make_async_remote_copy(
            src_ref=places.at[to], dst_ref=place_all.at[z], send_sem=p_s.at[r], recv_sem=p_r.at[r],
            device_id=(to * near + k, g), device_id_type=MESH)

    load_sends.wait()
    load_feat.wait()
    home = fill(slot)
    others = n_grp - 1 + layers - 1

    @pl.when(g == 0)
    def _():
        pl.semaphore_wait(barrier, n_src - 1 + others)

    @pl.when(g != 0)
    def _():
        pl.semaphore_wait(barrier, n_src + others)

    far = []
    for r in range(1, n_grp):
        y = (g + r) % n_grp
        to = dict(device_id=(q, y), device_id_type=MESH)
        theirs = pl.ds(pl.multiple_of(y * own, own), own)
        far.append(pltpu.make_async_remote_copy(
            src_ref=cot.at[:, theirs], dst_ref=cot_all.at[g],
            send_sem=cot_s.at[r - 1], recv_sem=cot_r.at[r - 1], **to))
        far.append(pltpu.make_async_remote_copy(
            src_ref=w_self, dst_ref=w_all.at[g, pl.ds(0, fw)],
            send_sem=w_s.at[r - 1, 0], recv_sem=w_r.at[r - 1, 0], **to))
        far.append(pltpu.make_async_remote_copy(
            src_ref=w_neigh, dst_ref=w_all.at[g, pl.ds(fw, fw)],
            send_sem=w_s.at[r - 1, 1], recv_sem=w_r.at[r - 1, 1], **to))

    @pl.when(g == 0)
    def _():
        pltpu.make_async_copy(stage.at[slot], inc.at[slot], recv.at[slot]).start()

    @pl.when(g != 0)
    def _():
        remote(slot, home).start()

    @pl.loop(1, n_src)
    def _(i):
        d = (slot + i) % n_src
        remote(d, fill(d)).start()

    for c in far + local[:3] + loads + small:
        c.start()

    per = 128 // own
    lane = lax.broadcasted_iota(jnp.int32, (1, 128), 1)

    @pl.loop(0, layers)
    def _(t):
        for c in range(pl.cdiv(near * slots, per)):
            spot = lane
            for u in range(per):
                if c * per + u < near * slots:
                    at = c * per + u
                    target = table[t * near + at // slots, at % slots]
                    spot = jnp.where(lane // own == u, lane + (target - u) * own, spot)
            places[t, c:c + 1, :] = spot

    local[3].start()
    local[4].start()
    each(1, layers, place, start)

    row = lax.broadcasted_iota(jnp.int32, (own + 16, blk), 0)
    lane = lax.broadcasted_iota(jnp.int32, (own + 16, blk), 1)
    pick = jnp.where((row == own) | (lane == row + g * own) & (row < own), 1.0, 0.0).astype(BF16)
    for c in loads:
        c.wait()

    @pl.loop(0, (n_out + n_in) // 8)
    def _(m):
        got = [lax.dot_general(pick, blocks[m * 8 + u], TRANS_B, preferred_element_type=F32) for u in range(8)]
        for u in range(8):
            cols[m * 8 + u] = got[u][:own].astype(BF16)
        row_sums[pl.ds(pl.multiple_of(m * 8, 8), 8), :] = jnp.concatenate([v[own:own + 1] for v in got], axis=0)

    keep = pltpu.make_async_copy(cols, cols_out, loc.at[10])
    keep.start()
    for c in small:
        c.wait()
    n_part = key_live.shape[1]
    first = slots * lax.broadcasted_iota(jnp.int32, (n_part, n_out), 0)
    at = lax.broadcasted_iota(jnp.int32, (n_part, n_out), 1) - first
    spread = jnp.where((at >= 0) & (at < slots), 1.0, 0.0)
    limit = jnp.dot(key_live[...].astype(F32), spread, precision=lax.Precision.HIGHEST, preferred_element_type=F32)
    index = jnp.sum(jnp.where((at >= 0) & (at < slots), at, 0), axis=0, keepdims=True)
    key = jnp.concatenate([jnp.where(index.astype(F32) < limit, key_out[...], n_blk), key_in[...]], axis=1)
    hits = jnp.where(lax.broadcasted_iota(jnp.int32, (n_blk, n_out + n_in), 0) == key, 1.0, 0.0)
    degree = 1.0 + jnp.dot(hits, row_sums[...], precision=lax.Precision.HIGHEST, preferred_element_type=F32)
    sel = (lax.broadcasted_iota(jnp.int32, (own, blk), 1) == lax.broadcasted_iota(jnp.int32, (own, blk), 0) + g * own)
    for b in range(n_blk):
        column = jnp.sum(jnp.where(sel, degree[b:b + 1], 0.0), axis=1, keepdims=True)
        divisor[b] = jnp.broadcast_to(column, (own, fw))

    keep_too = pltpu.make_async_copy(divisor, divisor_out, loc.at[11])
    keep_too.start()
    keep.wait()
    keep_too.wait()
    for c in local:
        c.wait()
    for c in far:
        c.wait()
    each(1, layers, place, wait)

    @pl.when(g != 0)
    def _():
        remote(slot, home).wait_send()

    @pl.loop(1, n_src)
    def _(i):
        d = (slot + i) % n_src
        remote(d, plane_peer(d, q, g, x)).wait_send()

    @pl.loop(0, n_src)
    def _(j):
        pltpu.make_async_copy(stage.at[j], inc.at[j], recv.at[j]).wait()


def aggregate_kernel(x, n_src, n_grp, i0, i1, i2, i3, features, inc, inner, outer, part, out_rows, live, in_rows, in_cols, i_sem, feat, acc, a_in, a_out, x_in, sem_f, sem_in, sem_out, sem_x):
    q, g = lax.axis_index("dom"), lax.axis_index("grp")
    slots = inc.shape[1]
    n_in = inner.shape[0] // n_grp
    indices = load_indices((i0, i1, i2, i3), (out_rows, live, in_rows, in_cols), i_sem)
    load_f = pltpu.make_async_copy(features, feat, sem_f)
    load_f.start()
    load_in = pltpu.make_async_copy(inner.at[pl.ds(g * n_in, n_in)], a_in, sem_in)
    load_in.start()
    load_x = pltpu.make_async_copy(inc, x_in, sem_x)
    load_x.start()

    def load(i):
        peer = plane_peer(i, q, g, x)
        return pltpu.make_async_copy(outer.at[pl.ds(peer * slots, slots)], a_out.at[i], sem_out)

    @pl.loop(0, n_src)
    def _(i):
        load(i).start()

    acc[...] = jnp.zeros_like(acc)
    for c in indices:
        c.wait()
    load_f.wait()
    load_in.wait()

    @pl.loop(0, n_in // 2)
    def _(m):
        value = [jnp.dot(a_in[m * 2 + u], feat[in_cols[0, g * n_in + m * 2 + u]], preferred_element_type=F32) for u in range(2)]
        for u in range(2):
            acc[in_rows[0, g * n_in + m * 2 + u]] += value[u]

    load_x.wait()
    pltpu.make_async_copy(a_out, a_out, sem_out).wait()

    @pl.loop(0, n_src)
    def _(i):
        peer = plane_peer(i, q, g, x)
        value = [jnp.dot(a_out[i, s], x_in[i, s], preferred_element_type=F32) for s in range(slots)]
        for s in range(slots):
            @pl.when(s < live[0, peer])
            def _(s=s):
                acc[out_rows[0, peer * slots + s]] += value[s]

    part[...] = acc[...].astype(BF16)


def dense_kernel(n_grp, part, feat, divisor, cots, ws, out_all, scaled, base, wgrad, cot_all, w_all, got, sent, s1, r1, s3, r3, loc):
    q, g = lax.axis_index("dom"), lax.axis_index("grp")
    n_blk, blk, fw = part.shape
    own = base.shape[1]
    rows, hid = n_blk * own, ws.shape[2]
    mine = pl.ds(pl.multiple_of(g * own, own), own)
    barrier = pltpu.get_barrier_semaphore()
    signal_group(q, g, n_grp)(barrier)
    loads = [
        pltpu.make_async_copy(ws, w_all, loc.at[1]),
        pltpu.make_async_copy(cots, cot_all, loc.at[2]),
    ]
    for c in loads:
        c.start()
    pl.semaphore_wait(barrier, n_grp - 1)
    copies, last = [], []
    for r in range(1, n_grp):
        y = (g + r) % n_grp
        to = dict(device_id=(q, y), device_id_type=MESH)
        theirs = pl.ds(pl.multiple_of(y * own, own), own)
        copies.append(pltpu.make_async_remote_copy(
            src_ref=part.at[:, theirs], dst_ref=got.at[r - 1], send_sem=s1.at[r - 1], recv_sem=r1.at[r - 1], **to))
        last.append(pltpu.make_async_remote_copy(
            src_ref=sent, dst_ref=scaled.at[:, mine], send_sem=s3.at[r - 1], recv_sem=r3.at[r - 1], **to))
    for c in copies:
        c.start()
    for c in loads:
        c.wait()
    for c in copies:
        c.wait()
    own_feat = feat[...]
    total = own_feat.astype(F32) + part[:, mine].astype(F32)
    for r in range(n_grp - 1):
        total = total + got[r].astype(F32)
    agg = (total / divisor[...]).astype(BF16)
    both = jnp.concatenate([own_feat.reshape(rows, fw), agg.reshape(rows, fw)], axis=1)
    back = jnp.zeros((rows, 2 * fw), F32)
    grads = []
    for j in range(n_grp):
        pre = jnp.dot(both, w_all[j], preferred_element_type=F32)
        sig = jax.nn.sigmoid(pre)
        out_all[j] = (pre * sig).astype(BF16).reshape(n_blk, own, hid)
        cot = cot_all[j].reshape(rows, hid).astype(F32)
        grad = (cot * sig * (1.0 + pre * (1.0 - sig))).astype(BF16)
        grads.append(grad)
        back = back + lax.dot_general(grad, w_all[j], TRANS_B, preferred_element_type=F32)
    down = (back[:, fw:].reshape(n_blk, own, fw) / divisor[...]).astype(BF16)
    sent[...] = down
    for c in last:
        c.start()
    scaled[:, mine] = down
    base[...] = back[:, :fw].reshape(n_blk, own, fw) + down.astype(F32)
    for j in range(n_grp):
        gw = lax.dot_general(both, grads[j], TRANS_A, preferred_element_type=F32).astype(BF16)
        for h in range(hid // 128):
            wgrad[j, h] = gw[:, 128 * h:128 * (h + 1)]
    for c in last:
        c.wait()


def backward_exchange(x, n_grp, n_in, i0, i1, i2, i3, scaled, cols, out_all, wgrad, places, base_sum, whole, out, grads,
                      out_rows, live, in_rows, in_cols, i_sem, inner_terms, inner_sum, sent, stage, inbox, right_out, right_in, left_out, left_in, w_got, pieces, near_got, far_sent, far_got,
                      send, recv, rs, rr, ls, lr, o_s, o_r, w_s, w_r, a_s, a_r, b_s, b_r, c_s, c_r, d_s, d_r, e_s, e_r, loc):
    q, g = lax.axis_index("dom"), lax.axis_index("grp")
    layers, near, slots, own, fw = stage.shape
    n_blk = whole.shape[0]
    cut = n_blk // 2
    half = layers // 2
    z, k = q // near, q % near
    indices = load_indices((i0, i1, i2, i3), (out_rows, live, in_rows, in_cols), i_sem)
    n_out = layers * near * slots
    barrier = pltpu.get_barrier_semaphore()
    signal_group(q, g, n_grp)(barrier)
    signal_ring(q, g, near, layers)(barrier)
    mine = pl.ds(pl.multiple_of(g * own, own), own)
    keep = pltpu.make_async_copy(out_all.at[g], out.at[:, mine], loc)
    keep.start()
    far, grad_far, last = [], [], []
    for r in range(1, n_grp):
        y = (g + r) % n_grp
        to = dict(device_id=(q, y), device_id_type=MESH)
        last.append(pltpu.make_async_remote_copy(
            src_ref=sent, dst_ref=whole.at[:, mine], send_sem=e_s.at[r - 1], recv_sem=e_r.at[r - 1], **to))
        far.append(pltpu.make_async_remote_copy(
            src_ref=out_all.at[y], dst_ref=out.at[:, mine], send_sem=o_s.at[r - 1], recv_sem=o_r.at[r - 1], **to))
        grad_far.append(pltpu.make_async_remote_copy(
            src_ref=wgrad.at[y], dst_ref=w_got.at[r - 1], send_sem=w_s.at[r - 1], recv_sem=w_r.at[r - 1], **to))

    def to_near(d, r):
        to = (k + r) % near
        return pltpu.make_async_remote_copy(
            src_ref=stage.at[d, to], dst_ref=inbox.at[d, k], send_sem=send.at[d, r], recv_sem=recv.at[d, r],
            device_id=(z * near + to, g), device_id_type=MESH)

    def own_term(d):
        return pltpu.make_async_copy(stage.at[d, k], inbox.at[d, k], recv.at[d, 0])

    def products(d):
        base = (z + d) % layers * near

        group = max(1, near // 2)

        @pl.loop(0, near // group)
        def _(r):
            value = []
            for u in range(group):
                for s in range(slots):
                    n = (base + r * group + u) * slots + s
                    value.append(jnp.dot(cols[n], scaled[out_rows[0, n]], preferred_element_type=F32))
            for u in range(group):
                to = r * group + u
                for s in range(slots):
                    stage[d, to, s] = jnp.where(s < live[0, base + to], value[u * slots + s], 0.0).astype(BF16)

    def ship(d):
        own_term(d).start()
        each(1, near, functools.partial(to_near, d), start)

    def reduce(d):
        own_term(d).wait()
        each(1, near, functools.partial(to_near, d), wait)
        n = near * slots * own
        spot = places[(z + d) % layers]
        row = lax.broadcasted_iota(jnp.int32, (n_blk * own, 128), 0)
        hot = [jnp.where(row == spot[c:c + 1], 1.0, 0.0).astype(BF16) for c in range(pl.cdiv(n, 128))]
        hot = jnp.concatenate(hot, axis=1)[:, :n] if len(hot) > 1 else hot[0][:, :n]
        terms = inbox[d].reshape(n, fw)
        return jnp.dot(hot, terms, preferred_element_type=F32).reshape(n_blk, own, fw)

    def ring(i, to_right):
        count = cut if i == 0 else n_blk
        held, lands, s_sem, r_sem, step = (right_out, right_in, rs, rr, 1) if to_right else (left_out, left_in, ls, lr, layers - 1)
        return pltpu.make_async_remote_copy(
            src_ref=held.at[i, pl.ds(0, count)], dst_ref=lands.at[i, pl.ds(0, count)], send_sem=s_sem.at[i], recv_sem=r_sem.at[i],
            device_id=((z + step) % layers * near + k, g), device_id_type=MESH)

    def with_right(i, value):
        ring(i, True).wait()
        if i == 0:
            return jnp.concatenate([value[:cut] + right_in[0, :cut].astype(F32), value[cut:]], axis=0)
        return value + right_in[i].astype(F32)

    def with_left(i, value):
        ring(i, False).wait()
        if i == 0:
            return jnp.concatenate([value[:cut], value[cut:] + left_in[0, :cut].astype(F32)], axis=0)
        return value + left_in[i].astype(F32)

    def near_reduce(r):
        to = (k + r) % near
        return pltpu.make_async_remote_copy(
            src_ref=pieces.at[pl.ds(to * layers, layers)], dst_ref=near_got.at[r],
            send_sem=a_s.at[r], recv_sem=a_r.at[r], device_id=(z * near + to, g), device_id_type=MESH)

    def far_reduce(r):
        to = (z + r) % layers
        return pltpu.make_async_remote_copy(
            src_ref=far_sent.at[to], dst_ref=far_got.at[r],
            send_sem=b_s.at[r], recv_sem=b_r.at[r], device_id=(to * near + k, g), device_id_type=MESH)

    def far_gather(r):
        to = (z + r) % layers
        return pltpu.make_async_remote_copy(
            src_ref=grads.at[k * layers + z], dst_ref=grads.at[k * layers + z],
            send_sem=c_s.at[r], recv_sem=c_r.at[r], device_id=(to * near + k, g), device_id_type=MESH)

    def near_gather(r):
        to = (k + r) % near
        return pltpu.make_async_remote_copy(
            src_ref=grads.at[pl.ds(k * layers, layers)], dst_ref=grads.at[pl.ds(k * layers, layers)],
            send_sem=d_s.at[r], recv_sem=d_r.at[r], device_id=(z * near + to, g), device_id_type=MESH)

    def sum_grp():
        for c in grad_far:
            c.wait()
        halves = wgrad.shape[1]
        per = pieces.shape[0] // halves
        for h in range(halves):
            total = wgrad[g, h].astype(F32)
            for r in range(n_grp - 1):
                total = total + w_got[r, h].astype(F32)
            pieces[h * per:(h + 1) * per] = total.reshape(per, pieces.shape[1], 128)
        each(1, near, near_reduce, start)

    def sum_near():
        each(1, near, near_reduce, wait)
        total = pieces[pl.ds(k * layers, layers)]
        for r in range(1, near):
            total = total + near_got[r]
        far_sent[...] = total
        each(1, layers, far_reduce, start)

    def sum_far():
        each(1, layers, far_reduce, wait)
        total = far_sent[z]
        for r in range(1, layers):
            total = total + far_got[r]
        grads[k * layers + z] = total
        each(1, layers, far_gather, start)

    def spread():
        each(1, layers, far_gather, wait)
        each(1, near, near_gather, start)

    def inner():
        per = 128 // own
        step = 4 * per

        @pl.loop(0, n_in // 8)
        def _(m):
            value = [jnp.dot(cols[n_out + m * 8 + u], scaled[in_rows[0, m * 8 + u]], preferred_element_type=F32) for u in range(8)]
            for u in range(8):
                inner_terms[m * 8 + u] = value[u].astype(BF16)

        lane = lax.broadcasted_iota(jnp.int32, (1, 128), 1)
        row = lax.broadcasted_iota(jnp.int32, (n_blk * own, 128), 0)
        inner_sum[...] = base_sum[...]

        def add(m, count):
            hot = []
            for c in range(count):
                spot = lane
                for u in range(per):
                    target = in_cols[0, m * step + c * per + u]
                    spot = jnp.where(lane // own == u, lane + (target - u) * own, spot)
                hot.append(jnp.where(row == spot, 1.0, 0.0).astype(BF16))
            hot = jnp.concatenate(hot, axis=1) if count > 1 else hot[0]
            terms = inner_terms[pl.ds(m * step, count * per)].reshape(count * per * own, fw)
            inner_sum[...] += jnp.dot(hot, terms, preferred_element_type=F32).reshape(n_blk, own, fw)

        if n_in % step:
            for m in range(n_in // step):
                add(m, 4)
            add(n_in // step, n_in % step // per)
        else:
            @pl.loop(0, n_in // step)
            def _(m):
                add(m, 4)

    for c in indices:
        c.wait()
    products(half)
    pl.semaphore_wait(barrier, n_grp - 1 + near - 1 + layers - 1)
    for c in grad_far:
        c.start()
    ship(half)
    for i in range(half):
        d = half - i
        if d > 1:
            for e in (d - 1, layers - d + 1):
                products(e)
                ship(e)
        else:
            products(0)
            ship(0)
        if i == 0:
            value = reduce(half)
            right_out[0, :cut] = value[:cut].astype(BF16)
            left_out[0, :cut] = value[cut:].astype(BF16)
        else:
            right_out[i] = with_right(i - 1, reduce(d)).astype(BF16)
            left_out[i] = with_left(i - 1, reduce(layers - d)).astype(BF16)
        ring(i, True).start()
        ring(i, False).start()
        if i == 0:
            inner()
            sum_grp()
            for c in far:
                c.start()
        if i == min(2, half - 1):
            sum_near()
    value = reduce(0) + inner_sum[...]
    sum_far()
    value = with_left(half - 1, with_right(half - 1, value)).astype(BF16)
    sent[...] = value
    for c in last:
        c.start()
    whole[:, mine] = value
    spread()
    keep.wait()
    for c in far:
        c.wait()
    each(1, near, near_gather, wait)
    for c in last:
        c.wait()


def results_kernel(whole, pieces, out_parts, feature_grad, self_grad, neigh_grad, out, wide, sem):
    keep = pltpu.make_async_copy(out_parts, out, sem.at[0])
    keep.start()
    wide[...] = whole[...].astype(F32)
    keep_too = pltpu.make_async_copy(wide, feature_grad, sem.at[1])
    keep_too.start()
    fw = self_grad.shape[0]
    halves = self_grad.shape[1] // 128
    per, depth = pieces.shape[0] // (2 * halves), pieces.shape[1]
    for h in range(halves):
        for m, to in enumerate((self_grad, neigh_grad)):
            at = (2 * h + m) * per
            to[:, 128 * h:128 * (h + 1)] = pieces[at:at + per].reshape(fw, 128)
    keep.wait()
    keep_too.wait()


def params(collective=None, vmem=48):
    if collective is None:
        return pltpu.CompilerParams(vmem_limit_bytes=vmem << 20)
    return pltpu.CompilerParams(vmem_limit_bytes=vmem << 20, collective_id=collective, has_side_effects=True)


def shards(features, w_self, w_neigh, cotangent, inner_rows, inner_cols, inner_values, send_blocks, outer_rows, outer_values, live_count):
    blk = inner_values.shape[-1]
    nodes, fw = features.shape
    n_blk = nodes // blk
    parts, n_grp = lax.axis_size("dom"), lax.axis_size("grp")
    x = x_extent(parts)
    near = 2 * x
    layers = parts // near
    n_src = parts // n_grp
    slots = send_blocks.shape[-1]
    hid = w_self.shape[1]
    own = blk // n_grp
    n_in, n_out = inner_values.shape[1], outer_values.shape[1]
    n_all = n_in + n_out
    inner, outer = inner_values[0], outer_values[0]
    feat = features.reshape(n_blk, blk, fw)
    dma, sds = pltpu.SemaphoreType.DMA, jax.ShapeDtypeStruct
    vm = pltpu.VMEM
    block = (n_src, slots, blk, fw)
    indices = (outer_rows, live_count, inner_rows, inner_cols)
    index_room = [pltpu.SMEM(a.shape, jnp.int32) for a in indices] + [dma((4,))]
    mine = (n_blk, own, fw)
    y_sem = dma((n_grp - 1,))

    inc, cot_all, w_all, place_all, cols, divisor, own_feat = pl.pallas_call(
        functools.partial(forward_exchange, x, n_src, n_grp),
        out_shape=(sds(block, BF16), sds((n_grp, n_blk, own, hid), BF16), sds((n_grp, 2 * fw, hid), BF16), sds((layers, 8, 128), jnp.int32),
                   sds((n_all, own, blk), BF16), sds(mine, F32), sds(mine, BF16)),
        in_specs=[HB] * 10,
        out_specs=(ANY,) * 7,
        scratch_shapes=[vm((n_blk, blk, fw), BF16), vm(block, BF16), vm((n_all, blk, blk), BF16), vm((n_all, blk), F32),
                        vm((layers, 8, 128), jnp.int32), vm((1, n_out), jnp.int32), vm((1, n_in), jnp.int32), vm((1, parts), jnp.int32), vm((n_all, own, blk), BF16), vm(mine, F32), pltpu.SMEM((parts, slots), jnp.int32),
                        dma((n_src,)), dma((n_src,)), y_sem, y_sem, dma((n_grp - 1, 2)), dma((n_grp - 1, 2)),
                        dma((layers,)), dma((layers,)), dma((14,))],
        compiler_params=params(0, 62), name="forward_exchange",
    )(send_blocks[0], outer_rows, inner_rows, live_count, feat, cotangent.reshape(n_blk, blk, hid), w_self, w_neigh, inner, outer)

    part = pl.pallas_call(
        functools.partial(aggregate_kernel, x, n_src, n_grp),
        out_shape=sds((n_blk, blk, fw), BF16),
        in_specs=[HB] * 5 + [ANY, HB, HB],
        out_specs=VM,
        scratch_shapes=index_room + [vm((n_blk, blk, fw), BF16), vm((n_blk, blk, fw), F32), vm((n_in // n_grp, blk, blk), BF16),
                        vm((n_src, slots, blk, blk), BF16), vm(block, BF16), dma, dma, dma, dma],
        compiler_params=params(None, 62), name="aggregate",
    )(*indices, feat, inc, inner, outer)

    halves = hid // 128
    out_all, scaled, base, wgrad = pl.pallas_call(
        functools.partial(dense_kernel, n_grp),
        out_shape=(sds((n_grp, n_blk, own, hid), BF16), sds((n_blk, blk, fw), BF16), sds(mine, F32), sds((n_grp, halves, 2 * fw, 128), BF16)),
        in_specs=[VM, VM, VM, ANY, ANY],
        out_specs=(VM,) * 4,
        scratch_shapes=[vm((n_grp, n_blk, own, hid), BF16), vm((n_grp, 2 * fw, hid), BF16),
                        vm((n_grp - 1,) + mine, BF16), vm(mine, BF16), y_sem, y_sem, y_sem, y_sem, dma((3,))],
        compiler_params=params(1), name="dense",
    )(part, own_feat, divisor, cot_all, w_all)

    depth = halves * 2 * fw // parts
    half = layers // 2
    near_sem, far_sem = dma((near,)), dma((layers,))
    whole, out_parts, grads = pl.pallas_call(
        functools.partial(backward_exchange, x, n_grp, n_in),
        out_shape=(sds((n_blk, blk, fw), BF16), sds((n_blk, blk, hid), BF16), sds((parts, depth, 128), F32)),
        in_specs=[HB] * 4 + [VM, VM, ANY, VM, VM, VM],
        out_specs=(VM, ANY, VM),
        scratch_shapes=index_room + [vm((n_in, own, fw), BF16), vm(mine, F32), vm(mine, BF16), vm((layers, near, slots, own, fw), BF16), vm((layers, near, slots, own, fw), BF16)]
        + [vm((half,) + mine, BF16)] * 4
        + [vm((n_grp - 1, halves, 2 * fw, 128), BF16), vm((parts, depth, 128), F32), vm((near, layers, depth, 128), F32),
           vm((layers, depth, 128), F32), vm((layers, depth, 128), F32)]
        + [dma((layers, near))] * 2 + [dma((half,))] * 4 + [y_sem] * 4
        + [near_sem] * 2 + [far_sem] * 4 + [near_sem] * 2 + [y_sem] * 2 + [dma],
        compiler_params=params(2), name="backward_exchange",
    )(*indices, scaled, cols, out_all, wgrad, place_all, base)

    feature_grad, self_grad, neigh_grad, layer_out = pl.pallas_call(
        results_kernel,
        out_shape=(sds((n_blk, blk, fw), F32), sds((fw, hid), F32), sds((fw, hid), F32), sds((n_blk, blk, hid), BF16)),
        in_specs=[VM, VM, ANY],
        out_specs=(ANY, VM, VM, ANY),
        scratch_shapes=[vm((n_blk, blk, fw), F32), dma((2,))],
        compiler_params=params(), name="results",
    )(whole, grads, out_parts)
    return layer_out.reshape(nodes, hid), feature_grad.reshape(nodes, fw), self_grad, neigh_grad


def solution(mesh):
    placed = (
        P("dom", None),
        P(None, "grp"),
        P(None, "grp"),
        P("dom", "grp"),
        P("dom", None),
        P("dom", None),
        P("dom", None, None, None),
        P("dom", None, None),
        P("dom", None),
        P("dom", None, None, None),
        P("dom", None),
    )
    return jax.shard_map(
        shards,
        mesh=mesh,
        in_specs=placed,
        out_specs=(P("dom", "grp"), P("dom", None), P(None, "grp"), P(None, "grp")),
        check_vma=False,
    )
```

```python
import functools

import jax
import jax.numpy as jnp
from jax import lax
from jax.experimental import pallas as pl
from jax.experimental.pallas import tpu as pltpu
from jax.sharding import PartitionSpec as P

MESH = pl.DeviceIdType.MESH
ANY = pl.BlockSpec(memory_space=pl.ANY)
VM = pl.BlockSpec(memory_space=pltpu.VMEM)
SM = pl.BlockSpec(memory_space=pltpu.SMEM)
HB = pl.BlockSpec(memory_space=pltpu.HBM)
F32 = jnp.float32
BF16 = jnp.bfloat16
TRANS_A = (((0,), (0,)), ((), ()))
TRANS_B = (((1,), (1,)), ((), ()))


def x_extent(parts):
    return 4 if parts == 64 else 1


def plane_peer(i, q, g, x):
    z = q // (2 * x)
    return (((i // x) * 2 + (z + g // 2) % 2) * x + i % x) * 2 + (q + g) % 2


def plane_slot(q, x):
    return (q // (4 * x)) * x + (q // 2) % x


def enter(peers, count):
    barrier = pltpu.get_barrier_semaphore()
    for peer in peers:
        peer(barrier)
    pl.semaphore_wait(barrier, count)


def signal_plane(q, g, x, n_src):
    slot = plane_slot(q, x)

    def go(barrier):
        @pl.when(g != 0)
        def _():
            pl.semaphore_signal(barrier, inc=1, device_id=(plane_peer(slot, q, g, x), g), device_id_type=MESH)

        @pl.loop(1, n_src)
        def _(i):
            peer = plane_peer((slot + i) % n_src, q, g, x)
            pl.semaphore_signal(barrier, inc=1, device_id=(peer, g), device_id_type=MESH)

    return go


def signal_group(q, g, n_grp):
    def go(barrier):
        for r in range(1, n_grp):
            pl.semaphore_signal(barrier, inc=1, device_id=(q, (g + r) % n_grp), device_id_type=MESH)

    return go


def load_indices(arrays, copies, sem):
    loads = [pltpu.make_async_copy(a, b, sem.at[n]) for n, (a, b) in enumerate(zip(arrays, copies))]
    for c in loads:
        c.start()
    return loads


def signal_ring(q, g, near, layers):
    z, k = q // near, q % near

    def go(barrier):
        @pl.loop(1, near)
        def _(r):
            pl.semaphore_signal(barrier, inc=1, device_id=(z * near + (k + r) % near, g), device_id_type=MESH)

        @pl.loop(1, layers)
        def _(r):
            pl.semaphore_signal(barrier, inc=1, device_id=((z + r) % layers * near + k, g), device_id_type=MESH)

    return go


def each(first, count, make, act):
    @pl.loop(first, count)
    def _(r):
        act(make(r))


def start(c):
    c.start()


def wait(c):
    c.wait()


def forward_exchange(x, n_src, n_grp, sends, rows_out, rows_in, live, features, cot, w_self, w_neigh, inner, outer,
                     inc, cot_all, w_all, place_all, cols_out, divisor_out, own_feat,
                     feat, stage, blocks, row_sums, places, key_out, key_in, key_live, cols, divisor, table, send, recv, cot_s, cot_r, w_s, w_r, p_s, p_r, loc):
    q, g = lax.axis_index("dom"), lax.axis_index("grp")
    slots = stage.shape[1]
    own = cot_all.shape[2]
    fw = w_self.shape[0]
    n_blk, blk, _ = feat.shape
    near = 2 * x
    layers = place_all.shape[0]
    z, k = q // near, q % near
    slot = plane_slot(q, x)
    n_out, n_in = outer.shape[0], inner.shape[0]
    barrier = pltpu.get_barrier_semaphore()
    load_feat = pltpu.make_async_copy(features, feat, loc.at[3])
    load_feat.start()
    load_sends = pltpu.make_async_copy(sends, table, loc.at[13])
    load_sends.start()
    signal_plane(q, g, x, n_src)(barrier)
    signal_group(q, g, n_grp)(barrier)

    @pl.loop(1, layers)
    def _(r):
        pl.semaphore_signal(barrier, inc=1, device_id=((z + r) % layers * near + k, g), device_id_type=MESH)

    mine = pl.ds(pl.multiple_of(g * own, own), own)
    local = [
        pltpu.make_async_copy(cot.at[:, mine], cot_all.at[g], loc.at[0]),
        pltpu.make_async_copy(w_self, w_all.at[g, pl.ds(0, fw)], loc.at[1]),
        pltpu.make_async_copy(w_neigh, w_all.at[g, pl.ds(fw, fw)], loc.at[2]),
        pltpu.make_async_copy(places.at[z], place_all.at[z], loc.at[6]),
        pltpu.make_async_copy(feat.at[:, mine], own_feat, loc.at[12]),
    ]
    small = [
        pltpu.make_async_copy(rows_out, key_out, loc.at[7]),
        pltpu.make_async_copy(rows_in, key_in, loc.at[8]),
        pltpu.make_async_copy(live, key_live, loc.at[9]),
    ]
    loads = [
        pltpu.make_async_copy(outer, blocks.at[pl.ds(0, n_out)], loc.at[4]),
        pltpu.make_async_copy(inner, blocks.at[pl.ds(n_out, n_in)], loc.at[5]),
    ]

    def fill(d):
        peer = plane_peer(d, q, g, x)
        for s in range(slots):
            stage[d, s] = feat[table[peer, s]]
        return peer

    def remote(d, peer):
        return pltpu.make_async_remote_copy(
            src_ref=stage.at[d], dst_ref=inc.at[slot], send_sem=send.at[d], recv_sem=recv.at[slot],
            device_id=(peer, g), device_id_type=MESH)

    def place(r):
        to = (z + r) % layers
        return pltpu.make_async_remote_copy(
            src_ref=places.at[to], dst_ref=place_all.at[z], send_sem=p_s.at[r], recv_sem=p_r.at[r],
            device_id=(to * near + k, g), device_id_type=MESH)

    load_sends.wait()
    load_feat.wait()
    home = fill(slot)
    others = n_grp - 1 + layers - 1

    @pl.when(g == 0)
    def _():
        pl.semaphore_wait(barrier, n_src - 1 + others)

    @pl.when(g != 0)
    def _():
        pl.semaphore_wait(barrier, n_src + others)

    far = []
    for r in range(1, n_grp):
        y = (g + r) % n_grp
        to = dict(device_id=(q, y), device_id_type=MESH)
        theirs = pl.ds(pl.multiple_of(y * own, own), own)
        far.append(pltpu.make_async_remote_copy(
            src_ref=cot.at[:, theirs], dst_ref=cot_all.at[g],
            send_sem=cot_s.at[r - 1], recv_sem=cot_r.at[r - 1], **to))
        far.append(pltpu.make_async_remote_copy(
            src_ref=w_self, dst_ref=w_all.at[g, pl.ds(0, fw)],
            send_sem=w_s.at[r - 1, 0], recv_sem=w_r.at[r - 1, 0], **to))
        far.append(pltpu.make_async_remote_copy(
            src_ref=w_neigh, dst_ref=w_all.at[g, pl.ds(fw, fw)],
            send_sem=w_s.at[r - 1, 1], recv_sem=w_r.at[r - 1, 1], **to))

    @pl.when(g == 0)
    def _():
        pltpu.make_async_copy(stage.at[slot], inc.at[slot], recv.at[slot]).start()

    @pl.when(g != 0)
    def _():
        remote(slot, home).start()

    @pl.loop(1, n_src)
    def _(i):
        d = (slot + i) % n_src
        remote(d, fill(d)).start()

    for c in far + local[:3] + loads + small:
        c.start()

    per = 128 // own
    lane = lax.broadcasted_iota(jnp.int32, (1, 128), 1)

    @pl.loop(0, layers)
    def _(t):
        for c in range(pl.cdiv(near * slots, per)):
            spot = lane
            for u in range(per):
                if c * per + u < near * slots:
                    at = c * per + u
                    target = table[t * near + at // slots, at % slots]
                    spot = jnp.where(lane // own == u, lane + (target - u) * own, spot)
            places[t, c:c + 1, :] = spot

    local[3].start()
    local[4].start()
    each(1, layers, place, start)

    row = lax.broadcasted_iota(jnp.int32, (own + 16, blk), 0)
    lane = lax.broadcasted_iota(jnp.int32, (own + 16, blk), 1)
    pick = jnp.where((row == own) | (lane == row + g * own) & (row < own), 1.0, 0.0).astype(BF16)
    for c in loads:
        c.wait()

    @pl.loop(0, (n_out + n_in) // 8)
    def _(m):
        got = [lax.dot_general(pick, blocks[m * 8 + u], TRANS_B, preferred_element_type=F32) for u in range(8)]
        for u in range(8):
            cols[m * 8 + u] = got[u][:own].astype(BF16)
        row_sums[pl.ds(pl.multiple_of(m * 8, 8), 8), :] = jnp.concatenate([v[own:own + 1] for v in got], axis=0)

    keep = pltpu.make_async_copy(cols, cols_out, loc.at[10])
    keep.start()
    for c in small:
        c.wait()
    n_part = key_live.shape[1]
    first = slots * lax.broadcasted_iota(jnp.int32, (n_part, n_out), 0)
    at = lax.broadcasted_iota(jnp.int32, (n_part, n_out), 1) - first
    spread = jnp.where((at >= 0) & (at < slots), 1.0, 0.0)
    limit = jnp.dot(key_live[...].astype(F32), spread, precision=lax.Precision.HIGHEST, preferred_element_type=F32)
    index = jnp.sum(jnp.where((at >= 0) & (at < slots), at, 0), axis=0, keepdims=True)
    key = jnp.concatenate([jnp.where(index.astype(F32) < limit, key_out[...], n_blk), key_in[...]], axis=1)
    hits = jnp.where(lax.broadcasted_iota(jnp.int32, (n_blk, n_out + n_in), 0) == key, 1.0, 0.0)
    degree = 1.0 + jnp.dot(hits, row_sums[...], precision=lax.Precision.HIGHEST, preferred_element_type=F32)
    sel = (lax.broadcasted_iota(jnp.int32, (own, blk), 1) == lax.broadcasted_iota(jnp.int32, (own, blk), 0) + g * own)
    for b in range(n_blk):
        column = jnp.sum(jnp.where(sel, degree[b:b + 1], 0.0), axis=1, keepdims=True)
        divisor[b] = jnp.broadcast_to(column, (own, fw))

    keep_too = pltpu.make_async_copy(divisor, divisor_out, loc.at[11])
    keep_too.start()
    keep.wait()
    keep_too.wait()
    for c in local:
        c.wait()
    for c in far:
        c.wait()
    each(1, layers, place, wait)

    @pl.when(g != 0)
    def _():
        remote(slot, home).wait_send()

    @pl.loop(1, n_src)
    def _(i):
        d = (slot + i) % n_src
        remote(d, plane_peer(d, q, g, x)).wait_send()

    @pl.loop(0, n_src)
    def _(j):
        pltpu.make_async_copy(stage.at[j], inc.at[j], recv.at[j]).wait()


def aggregate_kernel(x, n_src, n_grp, i0, i1, i2, i3, features, inc, inner, outer, part, out_rows, live, in_rows, in_cols, i_sem, feat, acc, a_in, a_out, x_in, sem_f, sem_in, sem_out, sem_x):
    q, g = lax.axis_index("dom"), lax.axis_index("grp")
    slots = inc.shape[1]
    n_in = inner.shape[0] // n_grp
    indices = load_indices((i0, i1, i2, i3), (out_rows, live, in_rows, in_cols), i_sem)
    load_f = pltpu.make_async_copy(features, feat, sem_f)
    load_f.start()
    load_in = pltpu.make_async_copy(inner.at[pl.ds(g * n_in, n_in)], a_in, sem_in)
    load_in.start()
    load_x = pltpu.make_async_copy(inc, x_in, sem_x)
    load_x.start()

    def load(i):
        peer = plane_peer(i, q, g, x)
        return pltpu.make_async_copy(outer.at[pl.ds(peer * slots, slots)], a_out.at[i], sem_out)

    @pl.loop(0, n_src)
    def _(i):
        load(i).start()

    acc[...] = jnp.zeros_like(acc)
    for c in indices:
        c.wait()
    load_f.wait()
    load_in.wait()

    @pl.loop(0, n_in // 2)
    def _(m):
        value = [jnp.dot(a_in[m * 2 + u], feat[in_cols[0, g * n_in + m * 2 + u]], preferred_element_type=F32) for u in range(2)]
        for u in range(2):
            acc[in_rows[0, g * n_in + m * 2 + u]] += value[u]

    load_x.wait()
    pltpu.make_async_copy(a_out, a_out, sem_out).wait()

    @pl.loop(0, n_src)
    def _(i):
        peer = plane_peer(i, q, g, x)
        value = [jnp.dot(a_out[i, s], x_in[i, s], preferred_element_type=F32) for s in range(slots)]
        for s in range(slots):
            @pl.when(s < live[0, peer])
            def _(s=s):
                acc[out_rows[0, peer * slots + s]] += value[s]

    part[...] = acc[...].astype(BF16)


def dense_kernel(n_grp, part, feat, divisor, cots, ws, out_all, scaled, base, wgrad, cot_all, w_all, got, sent, s1, r1, s3, r3, loc):
    q, g = lax.axis_index("dom"), lax.axis_index("grp")
    n_blk, blk, fw = part.shape
    own = base.shape[1]
    hid = ws.shape[2]
    mine = pl.ds(pl.multiple_of(g * own, own), own)
    barrier = pltpu.get_barrier_semaphore()
    signal_group(q, g, n_grp)(barrier)
    loads = [
        pltpu.make_async_copy(ws, w_all, loc.at[1]),
        pltpu.make_async_copy(cots, cot_all, loc.at[2]),
    ]
    for c in loads:
        c.start()
    pl.semaphore_wait(barrier, n_grp - 1)
    cuts = 2
    step = n_blk // cuts
    copies, last = [[] for _ in range(cuts)], [[] for _ in range(cuts)]
    for h in range(cuts):
        part_h = pl.ds(h * step, step)
        for r in range(1, n_grp):
            y = (g + r) % n_grp
            to = dict(device_id=(q, y), device_id_type=MESH)
            theirs = pl.ds(pl.multiple_of(y * own, own), own)
            copies[h].append(pltpu.make_async_remote_copy(
                src_ref=part.at[part_h, theirs], dst_ref=got.at[r - 1, part_h], send_sem=s1.at[h, r - 1], recv_sem=r1.at[h, r - 1], **to))
            last[h].append(pltpu.make_async_remote_copy(
                src_ref=sent.at[part_h], dst_ref=scaled.at[part_h, mine], send_sem=s3.at[h, r - 1], recv_sem=r3.at[h, r - 1], **to))
    for h in range(cuts):
        for c in copies[h]:
            c.start()
    for c in loads:
        c.wait()
    rows = step * own
    both, grads = [], []
    for h in range(cuts):
        for c in copies[h]:
            c.wait()
        at = slice(h * step, (h + 1) * step)
        own_feat = feat[at]
        total = own_feat.astype(F32) + part[at, mine].astype(F32)
        for r in range(n_grp - 1):
            total = total + got[r, at].astype(F32)
        agg = (total / divisor[at]).astype(BF16)
        both.append(jnp.concatenate([own_feat.reshape(rows, fw), agg.reshape(rows, fw)], axis=1))
        back = jnp.zeros((rows, 2 * fw), F32)
        for j in range(n_grp):
            pre = jnp.dot(both[h], w_all[j], preferred_element_type=F32)
            sig = jax.nn.sigmoid(pre)
            out_all[j, at] = (pre * sig).astype(BF16).reshape(step, own, hid)
            cot = cot_all[j, at].reshape(rows, hid).astype(F32)
            grad = (cot * sig * (1.0 + pre * (1.0 - sig))).astype(BF16)
            grads.append(grad)
            back = back + lax.dot_general(grad, w_all[j], TRANS_B, preferred_element_type=F32)
        down = (back[:, fw:].reshape(step, own, fw) / divisor[at]).astype(BF16)
        sent[at] = down
        for c in last[h]:
            c.start()
        scaled[at, mine] = down
        base[at] = back[:, :fw].reshape(step, own, fw) + down.astype(F32)
    for j in range(n_grp):
        gw = sum(lax.dot_general(both[h], grads[h * n_grp + j], TRANS_A, preferred_element_type=F32) for h in range(cuts)).astype(BF16)
        for h in range(hid // 128):
            wgrad[j, h] = gw[:, 128 * h:128 * (h + 1)]
    for h in range(cuts):
        for c in last[h]:
            c.wait()


def backward_exchange(x, n_grp, n_in, i0, i1, i2, i3, scaled, cols, out_all, wgrad, places, base_sum, whole, out, grads,
                      out_rows, live, in_rows, in_cols, i_sem, inner_terms, inner_sum, sent, stage, inbox, right_out, right_in, left_out, left_in, w_got, pieces, near_got, far_sent, far_got,
                      send, recv, rs, rr, ls, lr, o_s, o_r, w_s, w_r, a_s, a_r, b_s, b_r, c_s, c_r, d_s, d_r, e_s, e_r, loc):
    q, g = lax.axis_index("dom"), lax.axis_index("grp")
    layers, near, slots, own, fw = stage.shape
    n_blk = whole.shape[0]
    cut = n_blk // 2
    half = layers // 2
    z, k = q // near, q % near
    indices = load_indices((i0, i1, i2, i3), (out_rows, live, in_rows, in_cols), i_sem)
    n_out = layers * near * slots
    barrier = pltpu.get_barrier_semaphore()
    signal_group(q, g, n_grp)(barrier)
    signal_ring(q, g, near, layers)(barrier)
    mine = pl.ds(pl.multiple_of(g * own, own), own)
    keep = pltpu.make_async_copy(out_all.at[g], out.at[:, mine], loc)
    keep.start()
    far, grad_far, last = [], [], []
    for r in range(1, n_grp):
        y = (g + r) % n_grp
        to = dict(device_id=(q, y), device_id_type=MESH)
        last.append(pltpu.make_async_remote_copy(
            src_ref=sent, dst_ref=whole.at[:, mine], send_sem=e_s.at[r - 1], recv_sem=e_r.at[r - 1], **to))
        far.append(pltpu.make_async_remote_copy(
            src_ref=out_all.at[y], dst_ref=out.at[:, mine], send_sem=o_s.at[r - 1], recv_sem=o_r.at[r - 1], **to))
        grad_far.append(pltpu.make_async_remote_copy(
            src_ref=wgrad.at[y], dst_ref=w_got.at[r - 1], send_sem=w_s.at[r - 1], recv_sem=w_r.at[r - 1], **to))

    def to_near(d, r):
        to = (k + r) % near
        return pltpu.make_async_remote_copy(
            src_ref=stage.at[d, to], dst_ref=inbox.at[d, k], send_sem=send.at[d, r], recv_sem=recv.at[d, r],
            device_id=(z * near + to, g), device_id_type=MESH)

    def own_term(d):
        return pltpu.make_async_copy(stage.at[d, k], inbox.at[d, k], recv.at[d, 0])

    def products(d):
        base = (z + d) % layers * near

        group = max(1, near // 2)

        @pl.loop(0, near // group)
        def _(r):
            value = []
            for u in range(group):
                for s in range(slots):
                    n = (base + r * group + u) * slots + s
                    value.append(jnp.dot(cols[n], scaled[out_rows[0, n]], preferred_element_type=F32))
            for u in range(group):
                to = r * group + u
                for s in range(slots):
                    stage[d, to, s] = jnp.where(s < live[0, base + to], value[u * slots + s], 0.0).astype(BF16)

    def ship(d):
        own_term(d).start()
        each(1, near, functools.partial(to_near, d), start)

    def reduce(d):
        own_term(d).wait()
        each(1, near, functools.partial(to_near, d), wait)
        n = near * slots * own
        spot = places[(z + d) % layers]
        row = lax.broadcasted_iota(jnp.int32, (n_blk * own, 128), 0)
        hot = [jnp.where(row == spot[c:c + 1], 1.0, 0.0).astype(BF16) for c in range(pl.cdiv(n, 128))]
        hot = jnp.concatenate(hot, axis=1)[:, :n] if len(hot) > 1 else hot[0][:, :n]
        terms = inbox[d].reshape(n, fw)
        return jnp.dot(hot, terms, preferred_element_type=F32).reshape(n_blk, own, fw)

    def ring(i, to_right):
        count = cut if i == 0 else n_blk
        held, lands, s_sem, r_sem, step = (right_out, right_in, rs, rr, 1) if to_right else (left_out, left_in, ls, lr, layers - 1)
        return pltpu.make_async_remote_copy(
            src_ref=held.at[i, pl.ds(0, count)], dst_ref=lands.at[i, pl.ds(0, count)], send_sem=s_sem.at[i], recv_sem=r_sem.at[i],
            device_id=((z + step) % layers * near + k, g), device_id_type=MESH)

    def with_right(i, value):
        ring(i, True).wait()
        if i == 0:
            return jnp.concatenate([value[:cut] + right_in[0, :cut].astype(F32), value[cut:]], axis=0)
        return value + right_in[i].astype(F32)

    def with_left(i, value):
        ring(i, False).wait()
        if i == 0:
            return jnp.concatenate([value[:cut], value[cut:] + left_in[0, :cut].astype(F32)], axis=0)
        return value + left_in[i].astype(F32)

    def near_reduce(r):
        to = (k + r) % near
        return pltpu.make_async_remote_copy(
            src_ref=pieces.at[pl.ds(to * layers, layers)], dst_ref=near_got.at[r],
            send_sem=a_s.at[r], recv_sem=a_r.at[r], device_id=(z * near + to, g), device_id_type=MESH)

    def far_reduce(r):
        to = (z + r) % layers
        return pltpu.make_async_remote_copy(
            src_ref=far_sent.at[to], dst_ref=far_got.at[r],
            send_sem=b_s.at[r], recv_sem=b_r.at[r], device_id=(to * near + k, g), device_id_type=MESH)

    def far_gather(r):
        to = (z + r) % layers
        return pltpu.make_async_remote_copy(
            src_ref=grads.at[k * layers + z], dst_ref=grads.at[k * layers + z],
            send_sem=c_s.at[r], recv_sem=c_r.at[r], device_id=(to * near + k, g), device_id_type=MESH)

    def near_gather(r):
        to = (k + r) % near
        return pltpu.make_async_remote_copy(
            src_ref=grads.at[pl.ds(k * layers, layers)], dst_ref=grads.at[pl.ds(k * layers, layers)],
            send_sem=d_s.at[r], recv_sem=d_r.at[r], device_id=(z * near + to, g), device_id_type=MESH)

    def sum_grp():
        for c in grad_far:
            c.wait()
        halves = wgrad.shape[1]
        per = pieces.shape[0] // halves
        for h in range(halves):
            total = wgrad[g, h].astype(F32)
            for r in range(n_grp - 1):
                total = total + w_got[r, h].astype(F32)
            pieces[h * per:(h + 1) * per] = total.reshape(per, pieces.shape[1], 128)
        each(1, near, near_reduce, start)

    def sum_near():
        each(1, near, near_reduce, wait)
        total = pieces[pl.ds(k * layers, layers)]
        for r in range(1, near):
            total = total + near_got[r]
        far_sent[...] = total
        each(1, layers, far_reduce, start)

    def sum_far():
        each(1, layers, far_reduce, wait)
        total = far_sent[z]
        for r in range(1, layers):
            total = total + far_got[r]
        grads[k * layers + z] = total
        each(1, layers, far_gather, start)

    def spread():
        each(1, layers, far_gather, wait)
        each(1, near, near_gather, start)

    def inner():
        per = 128 // own
        step = 4 * per

        @pl.loop(0, n_in // 8)
        def _(m):
            value = [jnp.dot(cols[n_out + m * 8 + u], scaled[in_rows[0, m * 8 + u]], preferred_element_type=F32) for u in range(8)]
            for u in range(8):
                inner_terms[m * 8 + u] = value[u].astype(BF16)

        lane = lax.broadcasted_iota(jnp.int32, (1, 128), 1)
        row = lax.broadcasted_iota(jnp.int32, (n_blk * own, 128), 0)
        inner_sum[...] = base_sum[...]

        def add(m, count):
            hot = []
            for c in range(count):
                spot = lane
                for u in range(per):
                    target = in_cols[0, m * step + c * per + u]
                    spot = jnp.where(lane // own == u, lane + (target - u) * own, spot)
                hot.append(jnp.where(row == spot, 1.0, 0.0).astype(BF16))
            hot = jnp.concatenate(hot, axis=1) if count > 1 else hot[0]
            terms = inner_terms[pl.ds(m * step, count * per)].reshape(count * per * own, fw)
            inner_sum[...] += jnp.dot(hot, terms, preferred_element_type=F32).reshape(n_blk, own, fw)

        if n_in % step:
            for m in range(n_in // step):
                add(m, 4)
            add(n_in // step, n_in % step // per)
        else:
            @pl.loop(0, n_in // step)
            def _(m):
                add(m, 4)

    for c in indices:
        c.wait()
    products(half)
    pl.semaphore_wait(barrier, n_grp - 1 + near - 1 + layers - 1)
    for c in grad_far:
        c.start()
    ship(half)
    for i in range(half):
        d = half - i
        if d > 1:
            for e in (d - 1, layers - d + 1):
                products(e)
                ship(e)
        else:
            products(0)
            ship(0)
        if i == 0:
            value = reduce(half)
            right_out[0, :cut] = value[:cut].astype(BF16)
            left_out[0, :cut] = value[cut:].astype(BF16)
        else:
            right_out[i] = with_right(i - 1, reduce(d)).astype(BF16)
            left_out[i] = with_left(i - 1, reduce(layers - d)).astype(BF16)
        ring(i, True).start()
        ring(i, False).start()
        if i == 0:
            inner()
            sum_grp()
            for c in far:
                c.start()
        if i == min(2, half - 1):
            sum_near()
    value = reduce(0) + inner_sum[...]
    sum_far()
    value = with_left(half - 1, with_right(half - 1, value)).astype(BF16)
    sent[...] = value
    for c in last:
        c.start()
    whole[:, mine] = value
    spread()
    keep.wait()
    for c in far:
        c.wait()
    each(1, near, near_gather, wait)
    for c in last:
        c.wait()


def results_kernel(whole, pieces, out_parts, feature_grad, self_grad, neigh_grad, out, wide, sem):
    keep = pltpu.make_async_copy(out_parts, out, sem.at[0])
    keep.start()
    wide[...] = whole[...].astype(F32)
    keep_too = pltpu.make_async_copy(wide, feature_grad, sem.at[1])
    keep_too.start()
    fw = self_grad.shape[0]
    halves = self_grad.shape[1] // 128
    per, depth = pieces.shape[0] // (2 * halves), pieces.shape[1]
    for h in range(halves):
        for m, to in enumerate((self_grad, neigh_grad)):
            at = (2 * h + m) * per
            to[:, 128 * h:128 * (h + 1)] = pieces[at:at + per].reshape(fw, 128)
    keep.wait()
    keep_too.wait()


def params(collective=None, vmem=48):
    if collective is None:
        return pltpu.CompilerParams(vmem_limit_bytes=vmem << 20)
    return pltpu.CompilerParams(vmem_limit_bytes=vmem << 20, collective_id=collective, has_side_effects=True)


def shards(features, w_self, w_neigh, cotangent, inner_rows, inner_cols, inner_values, send_blocks, outer_rows, outer_values, live_count):
    blk = inner_values.shape[-1]
    nodes, fw = features.shape
    n_blk = nodes // blk
    parts, n_grp = lax.axis_size("dom"), lax.axis_size("grp")
    x = x_extent(parts)
    near = 2 * x
    layers = parts // near
    n_src = parts // n_grp
    slots = send_blocks.shape[-1]
    hid = w_self.shape[1]
    own = blk // n_grp
    n_in, n_out = inner_values.shape[1], outer_values.shape[1]
    n_all = n_in + n_out
    inner, outer = inner_values[0], outer_values[0]
    feat = features.reshape(n_blk, blk, fw)
    dma, sds = pltpu.SemaphoreType.DMA, jax.ShapeDtypeStruct
    vm = pltpu.VMEM
    block = (n_src, slots, blk, fw)
    indices = (outer_rows, live_count, inner_rows, inner_cols)
    index_room = [pltpu.SMEM(a.shape, jnp.int32) for a in indices] + [dma((4,))]
    mine = (n_blk, own, fw)
    y_sem = dma((n_grp - 1,))

    inc, cot_all, w_all, place_all, cols, divisor, own_feat = pl.pallas_call(
        functools.partial(forward_exchange, x, n_src, n_grp),
        out_shape=(sds(block, BF16), sds((n_grp, n_blk, own, hid), BF16), sds((n_grp, 2 * fw, hid), BF16), sds((layers, 8, 128), jnp.int32),
                   sds((n_all, own, blk), BF16), sds(mine, F32), sds(mine, BF16)),
        in_specs=[HB] * 10,
        out_specs=(ANY,) * 7,
        scratch_shapes=[vm((n_blk, blk, fw), BF16), vm(block, BF16), vm((n_all, blk, blk), BF16), vm((n_all, blk), F32),
                        vm((layers, 8, 128), jnp.int32), vm((1, n_out), jnp.int32), vm((1, n_in), jnp.int32), vm((1, parts), jnp.int32), vm((n_all, own, blk), BF16), vm(mine, F32), pltpu.SMEM((parts, slots), jnp.int32),
                        dma((n_src,)), dma((n_src,)), y_sem, y_sem, dma((n_grp - 1, 2)), dma((n_grp - 1, 2)),
                        dma((layers,)), dma((layers,)), dma((14,))],
        compiler_params=params(0, 62), name="forward_exchange",
    )(send_blocks[0], outer_rows, inner_rows, live_count, feat, cotangent.reshape(n_blk, blk, hid), w_self, w_neigh, inner, outer)

    part = pl.pallas_call(
        functools.partial(aggregate_kernel, x, n_src, n_grp),
        out_shape=sds((n_blk, blk, fw), BF16),
        in_specs=[HB] * 5 + [ANY, HB, HB],
        out_specs=VM,
        scratch_shapes=index_room + [vm((n_blk, blk, fw), BF16), vm((n_blk, blk, fw), F32), vm((n_in // n_grp, blk, blk), BF16),
                        vm((n_src, slots, blk, blk), BF16), vm(block, BF16), dma, dma, dma, dma],
        compiler_params=params(None, 62), name="aggregate",
    )(*indices, feat, inc, inner, outer)

    halves = hid // 128
    out_all, scaled, base, wgrad = pl.pallas_call(
        functools.partial(dense_kernel, n_grp),
        out_shape=(sds((n_grp, n_blk, own, hid), BF16), sds((n_blk, blk, fw), BF16), sds(mine, F32), sds((n_grp, halves, 2 * fw, 128), BF16)),
        in_specs=[VM, VM, VM, ANY, ANY],
        out_specs=(VM,) * 4,
        scratch_shapes=[vm((n_grp, n_blk, own, hid), BF16), vm((n_grp, 2 * fw, hid), BF16),
                        vm((n_grp - 1,) + mine, BF16), vm(mine, BF16)] + [dma((2, n_grp - 1))] * 4 + [dma((3,))],
        compiler_params=params(1), name="dense",
    )(part, own_feat, divisor, cot_all, w_all)

    depth = halves * 2 * fw // parts
    half = layers // 2
    near_sem, far_sem = dma((near,)), dma((layers,))
    whole, out_parts, grads = pl.pallas_call(
        functools.partial(backward_exchange, x, n_grp, n_in),
        out_shape=(sds((n_blk, blk, fw), BF16), sds((n_blk, blk, hid), BF16), sds((parts, depth, 128), F32)),
        in_specs=[HB] * 4 + [VM, VM, ANY, VM, VM, VM],
        out_specs=(VM, ANY, VM),
        scratch_shapes=index_room + [vm((n_in, own, fw), BF16), vm(mine, F32), vm(mine, BF16), vm((layers, near, slots, own, fw), BF16), vm((layers, near, slots, own, fw), BF16)]
        + [vm((half,) + mine, BF16)] * 4
        + [vm((n_grp - 1, halves, 2 * fw, 128), BF16), vm((parts, depth, 128), F32), vm((near, layers, depth, 128), F32),
           vm((layers, depth, 128), F32), vm((layers, depth, 128), F32)]
        + [dma((layers, near))] * 2 + [dma((half,))] * 4 + [y_sem] * 4
        + [near_sem] * 2 + [far_sem] * 4 + [near_sem] * 2 + [y_sem] * 2 + [dma],
        compiler_params=params(2), name="backward_exchange",
    )(*indices, scaled, cols, out_all, wgrad, place_all, base)

    feature_grad, self_grad, neigh_grad, layer_out = pl.pallas_call(
        results_kernel,
        out_shape=(sds((n_blk, blk, fw), F32), sds((fw, hid), F32), sds((fw, hid), F32), sds((n_blk, blk, hid), BF16)),
        in_specs=[VM, VM, ANY],
        out_specs=(ANY, VM, VM, ANY),
        scratch_shapes=[vm((n_blk, blk, fw), F32), dma((2,))],
        compiler_params=params(), name="results",
    )(whole, grads, out_parts)
    return layer_out.reshape(nodes, hid), feature_grad.reshape(nodes, fw), self_grad, neigh_grad


def solution(mesh):
    placed = (
        P("dom", None),
        P(None, "grp"),
        P(None, "grp"),
        P("dom", "grp"),
        P("dom", None),
        P("dom", None),
        P("dom", None, None, None),
        P("dom", None, None),
        P("dom", None),
        P("dom", None, None, None),
        P("dom", None),
    )
    return jax.shard_map(
        shards,
        mesh=mesh,
        in_specs=placed,
        out_specs=(P("dom", "grp"), P("dom", None), P(None, "grp"), P(None, "grp")),
        check_vma=False,
    )
```

```python
import functools

import jax
import jax.numpy as jnp
from jax import lax
from jax.experimental import pallas as pl
from jax.experimental.pallas import tpu as pltpu
from jax.sharding import PartitionSpec as P

MESH = pl.DeviceIdType.MESH
ANY = pl.BlockSpec(memory_space=pl.ANY)
VM = pl.BlockSpec(memory_space=pltpu.VMEM)
SM = pl.BlockSpec(memory_space=pltpu.SMEM)
HB = pl.BlockSpec(memory_space=pltpu.HBM)
F32 = jnp.float32
BF16 = jnp.bfloat16
TRANS_A = (((0,), (0,)), ((), ()))
TRANS_B = (((1,), (1,)), ((), ()))


def x_extent(parts):
    return 4 if parts == 64 else 1


def plane_peer(i, q, g, x):
    z = q // (2 * x)
    return (((i // x) * 2 + (z + g // 2) % 2) * x + i % x) * 2 + (q + g) % 2


def plane_slot(q, x):
    return (q // (4 * x)) * x + (q // 2) % x


def enter(peers, count):
    barrier = pltpu.get_barrier_semaphore()
    for peer in peers:
        peer(barrier)
    pl.semaphore_wait(barrier, count)


def signal_plane(q, g, x, n_src):
    slot = plane_slot(q, x)

    def go(barrier):
        @pl.when(g != 0)
        def _():
            pl.semaphore_signal(barrier, inc=1, device_id=(plane_peer(slot, q, g, x), g), device_id_type=MESH)

        @pl.loop(1, n_src)
        def _(i):
            peer = plane_peer((slot + i) % n_src, q, g, x)
            pl.semaphore_signal(barrier, inc=1, device_id=(peer, g), device_id_type=MESH)

    return go


def signal_group(q, g, n_grp):
    def go(barrier):
        for r in range(1, n_grp):
            pl.semaphore_signal(barrier, inc=1, device_id=(q, (g + r) % n_grp), device_id_type=MESH)

    return go


def load_indices(arrays, copies, sem):
    loads = [pltpu.make_async_copy(a, b, sem.at[n]) for n, (a, b) in enumerate(zip(arrays, copies))]
    for c in loads:
        c.start()
    return loads


def signal_ring(q, g, near, layers):
    z, k = q // near, q % near

    def go(barrier):
        @pl.loop(1, near)
        def _(r):
            pl.semaphore_signal(barrier, inc=1, device_id=(z * near + (k + r) % near, g), device_id_type=MESH)

        @pl.loop(1, layers)
        def _(r):
            pl.semaphore_signal(barrier, inc=1, device_id=((z + r) % layers * near + k, g), device_id_type=MESH)

    return go


def each(first, count, make, act):
    @pl.loop(first, count)
    def _(r):
        act(make(r))


def start(c):
    c.start()


def wait(c):
    c.wait()


def forward_exchange(x, n_src, n_grp, sends, rows_out, rows_in, live, features, cot, w_self, w_neigh, inner, outer,
                     inc, cot_all, w_all, place_all, cols_out, divisor_out, own_feat,
                     feat, stage, blocks, row_sums, places, key_out, key_in, key_live, cols, divisor, table, send, recv, cot_s, cot_r, w_s, w_r, p_s, p_r, loc):
    q, g = lax.axis_index("dom"), lax.axis_index("grp")
    slots = stage.shape[1]
    own = cot_all.shape[2]
    fw = w_self.shape[0]
    n_blk, blk, _ = feat.shape
    near = 2 * x
    layers = place_all.shape[0]
    z, k = q // near, q % near
    slot = plane_slot(q, x)
    n_out, n_in = outer.shape[0], inner.shape[0]
    barrier = pltpu.get_barrier_semaphore()
    load_feat = pltpu.make_async_copy(features, feat, loc.at[3])
    load_feat.start()
    load_sends = pltpu.make_async_copy(sends, table, loc.at[13])
    load_sends.start()
    signal_plane(q, g, x, n_src)(barrier)
    signal_group(q, g, n_grp)(barrier)

    @pl.loop(1, layers)
    def _(r):
        pl.semaphore_signal(barrier, inc=1, device_id=((z + r) % layers * near + k, g), device_id_type=MESH)

    mine = pl.ds(pl.multiple_of(g * own, own), own)
    local = [
        pltpu.make_async_copy(cot.at[:, mine], cot_all.at[g], loc.at[0]),
        pltpu.make_async_copy(w_self, w_all.at[g, pl.ds(0, fw)], loc.at[1]),
        pltpu.make_async_copy(w_neigh, w_all.at[g, pl.ds(fw, fw)], loc.at[2]),
        pltpu.make_async_copy(places.at[z], place_all.at[z], loc.at[6]),
        pltpu.make_async_copy(feat.at[:, mine], own_feat, loc.at[12]),
    ]
    small = [
        pltpu.make_async_copy(rows_out, key_out, loc.at[7]),
        pltpu.make_async_copy(rows_in, key_in, loc.at[8]),
        pltpu.make_async_copy(live, key_live, loc.at[9]),
    ]
    loads = [
        pltpu.make_async_copy(outer, blocks.at[pl.ds(0, n_out)], loc.at[4]),
        pltpu.make_async_copy(inner, blocks.at[pl.ds(n_out, n_in)], loc.at[5]),
    ]

    def fill(d):
        peer = plane_peer(d, q, g, x)
        for s in range(slots):
            stage[d, s] = feat[table[peer, s]]
        return peer

    def remote(d, peer):
        return pltpu.make_async_remote_copy(
            src_ref=stage.at[d], dst_ref=inc.at[slot], send_sem=send.at[d], recv_sem=recv.at[slot],
            device_id=(peer, g), device_id_type=MESH)

    def place(r):
        to = (z + r) % layers
        return pltpu.make_async_remote_copy(
            src_ref=places.at[to], dst_ref=place_all.at[z], send_sem=p_s.at[r], recv_sem=p_r.at[r],
            device_id=(to * near + k, g), device_id_type=MESH)

    load_sends.wait()
    load_feat.wait()
    home = fill(slot)
    others = n_grp - 1 + layers - 1

    @pl.when(g == 0)
    def _():
        pl.semaphore_wait(barrier, n_src - 1 + others)

    @pl.when(g != 0)
    def _():
        pl.semaphore_wait(barrier, n_src + others)

    far = []
    for r in range(1, n_grp):
        y = (g + r) % n_grp
        to = dict(device_id=(q, y), device_id_type=MESH)
        theirs = pl.ds(pl.multiple_of(y * own, own), own)
        far.append(pltpu.make_async_remote_copy(
            src_ref=cot.at[:, theirs], dst_ref=cot_all.at[g],
            send_sem=cot_s.at[r - 1], recv_sem=cot_r.at[r - 1], **to))
        far.append(pltpu.make_async_remote_copy(
            src_ref=w_self, dst_ref=w_all.at[g, pl.ds(0, fw)],
            send_sem=w_s.at[r - 1, 0], recv_sem=w_r.at[r - 1, 0], **to))
        far.append(pltpu.make_async_remote_copy(
            src_ref=w_neigh, dst_ref=w_all.at[g, pl.ds(fw, fw)],
            send_sem=w_s.at[r - 1, 1], recv_sem=w_r.at[r - 1, 1], **to))

    @pl.when(g == 0)
    def _():
        pltpu.make_async_copy(stage.at[slot], inc.at[slot], recv.at[slot]).start()

    @pl.when(g != 0)
    def _():
        remote(slot, home).start()

    @pl.loop(1, n_src)
    def _(i):
        d = (slot + i) % n_src
        remote(d, fill(d)).start()

    for c in far + local[:3] + loads + small:
        c.start()

    per = 128 // own
    lane = lax.broadcasted_iota(jnp.int32, (1, 128), 1)

    @pl.loop(0, layers)
    def _(t):
        for c in range(pl.cdiv(near * slots, per)):
            spot = lane
            for u in range(per):
                if c * per + u < near * slots:
                    at = c * per + u
                    target = table[t * near + at // slots, at % slots]
                    spot = jnp.where(lane // own == u, lane + (target - u) * own, spot)
            places[t, c:c + 1, :] = spot

    local[3].start()
    local[4].start()
    each(1, layers, place, start)

    row = lax.broadcasted_iota(jnp.int32, (own + 16, blk), 0)
    lane = lax.broadcasted_iota(jnp.int32, (own + 16, blk), 1)
    pick = jnp.where((row == own) | (lane == row + g * own) & (row < own), 1.0, 0.0).astype(BF16)
    for c in loads:
        c.wait()

    @pl.loop(0, (n_out + n_in) // 8)
    def _(m):
        got = [lax.dot_general(pick, blocks[m * 8 + u], TRANS_B, preferred_element_type=F32) for u in range(8)]
        for u in range(8):
            cols[m * 8 + u] = got[u][:own].astype(BF16)
        row_sums[pl.ds(pl.multiple_of(m * 8, 8), 8), :] = jnp.concatenate([v[own:own + 1] for v in got], axis=0)

    keep = pltpu.make_async_copy(cols, cols_out, loc.at[10])
    keep.start()
    for c in small:
        c.wait()
    n_part = key_live.shape[1]
    first = slots * lax.broadcasted_iota(jnp.int32, (n_part, n_out), 0)
    at = lax.broadcasted_iota(jnp.int32, (n_part, n_out), 1) - first
    spread = jnp.where((at >= 0) & (at < slots), 1.0, 0.0)
    limit = jnp.dot(key_live[...].astype(F32), spread, precision=lax.Precision.HIGHEST, preferred_element_type=F32)
    index = jnp.sum(jnp.where((at >= 0) & (at < slots), at, 0), axis=0, keepdims=True)
    key = jnp.concatenate([jnp.where(index.astype(F32) < limit, key_out[...], n_blk), key_in[...]], axis=1)
    hits = jnp.where(lax.broadcasted_iota(jnp.int32, (n_blk, n_out + n_in), 0) == key, 1.0, 0.0)
    degree = 1.0 + jnp.dot(hits, row_sums[...], precision=lax.Precision.HIGHEST, preferred_element_type=F32)
    sel = (lax.broadcasted_iota(jnp.int32, (own, blk), 1) == lax.broadcasted_iota(jnp.int32, (own, blk), 0) + g * own)
    for b in range(n_blk):
        column = jnp.sum(jnp.where(sel, degree[b:b + 1], 0.0), axis=1, keepdims=True)
        divisor[b] = jnp.broadcast_to(column, (own, fw))

    keep_too = pltpu.make_async_copy(divisor, divisor_out, loc.at[11])
    keep_too.start()
    keep.wait()
    keep_too.wait()
    for c in local:
        c.wait()
    for c in far:
        c.wait()
    each(1, layers, place, wait)

    @pl.when(g != 0)
    def _():
        remote(slot, home).wait_send()

    @pl.loop(1, n_src)
    def _(i):
        d = (slot + i) % n_src
        remote(d, plane_peer(d, q, g, x)).wait_send()

    @pl.loop(0, n_src)
    def _(j):
        pltpu.make_async_copy(stage.at[j], inc.at[j], recv.at[j]).wait()


def aggregate_kernel(x, n_src, n_grp, i0, i1, i2, i3, features, inc, inner, outer, part, out_rows, live, in_rows, in_cols, i_sem, feat, acc, a_in, a_out, x_in, sem_f, sem_in, sem_out, sem_x):
    q, g = lax.axis_index("dom"), lax.axis_index("grp")
    slots = inc.shape[1]
    n_in = inner.shape[0] // n_grp
    indices = load_indices((i0, i1, i2, i3), (out_rows, live, in_rows, in_cols), i_sem)
    load_f = pltpu.make_async_copy(features, feat, sem_f)
    load_f.start()
    load_in = pltpu.make_async_copy(inner.at[pl.ds(g * n_in, n_in)], a_in, sem_in)
    load_in.start()
    load_x = pltpu.make_async_copy(inc, x_in, sem_x)
    load_x.start()

    def load(i):
        peer = plane_peer(i, q, g, x)
        return pltpu.make_async_copy(outer.at[pl.ds(peer * slots, slots)], a_out.at[i], sem_out)

    @pl.loop(0, n_src)
    def _(i):
        load(i).start()

    acc[...] = jnp.zeros_like(acc)
    for c in indices:
        c.wait()
    load_f.wait()
    load_in.wait()

    @pl.loop(0, n_in // 2)
    def _(m):
        value = [jnp.dot(a_in[m * 2 + u], feat[in_cols[0, g * n_in + m * 2 + u]], preferred_element_type=F32) for u in range(2)]
        for u in range(2):
            acc[in_rows[0, g * n_in + m * 2 + u]] += value[u]

    load_x.wait()
    pltpu.make_async_copy(a_out, a_out, sem_out).wait()

    @pl.loop(0, n_src)
    def _(i):
        peer = plane_peer(i, q, g, x)
        value = [jnp.dot(a_out[i, s], x_in[i, s], preferred_element_type=F32) for s in range(slots)]
        for s in range(slots):
            @pl.when(s < live[0, peer])
            def _(s=s):
                acc[out_rows[0, peer * slots + s]] += value[s]

    part[...] = acc[...].astype(BF16)


def dense_kernel(n_grp, part, feat, divisor, cots, ws, out_all, scaled, base, wgrad, cot_all, w_all, got, sent, s1, r1, s3, r3, loc):
    q, g = lax.axis_index("dom"), lax.axis_index("grp")
    n_blk, blk, fw = part.shape
    own = base.shape[1]
    hid = ws.shape[2]
    mine = pl.ds(pl.multiple_of(g * own, own), own)
    barrier = pltpu.get_barrier_semaphore()
    signal_group(q, g, n_grp)(barrier)
    loads = [
        pltpu.make_async_copy(ws, w_all, loc.at[1]),
        pltpu.make_async_copy(cots, cot_all, loc.at[2]),
    ]
    for c in loads:
        c.start()
    pl.semaphore_wait(barrier, n_grp - 1)
    cuts = 4
    step = n_blk // cuts
    copies, last = [[] for _ in range(cuts)], [[] for _ in range(cuts)]
    for h in range(cuts):
        part_h = pl.ds(h * step, step)
        for r in range(1, n_grp):
            y = (g + r) % n_grp
            to = dict(device_id=(q, y), device_id_type=MESH)
            theirs = pl.ds(pl.multiple_of(y * own, own), own)
            copies[h].append(pltpu.make_async_remote_copy(
                src_ref=part.at[part_h, theirs], dst_ref=got.at[r - 1, part_h], send_sem=s1.at[h, r - 1], recv_sem=r1.at[h, r - 1], **to))
            last[h].append(pltpu.make_async_remote_copy(
                src_ref=sent.at[part_h], dst_ref=scaled.at[part_h, mine], send_sem=s3.at[h, r - 1], recv_sem=r3.at[h, r - 1], **to))
    for h in range(cuts):
        for c in copies[h]:
            c.start()
    for c in loads:
        c.wait()
    rows = step * own
    both, grads = [], []
    for h in range(cuts):
        for c in copies[h]:
            c.wait()
        at = slice(h * step, (h + 1) * step)
        own_feat = feat[at]
        total = own_feat.astype(F32) + part[at, mine].astype(F32)
        for r in range(n_grp - 1):
            total = total + got[r, at].astype(F32)
        agg = (total / divisor[at]).astype(BF16)
        both.append(jnp.concatenate([own_feat.reshape(rows, fw), agg.reshape(rows, fw)], axis=1))
        back = jnp.zeros((rows, 2 * fw), F32)
        for j in range(n_grp):
            pre = jnp.dot(both[h], w_all[j], preferred_element_type=F32)
            sig = jax.nn.sigmoid(pre)
            out_all[j, at] = (pre * sig).astype(BF16).reshape(step, own, hid)
            cot = cot_all[j, at].reshape(rows, hid).astype(F32)
            grad = (cot * sig * (1.0 + pre * (1.0 - sig))).astype(BF16)
            grads.append(grad)
            back = back + lax.dot_general(grad, w_all[j], TRANS_B, preferred_element_type=F32)
        down = (back[:, fw:].reshape(step, own, fw) / divisor[at]).astype(BF16)
        sent[at] = down
        for c in last[h]:
            c.start()
        scaled[at, mine] = down
        base[at] = back[:, :fw].reshape(step, own, fw) + down.astype(F32)
    for j in range(n_grp):
        gw = sum(lax.dot_general(both[h], grads[h * n_grp + j], TRANS_A, preferred_element_type=F32) for h in range(cuts)).astype(BF16)
        for h in range(hid // 128):
            wgrad[j, h] = gw[:, 128 * h:128 * (h + 1)]
    for h in range(cuts):
        for c in last[h]:
            c.wait()


def backward_exchange(x, n_grp, n_in, i0, i1, i2, i3, scaled, cols, out_all, wgrad, places, base_sum, whole, out, grads,
                      out_rows, live, in_rows, in_cols, i_sem, inner_terms, inner_sum, sent, stage, inbox, right_out, right_in, left_out, left_in, w_got, pieces, near_got, far_sent, far_got,
                      send, recv, rs, rr, ls, lr, o_s, o_r, w_s, w_r, a_s, a_r, b_s, b_r, c_s, c_r, d_s, d_r, e_s, e_r, loc):
    q, g = lax.axis_index("dom"), lax.axis_index("grp")
    layers, near, slots, own, fw = stage.shape
    n_blk = whole.shape[0]
    cut = n_blk // 2
    half = layers // 2
    z, k = q // near, q % near
    indices = load_indices((i0, i1, i2, i3), (out_rows, live, in_rows, in_cols), i_sem)
    n_out = layers * near * slots
    barrier = pltpu.get_barrier_semaphore()
    signal_group(q, g, n_grp)(barrier)
    signal_ring(q, g, near, layers)(barrier)
    mine = pl.ds(pl.multiple_of(g * own, own), own)
    keep = pltpu.make_async_copy(out_all.at[g], out.at[:, mine], loc)
    keep.start()
    far, grad_far, last = [], [], []
    for r in range(1, n_grp):
        y = (g + r) % n_grp
        to = dict(device_id=(q, y), device_id_type=MESH)
        last.append(pltpu.make_async_remote_copy(
            src_ref=sent, dst_ref=whole.at[:, mine], send_sem=e_s.at[r - 1], recv_sem=e_r.at[r - 1], **to))
        far.append(pltpu.make_async_remote_copy(
            src_ref=out_all.at[y], dst_ref=out.at[:, mine], send_sem=o_s.at[r - 1], recv_sem=o_r.at[r - 1], **to))
        grad_far.append(pltpu.make_async_remote_copy(
            src_ref=wgrad.at[y], dst_ref=w_got.at[r - 1], send_sem=w_s.at[r - 1], recv_sem=w_r.at[r - 1], **to))

    def to_near(d, r):
        to = (k + r) % near
        return pltpu.make_async_remote_copy(
            src_ref=stage.at[d, to], dst_ref=inbox.at[d, k], send_sem=send.at[d, r], recv_sem=recv.at[d, r],
            device_id=(z * near + to, g), device_id_type=MESH)

    def own_term(d):
        return pltpu.make_async_copy(stage.at[d, k], inbox.at[d, k], recv.at[d, 0])

    def products(d):
        base = (z + d) % layers * near

        group = max(1, near // 2)

        @pl.loop(0, near // group)
        def _(r):
            value = []
            for u in range(group):
                for s in range(slots):
                    n = (base + r * group + u) * slots + s
                    value.append(jnp.dot(cols[n], scaled[out_rows[0, n]], preferred_element_type=F32))
            for u in range(group):
                to = r * group + u
                for s in range(slots):
                    stage[d, to, s] = jnp.where(s < live[0, base + to], value[u * slots + s], 0.0).astype(BF16)

    def ship(d):
        own_term(d).start()
        each(1, near, functools.partial(to_near, d), start)

    def reduce(d):
        own_term(d).wait()
        each(1, near, functools.partial(to_near, d), wait)
        n = near * slots * own
        spot = places[(z + d) % layers]
        row = lax.broadcasted_iota(jnp.int32, (n_blk * own, 128), 0)
        hot = [jnp.where(row == spot[c:c + 1], 1.0, 0.0).astype(BF16) for c in range(pl.cdiv(n, 128))]
        hot = jnp.concatenate(hot, axis=1)[:, :n] if len(hot) > 1 else hot[0][:, :n]
        terms = inbox[d].reshape(n, fw)
        return jnp.dot(hot, terms, preferred_element_type=F32).reshape(n_blk, own, fw)

    def ring(i, to_right):
        count = cut if i == 0 else n_blk
        held, lands, s_sem, r_sem, step = (right_out, right_in, rs, rr, 1) if to_right else (left_out, left_in, ls, lr, layers - 1)
        return pltpu.make_async_remote_copy(
            src_ref=held.at[i, pl.ds(0, count)], dst_ref=lands.at[i, pl.ds(0, count)], send_sem=s_sem.at[i], recv_sem=r_sem.at[i],
            device_id=((z + step) % layers * near + k, g), device_id_type=MESH)

    def with_right(i, value):
        ring(i, True).wait()
        if i == 0:
            return jnp.concatenate([value[:cut] + right_in[0, :cut].astype(F32), value[cut:]], axis=0)
        return value + right_in[i].astype(F32)

    def with_left(i, value):
        ring(i, False).wait()
        if i == 0:
            return jnp.concatenate([value[:cut], value[cut:] + left_in[0, :cut].astype(F32)], axis=0)
        return value + left_in[i].astype(F32)

    def near_reduce(r):
        to = (k + r) % near
        return pltpu.make_async_remote_copy(
            src_ref=pieces.at[pl.ds(to * layers, layers)], dst_ref=near_got.at[r],
            send_sem=a_s.at[r], recv_sem=a_r.at[r], device_id=(z * near + to, g), device_id_type=MESH)

    def far_reduce(r):
        to = (z + r) % layers
        return pltpu.make_async_remote_copy(
            src_ref=far_sent.at[to], dst_ref=far_got.at[r],
            send_sem=b_s.at[r], recv_sem=b_r.at[r], device_id=(to * near + k, g), device_id_type=MESH)

    def far_gather(r):
        to = (z + r) % layers
        return pltpu.make_async_remote_copy(
            src_ref=grads.at[k * layers + z], dst_ref=grads.at[k * layers + z],
            send_sem=c_s.at[r], recv_sem=c_r.at[r], device_id=(to * near + k, g), device_id_type=MESH)

    def near_gather(r):
        to = (k + r) % near
        return pltpu.make_async_remote_copy(
            src_ref=grads.at[pl.ds(k * layers, layers)], dst_ref=grads.at[pl.ds(k * layers, layers)],
            send_sem=d_s.at[r], recv_sem=d_r.at[r], device_id=(z * near + to, g), device_id_type=MESH)

    def sum_grp():
        for c in grad_far:
            c.wait()
        halves = wgrad.shape[1]
        per = pieces.shape[0] // halves
        for h in range(halves):
            total = wgrad[g, h].astype(F32)
            for r in range(n_grp - 1):
                total = total + w_got[r, h].astype(F32)
            pieces[h * per:(h + 1) * per] = total.reshape(per, pieces.shape[1], 128)
        each(1, near, near_reduce, start)

    def sum_near():
        each(1, near, near_reduce, wait)
        total = pieces[pl.ds(k * layers, layers)]
        for r in range(1, near):
            total = total + near_got[r]
        far_sent[...] = total
        each(1, layers, far_reduce, start)

    def sum_far():
        each(1, layers, far_reduce, wait)
        total = far_sent[z]
        for r in range(1, layers):
            total = total + far_got[r]
        grads[k * layers + z] = total
        each(1, layers, far_gather, start)

    def spread():
        each(1, layers, far_gather, wait)
        each(1, near, near_gather, start)

    def inner():
        per = 128 // own
        step = 4 * per

        @pl.loop(0, n_in // 8)
        def _(m):
            value = [jnp.dot(cols[n_out + m * 8 + u], scaled[in_rows[0, m * 8 + u]], preferred_element_type=F32) for u in range(8)]
            for u in range(8):
                inner_terms[m * 8 + u] = value[u].astype(BF16)

        lane = lax.broadcasted_iota(jnp.int32, (1, 128), 1)
        row = lax.broadcasted_iota(jnp.int32, (n_blk * own, 128), 0)
        inner_sum[...] = base_sum[...]

        def add(m, count):
            hot = []
            for c in range(count):
                spot = lane
                for u in range(per):
                    target = in_cols[0, m * step + c * per + u]
                    spot = jnp.where(lane // own == u, lane + (target - u) * own, spot)
                hot.append(jnp.where(row == spot, 1.0, 0.0).astype(BF16))
            hot = jnp.concatenate(hot, axis=1) if count > 1 else hot[0]
            terms = inner_terms[pl.ds(m * step, count * per)].reshape(count * per * own, fw)
            inner_sum[...] += jnp.dot(hot, terms, preferred_element_type=F32).reshape(n_blk, own, fw)

        if n_in % step:
            for m in range(n_in // step):
                add(m, 4)
            add(n_in // step, n_in % step // per)
        else:
            @pl.loop(0, n_in // step)
            def _(m):
                add(m, 4)

    for c in indices:
        c.wait()
    products(half)
    pl.semaphore_wait(barrier, n_grp - 1 + near - 1 + layers - 1)
    for c in grad_far:
        c.start()
    ship(half)
    for i in range(half):
        d = half - i
        if d > 1:
            for e in (d - 1, layers - d + 1):
                products(e)
                ship(e)
        else:
            products(0)
            ship(0)
        if i == 0:
            value = reduce(half)
            right_out[0, :cut] = value[:cut].astype(BF16)
            left_out[0, :cut] = value[cut:].astype(BF16)
        else:
            right_out[i] = with_right(i - 1, reduce(d)).astype(BF16)
            left_out[i] = with_left(i - 1, reduce(layers - d)).astype(BF16)
        ring(i, True).start()
        ring(i, False).start()
        if i == 0:
            inner()
            sum_grp()
            for c in far:
                c.start()
        if i == min(2, half - 1):
            sum_near()
    value = reduce(0) + inner_sum[...]
    sum_far()
    value = with_left(half - 1, with_right(half - 1, value)).astype(BF16)
    sent[...] = value
    for c in last:
        c.start()
    whole[:, mine] = value
    spread()
    keep.wait()
    for c in far:
        c.wait()
    each(1, near, near_gather, wait)
    for c in last:
        c.wait()


def results_kernel(whole, pieces, out_parts, feature_grad, self_grad, neigh_grad, out, wide, sem):
    keep = pltpu.make_async_copy(out_parts, out, sem.at[0])
    keep.start()
    wide[...] = whole[...].astype(F32)
    keep_too = pltpu.make_async_copy(wide, feature_grad, sem.at[1])
    keep_too.start()
    fw = self_grad.shape[0]
    halves = self_grad.shape[1] // 128
    per, depth = pieces.shape[0] // (2 * halves), pieces.shape[1]
    for h in range(halves):
        for m, to in enumerate((self_grad, neigh_grad)):
            at = (2 * h + m) * per
            to[:, 128 * h:128 * (h + 1)] = pieces[at:at + per].reshape(fw, 128)
    keep.wait()
    keep_too.wait()


def params(collective=None, vmem=48):
    if collective is None:
        return pltpu.CompilerParams(vmem_limit_bytes=vmem << 20)
    return pltpu.CompilerParams(vmem_limit_bytes=vmem << 20, collective_id=collective, has_side_effects=True)


def shards(features, w_self, w_neigh, cotangent, inner_rows, inner_cols, inner_values, send_blocks, outer_rows, outer_values, live_count):
    blk = inner_values.shape[-1]
    nodes, fw = features.shape
    n_blk = nodes // blk
    parts, n_grp = lax.axis_size("dom"), lax.axis_size("grp")
    x = x_extent(parts)
    near = 2 * x
    layers = parts // near
    n_src = parts // n_grp
    slots = send_blocks.shape[-1]
    hid = w_self.shape[1]
    own = blk // n_grp
    n_in, n_out = inner_values.shape[1], outer_values.shape[1]
    n_all = n_in + n_out
    inner, outer = inner_values[0], outer_values[0]
    feat = features.reshape(n_blk, blk, fw)
    dma, sds = pltpu.SemaphoreType.DMA, jax.ShapeDtypeStruct
    vm = pltpu.VMEM
    block = (n_src, slots, blk, fw)
    indices = (outer_rows, live_count, inner_rows, inner_cols)
    index_room = [pltpu.SMEM(a.shape, jnp.int32) for a in indices] + [dma((4,))]
    mine = (n_blk, own, fw)
    y_sem = dma((n_grp - 1,))

    inc, cot_all, w_all, place_all, cols, divisor, own_feat = pl.pallas_call(
        functools.partial(forward_exchange, x, n_src, n_grp),
        out_shape=(sds(block, BF16), sds((n_grp, n_blk, own, hid), BF16), sds((n_grp, 2 * fw, hid), BF16), sds((layers, 8, 128), jnp.int32),
                   sds((n_all, own, blk), BF16), sds(mine, F32), sds(mine, BF16)),
        in_specs=[HB] * 10,
        out_specs=(ANY,) * 7,
        scratch_shapes=[vm((n_blk, blk, fw), BF16), vm(block, BF16), vm((n_all, blk, blk), BF16), vm((n_all, blk), F32),
                        vm((layers, 8, 128), jnp.int32), vm((1, n_out), jnp.int32), vm((1, n_in), jnp.int32), vm((1, parts), jnp.int32), vm((n_all, own, blk), BF16), vm(mine, F32), pltpu.SMEM((parts, slots), jnp.int32),
                        dma((n_src,)), dma((n_src,)), y_sem, y_sem, dma((n_grp - 1, 2)), dma((n_grp - 1, 2)),
                        dma((layers,)), dma((layers,)), dma((14,))],
        compiler_params=params(0, 62), name="forward_exchange",
    )(send_blocks[0], outer_rows, inner_rows, live_count, feat, cotangent.reshape(n_blk, blk, hid), w_self, w_neigh, inner, outer)

    part = pl.pallas_call(
        functools.partial(aggregate_kernel, x, n_src, n_grp),
        out_shape=sds((n_blk, blk, fw), BF16),
        in_specs=[HB] * 5 + [ANY, HB, HB],
        out_specs=VM,
        scratch_shapes=index_room + [vm((n_blk, blk, fw), BF16), vm((n_blk, blk, fw), F32), vm((n_in // n_grp, blk, blk), BF16),
                        vm((n_src, slots, blk, blk), BF16), vm(block, BF16), dma, dma, dma, dma],
        compiler_params=params(None, 62), name="aggregate",
    )(*indices, feat, inc, inner, outer)

    halves = hid // 128
    out_all, scaled, base, wgrad = pl.pallas_call(
        functools.partial(dense_kernel, n_grp),
        out_shape=(sds((n_grp, n_blk, own, hid), BF16), sds((n_blk, blk, fw), BF16), sds(mine, F32), sds((n_grp, halves, 2 * fw, 128), BF16)),
        in_specs=[VM, VM, VM, ANY, ANY],
        out_specs=(VM,) * 4,
        scratch_shapes=[vm((n_grp, n_blk, own, hid), BF16), vm((n_grp, 2 * fw, hid), BF16),
                        vm((n_grp - 1,) + mine, BF16), vm(mine, BF16)] + [dma((4, n_grp - 1))] * 4 + [dma((3,))],
        compiler_params=params(1), name="dense",
    )(part, own_feat, divisor, cot_all, w_all)

    depth = halves * 2 * fw // parts
    half = layers // 2
    near_sem, far_sem = dma((near,)), dma((layers,))
    whole, out_parts, grads = pl.pallas_call(
        functools.partial(backward_exchange, x, n_grp, n_in),
        out_shape=(sds((n_blk, blk, fw), BF16), sds((n_blk, blk, hid), BF16), sds((parts, depth, 128), F32)),
        in_specs=[HB] * 4 + [VM, VM, ANY, VM, VM, VM],
        out_specs=(VM, ANY, VM),
        scratch_shapes=index_room + [vm((n_in, own, fw), BF16), vm(mine, F32), vm(mine, BF16), vm((layers, near, slots, own, fw), BF16), vm((layers, near, slots, own, fw), BF16)]
        + [vm((half,) + mine, BF16)] * 4
        + [vm((n_grp - 1, halves, 2 * fw, 128), BF16), vm((parts, depth, 128), F32), vm((near, layers, depth, 128), F32),
           vm((layers, depth, 128), F32), vm((layers, depth, 128), F32)]
        + [dma((layers, near))] * 2 + [dma((half,))] * 4 + [y_sem] * 4
        + [near_sem] * 2 + [far_sem] * 4 + [near_sem] * 2 + [y_sem] * 2 + [dma],
        compiler_params=params(2), name="backward_exchange",
    )(*indices, scaled, cols, out_all, wgrad, place_all, base)

    feature_grad, self_grad, neigh_grad, layer_out = pl.pallas_call(
        results_kernel,
        out_shape=(sds((n_blk, blk, fw), F32), sds((fw, hid), F32), sds((fw, hid), F32), sds((n_blk, blk, hid), BF16)),
        in_specs=[VM, VM, ANY],
        out_specs=(ANY, VM, VM, ANY),
        scratch_shapes=[vm((n_blk, blk, fw), F32), dma((2,))],
        compiler_params=params(), name="results",
    )(whole, grads, out_parts)
    return layer_out.reshape(nodes, hid), feature_grad.reshape(nodes, fw), self_grad, neigh_grad


def solution(mesh):
    placed = (
        P("dom", None),
        P(None, "grp"),
        P(None, "grp"),
        P("dom", "grp"),
        P("dom", None),
        P("dom", None),
        P("dom", None, None, None),
        P("dom", None, None),
        P("dom", None),
        P("dom", None, None, None),
        P("dom", None),
    )
    return jax.shard_map(
        shards,
        mesh=mesh,
        in_specs=placed,
        out_specs=(P("dom", "grp"), P("dom", None), P(None, "grp"), P(None, "grp")),
        check_vma=False,
    )
```
